256 devices in a mesh: child: 2 (over y_hi), row: 32 (over z, y_lo, core), col: 4 (over x).
Axes of the slice: x: 4, y: 4 (y_hi: 2, y_lo: 2; y = y_hi * 2 + y_lo), z: 8, core: 2. Of those that a mesh axis runs over, the one named last changes fastest.
Arguments:
- front: bfloat16 [131072, 2048], P(('row', 'child'), 'col'), as said below
- left_factors: bfloat16 [2, 4, 64, 131072], P('child', 'col', None, 'row'), may hold values from -2.5 to 2.5
- right_factors: bfloat16 [2, 256, 64, 2048], P('child', 'row', None, 'col'), may hold values from -2.5 to 2.5
Outputs:
- panel_t: bfloat16 [2048, 131072], P('col', ('row', 'child'))
The draws below stay inside these ranges and needn't reach their ends.
Inputs may be any that keep to these rules, and one draw needn't show every extreme that they name: The first 2048 rows of front make the symmetric part of the assembled diagonal block positive definite: its diagonal entries exceed the spectral norm of the rest of that part several times.
All inputs are finite; a program needn't handle non-finite values.
Results may differ from the reference program's by a relative error of at most 0.012.
Values may be sent and summed in bfloat16 or wider, within the bound.
No kernel may reach another device: no remote copies, remote signals or barrier semaphores. Data moves between devices by JAX's collectives and lax.ppermute only.
A program may use at most 128 MiB of HBM per device.

```python
import jax
import jax.numpy as jnp
from jax import lax

TILE = 512
RANK = 64
PW = 2048
ROWS = 131072


def draw_front(key, part):
    first, second = jax.random.split(key)
    values = jax.random.normal(first, (ROWS, PW), jnp.float32)
    values = jnp.clip(values, -6.0, 6.0)
    row_ids = jnp.arange(ROWS, dtype=jnp.int32)[:, None]
    col_ids = jnp.arange(PW, dtype=jnp.int32)[None, :]
    scales = jax.random.uniform(second, (ROWS, 1), jnp.float32, 1.0, 2.0)
    diag_part = jnp.where(row_ids == col_ids, 8.0 * PW ** 0.5 * scales, 0.0)
    return (values + diag_part).astype(jnp.bfloat16)


def levels(stream_key, shape, pieces, least, high):
    level = 1.0
    for axis_at, shards_of in pieces:
        heights = jax.random.uniform(jax.random.fold_in(jax.random.fold_in(stream_key, 6), axis_at), (shards_of,), jnp.float32, least / len(pieces), high / len(pieces))
        level = level * jnp.repeat(jnp.exp(heights), shape[axis_at] // shards_of).reshape((-1,) + (1,) * (len(shape) - 1 - axis_at))
    return level


def centred(rng, extent, spread, bound, shards=(), kind=jnp.bfloat16):
    drawn = jax.random.normal(rng, extent, jnp.float32) * spread
    if len(shards) > 0:
        drawn = levels(rng, extent, shards, -0.22, 0.18) * drawn
    return jnp.clip(drawn, min=-bound, max=bound).astype(kind)


def setup_inputs(seed: int = 0) -> dict:
    seeds = jax.random.split(jax.random.key(seed), 4)
    front = draw_front(jax.random.fold_in(seeds[3], 71), 0)
    left_factors = centred(seeds[1], (2, PW // TILE, RANK, ROWS), 0.35, 2.5, ((0, 2), (1, 4), (3, 32)))
    right_factors = centred(seeds[2], (2, ROWS // TILE, RANK, PW), 0.35, 2.5, ((0, 2), (1, 32), (3, 4)))
    return dict(front=front, left_factors=left_factors, right_factors=right_factors)


def inverse_transpose(top):
    factor = jnp.linalg.cholesky(top.astype(jnp.float32))
    identity = jnp.eye(PW, dtype=jnp.float32)
    inverse = lax.linalg.triangular_solve(factor, identity, left_side=True, lower=True)
    return inverse.T.astype(jnp.bfloat16)

def reference(front, left_factors, right_factors):

    def assemble(tile_index):
        rows_f = lax.dynamic_slice_in_dim(front, tile_index * TILE, TILE, 0).astype(jnp.float32)
        left_part = lax.dynamic_slice_in_dim(left_factors, tile_index * TILE, TILE, 3).astype(jnp.float32)
        right_part = lax.dynamic_index_in_dim(right_factors, tile_index, 1, keepdims=False).astype(jnp.float32)
        right_part = right_part.reshape(2, RANK, PW // TILE, TILE)
        update = jnp.einsum('cjrk,crjn->kjn', left_part, right_part).reshape(TILE, PW)
        return (rows_f - update).astype(jnp.bfloat16)
    top = jnp.concatenate([assemble(jnp.int32(i)) for i in range(PW // TILE)], axis=0)
    inverse_t = inverse_transpose(top)

    def panel(tile_index):
        return jnp.dot(assemble(tile_index).astype(jnp.float32), inverse_t.astype(jnp.float32), preferred_element_type=jnp.float32).astype(jnp.bfloat16)
    blocks = lax.map(panel, jnp.arange(ROWS // TILE, dtype=jnp.int32))
    return blocks.reshape(ROWS, PW).T
```

```python
import functools

import jax
import jax.numpy as jnp
from jax import lax
from jax.experimental import pallas as pl
from jax.experimental.pallas import tpu as pltpu
from jax.sharding import PartitionSpec as P

TILE = 512
RANK = 64
PW = 2048
BLOCKS = PW // TILE
ROOT_ITERS = 3
ALL = ("child", "row", "col")
NT = (((1,), (1,)), ((), ()))
NN = (((1,), (0,)), ((), ()))


def mxu(left, right, dims):
    return lax.dot_general(
        left.astype(jnp.bfloat16),
        right.astype(jnp.bfloat16),
        dims,
        preferred_element_type=jnp.float32,
    )


def leaf_inverse(tile_ref, x_ref, g_ref, n_ref, e_ref):
    rows = lax.broadcasted_iota(jnp.int32, (TILE, TILE), 0)
    cols = lax.broadcasted_iota(jnp.int32, (TILE, TILE), 1)
    diag = rows == cols
    tile = tile_ref[...]
    picked = jnp.where(diag, tile, 0.0)
    down = lax.rsqrt(jnp.sum(picked, axis=1, keepdims=True))
    across = lax.rsqrt(jnp.sum(picked, axis=0, keepdims=True))
    gram = tile * down * across - diag.astype(jnp.float32)

    def lower(mat):
        return jnp.where(rows > cols, mat, jnp.where(diag, 0.5 * mat, 0.0))

    g_ref[...] = gram
    n_ref[...] = lower(gram)

    def step(_, carry):
        n = n_ref[...]
        e = g_ref[...] - n - mxu(n, g_ref[...], NN)
        e_ref[...] = e.astype(jnp.bfloat16)
        phi = lower(e - n.T - mxu(e_ref[...], n, NT))
        n_ref[...] = n + phi - mxu(phi, n, NN)
        return carry

    lax.fori_loop(0, ROOT_ITERS, step, 0)
    x_ref[...] = ((diag.astype(jnp.float32) - n_ref[...]) * across).astype(jnp.bfloat16)


def factor_kernel(where_ref, own, left, right, far_a, far_b, *refs):
    outs = refs[:8]
    t_ref, s_ref, l_ref, x_ref, r_ref, g_ref, n_ref, e_ref, sems = refs[8:]
    col = where_ref[1]
    half = PW // 2

    @pl.when(where_ref[0] == 1)
    def _():
        far = lax.rem(col + 2, BLOCKS)
        copies = [
            pltpu.make_async_copy(own, t_ref.at[col], sems.at[0]),
            pltpu.make_async_copy(left, t_ref.at[lax.rem(col + 3, BLOCKS)], sems.at[1]),
            pltpu.make_async_copy(right, t_ref.at[lax.rem(col + 1, BLOCKS)], sems.at[2]),
            pltpu.make_async_copy(far_a, t_ref.at[far, pl.ds(0, half)], sems.at[3]),
            pltpu.make_async_copy(far_b, t_ref.at[far, pl.ds(half, half)], sems.at[4]),
        ]
        for copy in copies:
            copy.start()
        for copy in copies:
            copy.wait()

        def rows_of(i):
            return pl.ds(pl.multiple_of(i * TILE, TILE), TILE)

        @pl.loop(0, col + 1)
        def _(i):
            @pl.loop(0, i + 1)
            def _(j):
                low = t_ref[j, rows_of(i), :].astype(jnp.float32)
                high = t_ref[i, rows_of(j), :].astype(jnp.float32)
                s_ref[i, j] = 0.5 * (low + high.T)

        @pl.loop(0, col + 1)
        def _(j):
            leaf_inverse(s_ref.at[j, j], x_ref.at[j], g_ref, n_ref, e_ref)

            @pl.loop(j + 1, col + 1)
            def _(i):
                l_ref[i, j] = mxu(s_ref[i, j], x_ref[j], NT).astype(jnp.bfloat16)

                @pl.loop(j + 1, i + 1)
                def _(k):
                    s_ref[i, k] = s_ref[i, k] - mxu(l_ref[i, j], l_ref[k, j], NT)

        r_ref[col] = x_ref[col]

        @pl.loop(0, BLOCKS)
        def _(step):
            k = BLOCKS - 1 - step

            @pl.when(k > col)
            def _():
                r_ref[k] = jnp.zeros((TILE, TILE), jnp.bfloat16)

            @pl.when(k < col)
            def _():
                n_ref[...] = jnp.zeros((TILE, TILE), jnp.float32)

                @pl.loop(k + 1, col + 1)
                def _(m):
                    n_ref[...] += mxu(r_ref[m], l_ref[m, k], NN)

                r_ref[k] = (-mxu(n_ref[...], x_ref[k], NN)).astype(jnp.bfloat16)

        for z in range(8):
            for k in range(BLOCKS):
                outs[z][:, k * TILE : (k + 1) * TILE] = r_ref[k, z * 64 : (z + 1) * 64, :]


def factor_rows(where, own, left, right, far_a, far_b):
    any_spec = pl.BlockSpec(memory_space=pl.ANY)
    return pl.pallas_call(
        factor_kernel,
        out_shape=[jax.ShapeDtypeStruct((64, PW), jnp.bfloat16)] * 8,
        in_specs=[pl.BlockSpec(memory_space=pltpu.SMEM)] + [any_spec] * 5,
        out_specs=[pl.BlockSpec(memory_space=pltpu.VMEM)] * 8,
        scratch_shapes=[
            pltpu.VMEM((BLOCKS, PW, TILE), jnp.bfloat16),
            pltpu.VMEM((BLOCKS, BLOCKS, TILE, TILE), jnp.float32),
            pltpu.VMEM((BLOCKS, BLOCKS, TILE, TILE), jnp.bfloat16),
            pltpu.VMEM((BLOCKS, TILE, TILE), jnp.bfloat16),
            pltpu.VMEM((BLOCKS, TILE, TILE), jnp.bfloat16),
            pltpu.VMEM((TILE, TILE), jnp.float32),
            pltpu.VMEM((TILE, TILE), jnp.float32),
            pltpu.VMEM((TILE, TILE), jnp.bfloat16),
            pltpu.SemaphoreType.DMA((5,)),
        ],
        compiler_params=pltpu.CompilerParams(vmem_limit_bytes=60 << 20),
        name="factor_rows",
    )(where, own, left, right, far_a, far_b)


def apply_kernel(where_ref, own, left, right, far_a, far_b, *refs):
    chunks = refs[:8]
    out = refs[8]
    p_ref, r_ref, psems, rsems = refs[9:]
    col, z, core = where_ref[1], where_ref[2], where_ref[3]
    half = PW // 2
    sign = 1 - 2 * core
    rcopies = []
    for slot in range(8):
        if slot == 0:
            at = z
        elif slot <= 4:
            at = lax.rem(z - sign * slot + 8, 8)
        else:
            at = lax.rem(z + sign * (slot - 4) + 8, 8)
        rows = pl.ds(pl.multiple_of(at * 64, 64), 64)
        rcopies.append(pltpu.make_async_copy(chunks[slot], r_ref.at[rows], rsems.at[slot]))
    far = lax.rem(col + 2, BLOCKS)
    pcopies = [
        pltpu.make_async_copy(own, p_ref.at[col], psems.at[0]),
        pltpu.make_async_copy(left, p_ref.at[lax.rem(col + 3, BLOCKS)], psems.at[1]),
        pltpu.make_async_copy(right, p_ref.at[lax.rem(col + 1, BLOCKS)], psems.at[2]),
        pltpu.make_async_copy(far_a, p_ref.at[far, pl.ds(0, half)], psems.at[3]),
        pltpu.make_async_copy(far_b, p_ref.at[far, pl.ds(half, half)], psems.at[4]),
    ]
    for copy in rcopies + pcopies:
        copy.start()
    for copy in rcopies + pcopies:
        copy.wait()

    @pl.loop(0, PW // TILE)
    def _(tile):
        at = pl.ds(pl.multiple_of(tile * TILE, TILE), TILE)
        acc = jnp.zeros((TILE, TILE), jnp.float32)
        for k in range(BLOCKS):
            acc = acc + mxu(r_ref[:, k * TILE : (k + 1) * TILE], p_ref[k, at, :], NT)
        out[:, at] = acc.astype(jnp.bfloat16)


def apply_rows(where, own, left, right, far_a, far_b, chunks):
    any_spec = pl.BlockSpec(memory_space=pl.ANY)
    return pl.pallas_call(
        apply_kernel,
        out_shape=jax.ShapeDtypeStruct((TILE, PW), jnp.bfloat16),
        in_specs=[pl.BlockSpec(memory_space=pltpu.SMEM)] + [any_spec] * 13,
        out_specs=pl.BlockSpec(memory_space=pltpu.VMEM),
        scratch_shapes=[
            pltpu.VMEM((BLOCKS, PW, TILE), jnp.bfloat16),
            pltpu.VMEM((TILE, PW), jnp.bfloat16),
            pltpu.SemaphoreType.DMA((5,)),
            pltpu.SemaphoreType.DMA((8,)),
        ],
        compiler_params=pltpu.CompilerParams(vmem_limit_bytes=40 << 20),
        name="apply_rows",
    )(where, own, left, right, far_a, far_b, *chunks)


def device(child, z, ylo, core, col):
    return (child * 32 + z * 4 + ylo * 2 + core) * 4 + col


def pairs_of(move):
    found = []
    for child in range(2):
        for z in range(8):
            for ylo in range(2):
                for core in range(2):
                    for col in range(4):
                        target = move(child, z, ylo, core, col)
                        if target is not None:
                            found.append((device(child, z, ylo, core, col), device(*target)))
    return found


def gather_columns(part):
    def shift(by):
        return pairs_of(lambda c, z, y, k, j: (c, z, y, k, (j + by) % 4))

    half = PW // 2
    left = lax.ppermute(part, ALL, shift(1))
    right = lax.ppermute(part, ALL, shift(3))
    far_a = lax.ppermute(left[:half], ALL, shift(1))
    far_b = lax.ppermute(right[half:], ALL, shift(3))
    return left, right, far_a, far_b


def spread_rows(chunks, z, y, core):
    kept = chunks[0]
    total = None
    for k in range(1, 8):
        pairs = pairs_of(
            lambda c, zz, yy, kk, j: (0, k, 0, 0, j) if (c, zz, yy, kk) == (0, 0, 0, 0) else None
        )
        got = lax.ppermute(chunks[k], ALL, pairs)
        total = got if total is None else total + got
    chunk = jnp.where(z == 0, kept, total)
    total = None
    for to in (1, 3, 2):
        pairs = pairs_of(
            lambda c, zz, yy, kk, j: (to // 2, zz, to % 2, 0, j) if (c, yy, kk) == (0, 0, 0) else None
        )
        got = lax.ppermute(chunk, ALL, pairs)
        total = got if total is None else total + got
    chunk = jnp.where(y == 0, chunk, total)
    got = lax.ppermute(
        chunk, ALL, pairs_of(lambda c, zz, yy, kk, j: (c, zz, yy, 1, j) if kk == 0 else None)
    )
    chunk = jnp.where(core == 0, chunk, got)
    ring = pairs_of(lambda c, zz, yy, kk, j: (c, (zz + 1 - 2 * kk) % 8, yy, kk, j))
    swap = pairs_of(lambda c, zz, yy, kk, j: (c, zz, yy, 1 - kk, j))
    slots = [chunk]
    swapped = []
    current = chunk
    for step in range(4):
        current = lax.ppermute(current, ALL, ring)
        slots.append(current)
        if step < 3:
            swapped.append(lax.ppermute(current, ALL, swap))
    return slots + swapped


def shards(front, left_factors, right_factors):
    side = lax.axis_index("child")
    row = lax.axis_index("row")
    column = lax.axis_index("col")
    z, y, core = row // 4, 2 * side + (row // 2) % 2, row % 2
    left_all = left_factors[0, 0]
    right_all = right_factors[0]
    half = PW
    swap = [(0, 1), (1, 0)]
    tiles = right_all.shape[0] // 2
    got_left = lax.ppermute(
        lax.dynamic_slice_in_dim(left_all, (1 - side) * half, half, 1), "child", swap
    )
    got_right = lax.ppermute(
        lax.dynamic_slice_in_dim(right_all, (1 - side) * tiles, tiles, 0), "child", swap
    )
    own_left = lax.dynamic_slice_in_dim(left_all, side * half, half, 1)
    own_right = lax.dynamic_slice_in_dim(right_all, side * tiles, tiles, 0)
    left = jnp.concatenate([own_left, got_left], axis=0).reshape(2 * RANK, tiles, TILE)
    right = jnp.concatenate([own_right, got_right], axis=1)
    update = jnp.einsum("rtk,trn->tkn", left, right, preferred_element_type=jnp.float32)
    panel_rows = (front.astype(jnp.float32) - update.reshape(PW, TILE)).astype(jnp.bfloat16)
    parts = gather_columns(panel_rows)
    is_root = jnp.logical_and(side == 0, row == 0).astype(jnp.int32)
    where = jnp.stack([is_root, column, z, core]).astype(jnp.int32)
    chunks = factor_rows(where, panel_rows, *parts)
    chunks = spread_rows(chunks, z, y, core)
    return apply_rows(where, panel_rows, *parts, chunks)


def solution(mesh):
    in_specs = (
        P(("row", "child"), "col"),
        P("child", "col", None, "row"),
        P("child", "row", None, "col"),
    )
    out_specs = P("col", ("row", "child"))
    return jax.shard_map(shards, mesh=mesh, in_specs=in_specs, out_specs=out_specs, check_vma=False)
```

```python
import functools

import jax
import jax.numpy as jnp
from jax import lax
from jax.experimental import pallas as pl
from jax.experimental.pallas import tpu as pltpu
from jax.sharding import PartitionSpec as P

TILE = 512
RANK = 64
PW = 2048
BLOCKS = PW // TILE
ROOT_ITERS = 3
ALL = ("child", "row", "col")
NT = (((1,), (1,)), ((), ()))
NN = (((1,), (0,)), ((), ()))


def mxu(left, right, dims):
    return lax.dot_general(
        left.astype(jnp.bfloat16),
        right.astype(jnp.bfloat16),
        dims,
        preferred_element_type=jnp.float32,
    )


def leaf_inverse(tile_ref, x_ref, g_ref, n_ref, e_ref):
    rows = lax.broadcasted_iota(jnp.int32, (TILE, TILE), 0)
    cols = lax.broadcasted_iota(jnp.int32, (TILE, TILE), 1)
    diag = rows == cols
    tile = tile_ref[...]
    picked = jnp.where(diag, tile, 0.0)
    down = lax.rsqrt(jnp.sum(picked, axis=1, keepdims=True))
    across = lax.rsqrt(jnp.sum(picked, axis=0, keepdims=True))
    gram = tile * down * across - diag.astype(jnp.float32)

    def lower(mat):
        return jnp.where(rows > cols, mat, jnp.where(diag, 0.5 * mat, 0.0))

    g_ref[...] = gram
    n_ref[...] = lower(gram)

    def step(_, carry):
        n = n_ref[...]
        e = g_ref[...] - n - mxu(n, g_ref[...], NN)
        e_ref[...] = e.astype(jnp.bfloat16)
        phi = lower(e - n.T - mxu(e_ref[...], n, NT))
        n_ref[...] = n + phi - mxu(phi, n, NN)
        return carry

    lax.fori_loop(0, ROOT_ITERS, step, 0)
    x_ref[...] = ((diag.astype(jnp.float32) - n_ref[...]) * across).astype(jnp.bfloat16)


def fetch_columns(group, col, own, groups, dest, sems):
    half = PW // 2

    def copies(parts):
        found = []
        for slot, part in enumerate(own + parts):
            column = lax.rem(col + (0, 3, 1, 2)[slot // 2], BLOCKS)
            rows = pl.ds((slot % 2) * half, half)
            found.append(pltpu.make_async_copy(part, dest.at[column, rows], sems.at[slot]))
        return found

    for index, parts in enumerate(groups):

        @pl.when(group == index)
        def _():
            for copy in copies(parts):
                copy.start()

    return copies(groups[0])


def factor_kernel(where_ref, *refs):
    own, parts, outs = list(refs[:2]), list(refs[2:8]), refs[8:16]
    t_ref, s_ref, l_ref, x_ref, r_ref, g_ref, n_ref, e_ref, sems = refs[16:]
    col = where_ref[1]

    @pl.when(where_ref[0] == 0)
    def _():
        for copy in fetch_columns(0, col, own, [parts], t_ref, sems):
            copy.wait()

        def rows_of(i):
            return pl.ds(pl.multiple_of(i * TILE, TILE), TILE)

        @pl.loop(0, col + 1)
        def _(i):
            @pl.loop(0, i + 1)
            def _(j):
                low = t_ref[j, rows_of(i), :].astype(jnp.float32)
                high = t_ref[i, rows_of(j), :].astype(jnp.float32)
                s_ref[i, j] = 0.5 * (low + high.T)

        @pl.loop(0, col + 1)
        def _(j):
            leaf_inverse(s_ref.at[j, j], x_ref.at[j], g_ref, n_ref, e_ref)

            @pl.loop(j + 1, col + 1)
            def _(i):
                l_ref[i, j] = mxu(s_ref[i, j], x_ref[j], NT).astype(jnp.bfloat16)

                @pl.loop(j + 1, i + 1)
                def _(k):
                    s_ref[i, k] = s_ref[i, k] - mxu(l_ref[i, j], l_ref[k, j], NT)

        r_ref[col] = x_ref[col]

        @pl.loop(0, BLOCKS)
        def _(step):
            k = BLOCKS - 1 - step

            @pl.when(k > col)
            def _():
                r_ref[k] = jnp.zeros((TILE, TILE), jnp.bfloat16)

            @pl.when(k < col)
            def _():
                n_ref[...] = jnp.zeros((TILE, TILE), jnp.float32)

                @pl.loop(k + 1, col + 1)
                def _(m):
                    n_ref[...] += mxu(r_ref[m], l_ref[m, k], NN)

                r_ref[k] = (-mxu(n_ref[...], x_ref[k], NN)).astype(jnp.bfloat16)

        for z in range(8):
            for k in range(BLOCKS):
                outs[z][:, k * TILE : (k + 1) * TILE] = r_ref[k, z * 64 : (z + 1) * 64, :]


HBM = pl.BlockSpec(memory_space=pltpu.HBM)


def factor_rows(where, own, parts):
    return pl.pallas_call(
        factor_kernel,
        out_shape=[jax.ShapeDtypeStruct((64, PW), jnp.bfloat16)] * 8,
        in_specs=[pl.BlockSpec(memory_space=pltpu.SMEM)] + [HBM] * 8,
        out_specs=[pl.BlockSpec(memory_space=pltpu.VMEM)] * 8,
        scratch_shapes=[
            pltpu.VMEM((BLOCKS, PW, TILE), jnp.bfloat16),
            pltpu.VMEM((BLOCKS, BLOCKS, TILE, TILE), jnp.float32),
            pltpu.VMEM((BLOCKS, BLOCKS, TILE, TILE), jnp.bfloat16),
            pltpu.VMEM((BLOCKS, TILE, TILE), jnp.bfloat16),
            pltpu.VMEM((BLOCKS, TILE, TILE), jnp.bfloat16),
            pltpu.VMEM((TILE, TILE), jnp.float32),
            pltpu.VMEM((TILE, TILE), jnp.float32),
            pltpu.VMEM((TILE, TILE), jnp.bfloat16),
            pltpu.SemaphoreType.DMA((8,)),
        ],
        compiler_params=pltpu.CompilerParams(vmem_limit_bytes=56 << 20),
        name="factor_rows",
    )(where, *own, *parts)


CHUNKS = 9


def apply_kernel(where_ref, *refs):
    own = list(refs[:2])
    groups = [list(refs[2 + 6 * g : 8 + 6 * g]) for g in range(3)]
    chunks = refs[20 : 20 + CHUNKS]
    out, p_ref, r_ref, psems, rsems = refs[20 + CHUNKS :]
    group, col, z, core = where_ref[0], where_ref[1], where_ref[2], where_ref[3]
    sign = 1 - 2 * core
    copies = []
    for slot in range(CHUNKS):
        size = 64
        if slot <= 3:
            at = lax.rem(z - sign * slot + 8, 8) * 64
        elif slot <= 6:
            at = lax.rem(z + sign * (slot - 3) + 8, 8) * 64
        else:
            size = 32
            at = lax.rem(z + 4, 8) * 64 + (core if slot == 7 else 1 - core) * 32
        rows = pl.ds(pl.multiple_of(at, size), size)
        copies.append(pltpu.make_async_copy(chunks[slot], r_ref.at[rows], rsems.at[slot]))
    for copy in copies:
        copy.start()
    copies = copies + fetch_columns(group, col, own, groups, p_ref, psems)
    for copy in copies:
        copy.wait()

    @pl.loop(0, PW // TILE)
    def _(tile):
        at = pl.ds(pl.multiple_of(tile * TILE, TILE), TILE)
        acc = jnp.zeros((TILE, TILE), jnp.float32)
        for k in range(BLOCKS):
            acc = acc + mxu(r_ref[:, k * TILE : (k + 1) * TILE], p_ref[k, at, :], NT)
        out[:, at] = acc.astype(jnp.bfloat16)


def apply_rows(where, own, groups, chunks):
    return pl.pallas_call(
        apply_kernel,
        out_shape=jax.ShapeDtypeStruct((TILE, PW), jnp.bfloat16),
        in_specs=[pl.BlockSpec(memory_space=pltpu.SMEM)] + [HBM] * (20 + CHUNKS),
        out_specs=pl.BlockSpec(memory_space=pltpu.VMEM),
        scratch_shapes=[
            pltpu.VMEM((BLOCKS, PW, TILE), jnp.bfloat16),
            pltpu.VMEM((TILE, PW), jnp.bfloat16),
            pltpu.SemaphoreType.DMA((8,)),
            pltpu.SemaphoreType.DMA((CHUNKS,)),
        ],
        compiler_params=pltpu.CompilerParams(vmem_limit_bytes=40 << 20),
        name="apply_rows",
    )(where, *own, *groups[0], *groups[1], *groups[2], *chunks)


def device(child, z, ylo, core, col):
    return (child * 32 + z * 4 + ylo * 2 + core) * 4 + col


def pairs_of(move):
    found = []
    for child in range(2):
        for z in range(8):
            for ylo in range(2):
                for core in range(2):
                    for col in range(4):
                        target = move(child, z, ylo, core, col)
                        if target is not None:
                            found.append((device(child, z, ylo, core, col), device(*target)))
    return found


def group_of(child, z, ylo, core):
    if (child, z, ylo) == (0, 0, 0):
        return 0 if core == 0 else 2
    return 1


def gather_columns(own, group):
    def shift(by):
        return pairs_of(
            lambda c, z, y, k, j: (c, z, y, k, (j + by) % 4) if group_of(c, z, y, k) == group else None
        )

    upper, lower = own
    left_a = lax.ppermute(upper, ALL, shift(1))
    right_b = lax.ppermute(lower, ALL, shift(3))
    left_b = lax.ppermute(lower, ALL, shift(1))
    right_a = lax.ppermute(upper, ALL, shift(3))
    far_a = lax.ppermute(left_a, ALL, shift(1))
    far_b = lax.ppermute(right_b, ALL, shift(3))
    return [left_a, left_b, right_a, right_b, far_a, far_b]


def spread_rows(chunks, z, y, core):
    kept = chunks[0]
    total = None
    for k in range(1, 8):
        pairs = pairs_of(
            lambda c, zz, yy, kk, j: (0, k, 0, 0, j) if (c, zz, yy, kk) == (0, 0, 0, 0) else None
        )
        got = lax.ppermute(chunks[k], ALL, pairs)
        total = got if total is None else total + got
    chunk = jnp.where(z == 0, kept, total)
    total = None
    for to in (1, 3, 2):
        pairs = pairs_of(
            lambda c, zz, yy, kk, j: (to // 2, zz, to % 2, 0, j) if (c, yy, kk) == (0, 0, 0) else None
        )
        got = lax.ppermute(chunk, ALL, pairs)
        total = got if total is None else total + got
    chunk = jnp.where(y == 0, chunk, total)
    got = lax.ppermute(
        chunk, ALL, pairs_of(lambda c, zz, yy, kk, j: (c, zz, yy, 1, j) if kk == 0 else None)
    )
    chunk = jnp.where(core == 0, chunk, got)
    swap = pairs_of(lambda c, zz, yy, kk, j: (c, zz, yy, 1 - kk, j))
    across = pairs_of(lambda c, zz, yy, kk, j: (c, (zz + 4) % 8, yy, kk, j))
    part = lax.dynamic_slice_in_dim(chunk, core * 32, 32, 0)
    half = lax.ppermute(part, ALL, across)
    direct = {}
    for by in (3, 2, 1):
        pairs = pairs_of(lambda c, zz, yy, kk, j: (c, (zz + (1 - 2 * kk) * by) % 8, yy, kk, j))
        direct[by] = lax.ppermute(chunk, ALL, pairs)
    mine = [direct[by] for by in (1, 2, 3)]
    theirs = [lax.ppermute(direct[by], ALL, swap) for by in (1, 2, 3)]
    return [chunk] + mine + theirs + [half, lax.ppermute(half, ALL, swap)]


def assemble(front, left, right, got_left, got_right):
    tiles = right.shape[0]
    left = jnp.concatenate([left, got_left], axis=0).reshape(2 * RANK, tiles, TILE)
    right = jnp.concatenate([right, got_right], axis=1)
    update = jnp.einsum("rtk,trn->tkn", left, right, preferred_element_type=jnp.float32)
    update = update.reshape(tiles * TILE, TILE)
    return (front.astype(jnp.float32) - update).astype(jnp.bfloat16)


def assemble_halves(front, left, right, got_left, got_right):
    half = PW // 2
    tiles = right.shape[0] // 2
    return [
        assemble(
            front[at * half : (at + 1) * half],
            left[:, at * half : (at + 1) * half],
            right[at * tiles : (at + 1) * tiles],
            got_left[:, at * half : (at + 1) * half],
            got_right[at * tiles : (at + 1) * tiles],
        )
        for at in range(2)
    ]


def shards(front, left_factors, right_factors):
    side = lax.axis_index("child")
    row = lax.axis_index("row")
    column = lax.axis_index("col")
    z, y, core = row // 4, 2 * side + (row // 2) % 2, row % 2
    left_all = left_factors[0, 0]
    right_all = right_factors[0]
    tiles = right_all.shape[0] // 2
    send_left = lax.dynamic_slice_in_dim(left_all, (1 - side) * PW, PW, 1)
    send_right = lax.dynamic_slice_in_dim(right_all, (1 - side) * tiles, tiles, 0)
    own_left = lax.dynamic_slice_in_dim(left_all, side * PW, PW, 1)
    own_right = lax.dynamic_slice_in_dim(right_all, side * tiles, tiles, 0)

    def swap(first):
        return pairs_of(
            lambda c, zz, yy, kk, j: (1 - c, zz, yy, kk, j)
            if first == ((c, zz, yy, kk) == (1, 0, 0, 0))
            else None
        )

    top_left = lax.ppermute(send_left, ALL, swap(True))
    top_right = lax.ppermute(send_right, ALL, swap(True))
    top = assemble_halves(front, own_left, own_right, top_left, top_right)
    top_parts = gather_columns(top, 0)
    send_left, send_right, top_left, top_right = lax.optimization_barrier(
        (send_left, send_right, top_left, top_right)
    )
    got_left = lax.ppermute(send_left, ALL, swap(False)) + top_left
    got_right = lax.ppermute(send_right, ALL, swap(False)) + top_right
    own = assemble_halves(front, own_left, own_right, got_left, got_right)
    parts = gather_columns(own, 1)
    group = jnp.where(jnp.logical_and(y == 0, z == 0), 2 * core, 1)
    where = jnp.stack([group, column, z, core]).astype(jnp.int32)
    token = lax.ppermute(
        top_parts[4][:8, :128] + top_parts[5][:8, :128],
        ALL,
        pairs_of(lambda c, zz, yy, kk, j: (c, zz, yy, 1, j) if (c, zz, yy, kk) == (0, 0, 0, 0) else None),
    )
    late = lax.optimization_barrier((own[0], own[1], token))[:2]
    late_parts = gather_columns(late, 2)
    chunks = factor_rows(where, top, top_parts)
    chunks = spread_rows(chunks, z, y, core)
    return apply_rows(where, own, [top_parts, parts, late_parts], chunks)


def solution(mesh):
    in_specs = (
        P(("row", "child"), "col"),
        P("child", "col", None, "row"),
        P("child", "row", None, "col"),
    )
    out_specs = P("col", ("row", "child"))
    return jax.shard_map(shards, mesh=mesh, in_specs=in_specs, out_specs=out_specs, check_vma=False)
```

```python
import functools

import jax
import jax.numpy as jnp
from jax import lax
from jax.experimental import pallas as pl
from jax.experimental.pallas import tpu as pltpu
from jax.sharding import PartitionSpec as P

TILE = 512
RANK = 64
PW = 2048
BLOCKS = PW // TILE
ROOT_ITERS = 3
ALL = ("child", "row", "col")
NT = (((1,), (1,)), ((), ()))
NN = (((1,), (0,)), ((), ()))


def mxu(left, right, dims):
    return lax.dot_general(
        left.astype(jnp.bfloat16),
        right.astype(jnp.bfloat16),
        dims,
        preferred_element_type=jnp.float32,
    )


def leaf_inverse(tile_ref, x_ref, g_ref, n_ref, e_ref):
    rows = lax.broadcasted_iota(jnp.int32, (TILE, TILE), 0)
    cols = lax.broadcasted_iota(jnp.int32, (TILE, TILE), 1)
    diag = rows == cols
    tile = tile_ref[...]
    picked = jnp.where(diag, tile, 0.0)
    down = lax.rsqrt(jnp.sum(picked, axis=1, keepdims=True))
    across = lax.rsqrt(jnp.sum(picked, axis=0, keepdims=True))
    gram = tile * down * across - diag.astype(jnp.float32)

    def lower(mat):
        return jnp.where(rows > cols, mat, jnp.where(diag, 0.5 * mat, 0.0))

    g_ref[...] = gram
    n_ref[...] = lower(gram)

    def step(_, carry):
        n = n_ref[...]
        e = g_ref[...] - n - mxu(n, g_ref[...], NN)
        e_ref[...] = e.astype(jnp.bfloat16)
        phi = lower(e - n.T - mxu(e_ref[...], n, NT))
        n_ref[...] = n + phi - mxu(phi, n, NN)
        return carry

    lax.fori_loop(0, ROOT_ITERS, step, 0)
    x_ref[...] = ((diag.astype(jnp.float32) - n_ref[...]) * across).astype(jnp.bfloat16)


HALF = PW // 2
HBM = pl.BlockSpec(memory_space=pltpu.HBM)


def column_copies(col, next_parts, wrap_parts, far_parts, dest, sems):
    size = PW // len(next_parts)
    found = {1: [], 2: [], 3: []}
    for at in range(len(next_parts)):
        rows = pl.ds(at * size, size)
        slots = [3 * at, 3 * at + 1, 3 * at + 2]
        found[1].append(
            pltpu.make_async_copy(next_parts[at], dest.at[col - 1, rows], sems.at[slots[0]])
        )
        found[2].append(
            pltpu.make_async_copy(far_parts[at], dest.at[col - 2, rows], sems.at[slots[1]])
        )
        found[3].append(pltpu.make_async_copy(wrap_parts[at], dest.at[0, rows], sems.at[slots[2]]))

    for least in (1, 2, 3):

        @pl.when(col >= least)
        def _():
            for copy in found[least]:
                copy.start()

    for least in (1, 2, 3):

        @pl.when(col >= least)
        def _():
            for copy in found[least]:
                copy.wait()


def factor_kernel(where_ref, own, *refs):
    tops, outs = refs[:6], refs[6:14]
    t_ref, s_ref, l_ref, x_ref, r_ref, g_ref, n_ref, e_ref, sems = refs[14:]
    col = where_ref[1]

    @pl.when(where_ref[0] == 0)
    def _():
        mine = pltpu.make_async_copy(own, t_ref.at[col], sems.at[6])
        mine.start()
        column_copies(col, tops[0:2], tops[2:4], tops[4:6], t_ref, sems)
        mine.wait()

        def rows_of(i):
            return pl.ds(pl.multiple_of(i * TILE, TILE), TILE)

        @pl.loop(0, col + 1)
        def _(i):
            @pl.loop(0, i + 1)
            def _(j):
                low = t_ref[j, rows_of(i), :].astype(jnp.float32)
                high = t_ref[i, rows_of(j), :].astype(jnp.float32)
                s_ref[i, j] = 0.5 * (low + high.T)

        @pl.loop(0, col + 1)
        def _(j):
            leaf_inverse(s_ref.at[j, j], x_ref.at[j], g_ref, n_ref, e_ref)

            @pl.loop(j + 1, col + 1)
            def _(i):
                l_ref[i, j] = mxu(s_ref[i, j], x_ref[j], NT).astype(jnp.bfloat16)

                @pl.loop(j + 1, i + 1)
                def _(k):
                    s_ref[i, k] = s_ref[i, k] - mxu(l_ref[i, j], l_ref[k, j], NT)

        r_ref[col] = x_ref[col]

        @pl.loop(0, BLOCKS)
        def _(step):
            k = BLOCKS - 1 - step

            @pl.when(k > col)
            def _():
                r_ref[k] = jnp.zeros((TILE, TILE), jnp.bfloat16)

            @pl.when(k < col)
            def _():
                n_ref[...] = jnp.zeros((TILE, TILE), jnp.float32)

                @pl.loop(k + 1, col + 1)
                def _(m):
                    n_ref[...] += mxu(r_ref[m], l_ref[m, k], NN)

                r_ref[k] = (-mxu(n_ref[...], x_ref[k], NN)).astype(jnp.bfloat16)

        for z in range(8):
            for k in range(BLOCKS):
                outs[z][:, k * TILE : (k + 1) * TILE] = r_ref[k, z * 64 : (z + 1) * 64, :]


HBM = pl.BlockSpec(memory_space=pltpu.HBM)


def factor_rows(where, own, tops):
    return pl.pallas_call(
        factor_kernel,
        out_shape=[jax.ShapeDtypeStruct((64, PW), jnp.bfloat16)] * 8,
        in_specs=[pl.BlockSpec(memory_space=pltpu.SMEM)] + [HBM] * 7,
        out_specs=[pl.BlockSpec(memory_space=pltpu.VMEM)] * 8,
        scratch_shapes=[
            pltpu.VMEM((BLOCKS, PW, TILE), jnp.bfloat16),
            pltpu.VMEM((BLOCKS, BLOCKS, TILE, TILE), jnp.float32),
            pltpu.VMEM((BLOCKS, BLOCKS, TILE, TILE), jnp.bfloat16),
            pltpu.VMEM((BLOCKS, TILE, TILE), jnp.bfloat16),
            pltpu.VMEM((BLOCKS, TILE, TILE), jnp.bfloat16),
            pltpu.VMEM((TILE, TILE), jnp.float32),
            pltpu.VMEM((TILE, TILE), jnp.float32),
            pltpu.VMEM((TILE, TILE), jnp.bfloat16),
            pltpu.SemaphoreType.DMA((7,)),
        ],
        compiler_params=pltpu.CompilerParams(vmem_limit_bytes=56 << 20),
        name="factor_rows",
    )(where, own, *tops)


CHUNKS = 9


def apply_kernel(where_ref, own, *refs):
    main, late, tops = refs[:3], refs[3:6], refs[6:12]
    chunks = refs[12 : 12 + CHUNKS]
    out, p_ref, r_ref, acc_ref, psems, rsems = refs[13 + CHUNKS :]
    group, col, z, core = where_ref[0], where_ref[1], where_ref[2], where_ref[3]
    sign = 1 - 2 * core
    copies = []
    for slot in range(CHUNKS):
        size = 64
        if slot <= 3:
            at = lax.rem(z - sign * slot + 8, 8) * 64
        elif slot <= 6:
            at = lax.rem(z + sign * (slot - 3) + 8, 8) * 64
        else:
            size = 32
            at = lax.rem(z + 4, 8) * 64 + (core if slot == 7 else 1 - core) * 32
        rows = pl.ds(pl.multiple_of(at, size), size)
        copies.append(pltpu.make_async_copy(chunks[slot], r_ref.at[rows], rsems.at[slot]))
    copies.append(pltpu.make_async_copy(own, p_ref.at[col], psems.at[6]))
    for copy in copies:
        copy.start()

    @pl.when(group == 0)
    def _():
        column_copies(col, tops[0:2], tops[2:4], tops[4:6], p_ref, psems)

    for index, parts in ((1, main), (2, late)):

        @pl.when(group == index)
        def _():
            column_copies(col, parts[0:1], parts[1:2], parts[2:3], p_ref, psems)

    for copy in copies:
        copy.wait()

    @pl.loop(0, PW // TILE)
    def _(tile):
        at = pl.ds(pl.multiple_of(tile * TILE, TILE), TILE)
        acc_ref[...] = mxu(r_ref[:, :TILE], p_ref[0, at, :], NT)
        for k in range(1, BLOCKS):

            @pl.when(k <= col)
            def _():
                acc_ref[...] += mxu(r_ref[:, k * TILE : (k + 1) * TILE], p_ref[k, at, :], NT)

        out[:, at] = acc_ref[...].astype(jnp.bfloat16)


def apply_rows(where, own, main, late, tops, chunks, token):
    return pl.pallas_call(
        apply_kernel,
        out_shape=jax.ShapeDtypeStruct((TILE, PW), jnp.bfloat16),
        in_specs=[pl.BlockSpec(memory_space=pltpu.SMEM)] + [HBM] * (14 + CHUNKS),
        out_specs=pl.BlockSpec(memory_space=pltpu.VMEM),
        scratch_shapes=[
            pltpu.VMEM((BLOCKS, PW, TILE), jnp.bfloat16),
            pltpu.VMEM((TILE, PW), jnp.bfloat16),
            pltpu.VMEM((TILE, TILE), jnp.float32),
            pltpu.SemaphoreType.DMA((7,)),
            pltpu.SemaphoreType.DMA((CHUNKS,)),
        ],
        compiler_params=pltpu.CompilerParams(vmem_limit_bytes=40 << 20),
        name="apply_rows",
    )(where, own, *main, *late, *tops, *chunks, token)


def device(child, z, ylo, core, col):
    return (child * 32 + z * 4 + ylo * 2 + core) * 4 + col


def pairs_of(move):
    found = []
    for child in range(2):
        for z in range(8):
            for ylo in range(2):
                for core in range(2):
                    for col in range(4):
                        target = move(child, z, ylo, core, col)
                        if target is not None:
                            found.append((device(child, z, ylo, core, col), device(*target)))
    return found


def owner(core, col):
    return device(0, 0, 0, core, col)


def up_pairs(member, least, step=1):
    return pairs_of(
        lambda c, z, y, k, j: (c, z, y, k, (j + step) % 4)
        if member(c, z, y, k) and least <= j <= (2 if step == 1 else 0)
        else None
    )


def is_first(c, z, y, k):
    return (c, z, y, k) == (0, 0, 0, 0)


def is_second(c, z, y, k):
    return (c, z, y, k) == (0, 0, 0, 1)


def is_other(c, z, y, k):
    return (c, z, y) != (0, 0, 0)


def gather_part(part, member):
    near = lax.ppermute(part, ALL, up_pairs(member, 0))
    wrap = lax.ppermute(part, ALL, up_pairs(member, 0, 3))
    return near, wrap


def forward_part(near, member):
    return lax.ppermute(near, ALL, up_pairs(member, 1))


def spread_rows(chunks, z, y, core, far_a, far_b):
    kept = chunks[0]
    total = None
    for k in range(1, 8):
        pairs = pairs_of(
            lambda c, zz, yy, kk, j: (0, k, 0, 0, j) if (c, zz, yy, kk) == (0, 0, 0, 0) else None
        )
        got = lax.ppermute(chunks[k], ALL, pairs)
        total = got if total is None else total + got
    chunk = jnp.where(z == 0, kept, total)
    chunk, far_a, far_b = lax.optimization_barrier((chunk, far_a, far_b))
    total = None
    for to in (1, 3, 2):
        pairs = pairs_of(
            lambda c, zz, yy, kk, j: (to // 2, zz, to % 2, 0, j) if (c, yy, kk) == (0, 0, 0) else None
        )
        got = lax.ppermute(chunk, ALL, pairs)
        total = got if total is None else total + got
    chunk = jnp.where(y == 0, chunk, total)
    got = lax.ppermute(
        chunk, ALL, pairs_of(lambda c, zz, yy, kk, j: (c, zz, yy, 1, j) if kk == 0 else None)
    )
    chunk = jnp.where(core == 0, chunk, got)
    swap = pairs_of(lambda c, zz, yy, kk, j: (c, zz, yy, 1 - kk, j))
    across = pairs_of(lambda c, zz, yy, kk, j: (c, (zz + 4) % 8, yy, kk, j))
    part = lax.dynamic_slice_in_dim(chunk, core * 32, 32, 0)
    half = lax.ppermute(part, ALL, across)
    direct = {}
    for by in (3, 2, 1):
        pairs = pairs_of(lambda c, zz, yy, kk, j: (c, (zz + (1 - 2 * kk) * by) % 8, yy, kk, j))
        direct[by] = lax.ppermute(chunk, ALL, pairs)
    mine = [direct[by] for by in (1, 2, 3)]
    theirs = [lax.ppermute(direct[by], ALL, swap) for by in (1, 2, 3)]
    return [chunk] + mine + theirs + [half, lax.ppermute(half, ALL, swap)], far_a, far_b


def assemble(front, left, right, got_left, got_right):
    tiles = right.shape[0]
    left = jnp.concatenate([left, got_left], axis=0).reshape(2 * RANK, tiles, TILE)
    right = jnp.concatenate([right, got_right], axis=1)
    update = jnp.einsum("rtk,trn->tkn", left, right, preferred_element_type=jnp.float32)
    update = update.reshape(tiles * TILE, TILE)
    return (front.astype(jnp.float32) - update).astype(jnp.bfloat16)


def shards(front, left_factors, right_factors):
    side = lax.axis_index("child")
    row = lax.axis_index("row")
    column = lax.axis_index("col")
    z, y, core = row // 4, 2 * side + (row // 2) % 2, row % 2
    left_all = left_factors[0, 0]
    right_all = right_factors[0]
    tiles = right_all.shape[0] // 2
    send_left = lax.dynamic_slice_in_dim(left_all, (1 - side) * PW, PW, 1)
    send_right = lax.dynamic_slice_in_dim(right_all, (1 - side) * tiles, tiles, 0)
    own_left = lax.dynamic_slice_in_dim(left_all, side * PW, PW, 1)
    own_right = lax.dynamic_slice_in_dim(right_all, side * tiles, tiles, 0)

    swap = pairs_of(lambda c, zz, yy, kk, j: (1 - c, zz, yy, kk, j))
    got_left = lax.ppermute(send_left, ALL, swap)
    got_right = lax.ppermute(send_right, ALL, swap)
    own = assemble(front, own_left, own_right, got_left, got_right)
    near_a, wrap_a = gather_part(own[:HALF], is_first)
    near_b, wrap_b = gather_part(own[HALF:], is_first)
    far_a = forward_part(near_a, is_first)
    far_b = forward_part(near_b, is_first)
    tops = [near_a, near_b, wrap_a, wrap_b, far_a, far_b]
    near, wrap = gather_part(own, is_other)
    far = forward_part(near, is_other)
    token = lax.ppermute(
        near[:8, :128],
        ALL,
        [(device(0, 1, 0, 1, j), owner(1, j)) for j in range(1, 4)]
        + [(device(0, 1, 0, 0, 1), owner(1, 0))],
    )
    own_late, token = lax.optimization_barrier((own, token))
    late_near, late_wrap = gather_part(own_late, is_second)
    group = jnp.where(jnp.logical_and(y == 0, z == 0), 2 * core, 1)
    where = jnp.stack([group, column, z, core]).astype(jnp.int32)
    where, near, wrap, late_near = lax.optimization_barrier((where, near, wrap, late_near))
    late_far = forward_part(late_near, is_second)
    chunks = factor_rows(where, own, tops)
    chunks, far, late_wrap = spread_rows(chunks, z, y, core, far, late_wrap)
    main = [near, wrap, far]
    late = [late_near, late_wrap, late_far]
    return apply_rows(where, own, main, late, tops, chunks, token)


def solution(mesh):
    in_specs = (
        P(("row", "child"), "col"),
        P("child", "col", None, "row"),
        P("child", "row", None, "col"),
    )
    out_specs = P("col", ("row", "child"))
    return jax.shard_map(shards, mesh=mesh, in_specs=in_specs, out_specs=out_specs, check_vma=False)
```

```python
import functools

import jax
import jax.numpy as jnp
from jax import lax
from jax.experimental import pallas as pl
from jax.experimental.pallas import tpu as pltpu
from jax.sharding import PartitionSpec as P

TILE = 512
RANK = 64
PW = 2048
BLOCKS = PW // TILE
ROOT_ITERS = 3
ALL = ("child", "row", "col")
NT = (((1,), (1,)), ((), ()))
NN = (((1,), (0,)), ((), ()))


def mxu(left, right, dims):
    return lax.dot_general(
        left.astype(jnp.bfloat16),
        right.astype(jnp.bfloat16),
        dims,
        preferred_element_type=jnp.float32,
    )


def leaf_inverse(tile_ref, x_ref, g_ref, n_ref, e_ref):
    rows = lax.broadcasted_iota(jnp.int32, (TILE, TILE), 0)
    cols = lax.broadcasted_iota(jnp.int32, (TILE, TILE), 1)
    diag = rows == cols
    tile = tile_ref[...]
    picked = jnp.where(diag, tile, 0.0)
    down = lax.rsqrt(jnp.sum(picked, axis=1, keepdims=True))
    across = lax.rsqrt(jnp.sum(picked, axis=0, keepdims=True))
    gram = tile * down * across - diag.astype(jnp.float32)

    def lower(mat):
        return jnp.where(rows > cols, mat, jnp.where(diag, 0.5 * mat, 0.0))

    g_ref[...] = gram
    n_ref[...] = lower(gram)

    def step(_, carry):
        n = n_ref[...]
        e = g_ref[...] - n - mxu(n, g_ref[...], NN)
        e_ref[...] = e.astype(jnp.bfloat16)
        phi = lower(e - n.T - mxu(e_ref[...], n, NT))
        n_ref[...] = n + phi - mxu(phi, n, NN)
        return carry

    lax.fori_loop(0, ROOT_ITERS, step, 0)
    x_ref[...] = ((diag.astype(jnp.float32) - n_ref[...]) * across).astype(jnp.bfloat16)


HALF = PW // 2
HBM = pl.BlockSpec(memory_space=pltpu.HBM)


def run_copies(found, dest, sems):
    copies = [
        pltpu.make_async_copy(part, dest.at[column, pl.ds(at * HALF, size)], sems.at[slot])
        for slot, (part, column, at, size) in enumerate(found)
    ]
    for copy in copies:
        copy.start()
    for copy in copies:
        copy.wait()


def fetch_tops(col, tops, dest, sems):
    u0, u2_u1, w0_w1, w2, w1, u1_u0, w0, u0_next, w0_next = tops
    found = {
        1: [(u0_next, 0, 0, HALF), (w0_next, 0, 1, HALF)],
        2: [(u2_u1, 1, 0, HALF), (w0_w1, 1, 1, HALF), (u1_u0, 0, 0, HALF), (w0, 0, 1, HALF)],
        3: [
            (u0, 0, 0, HALF),
            (w0_w1, 0, 1, HALF),
            (u2_u1, 2, 0, HALF),
            (w2, 2, 1, HALF),
            (u1_u0, 1, 0, HALF),
            (w1, 1, 1, HALF),
        ],
    }
    for column, parts in found.items():

        @pl.when(col == column)
        def _():
            run_copies(parts, dest, sems)


def fetch_rows(col, parts, dest, sems):
    near, wrap, upper, lower = parts
    found = {
        1: [(near, 0, 0, PW)],
        2: [(near, 1, 0, PW), (upper, 0, 0, HALF), (lower, 0, 1, HALF)],
        3: [(near, 2, 0, PW), (wrap, 0, 0, PW), (upper, 1, 0, HALF), (lower, 1, 1, HALF)],
    }
    for column, parts in found.items():

        @pl.when(col == column)
        def _():
            run_copies(parts, dest, sems)


def factor_kernel(where_ref, own, *refs):
    tops, outs = refs[:9], refs[9:17]
    t_ref, s_ref, l_ref, x_ref, r_ref, g_ref, n_ref, e_ref, sems = refs[17:]
    col = where_ref[1]

    @pl.when(where_ref[0] == 0)
    def _():
        mine = pltpu.make_async_copy(own, t_ref.at[col], sems.at[6])
        mine.start()
        fetch_tops(col, tops, t_ref, sems)
        mine.wait()

        def rows_of(i):
            return pl.ds(pl.multiple_of(i * TILE, TILE), TILE)

        @pl.loop(0, col + 1)
        def _(i):
            @pl.loop(0, i + 1)
            def _(j):
                low = t_ref[j, rows_of(i), :].astype(jnp.float32)
                high = t_ref[i, rows_of(j), :].astype(jnp.float32)
                s_ref[i, j] = 0.5 * (low + high.T)

        @pl.loop(0, col + 1)
        def _(j):
            leaf_inverse(s_ref.at[j, j], x_ref.at[j], g_ref, n_ref, e_ref)

            @pl.loop(j + 1, col + 1)
            def _(i):
                l_ref[i, j] = mxu(s_ref[i, j], x_ref[j], NT).astype(jnp.bfloat16)

                @pl.loop(j + 1, i + 1)
                def _(k):
                    s_ref[i, k] = s_ref[i, k] - mxu(l_ref[i, j], l_ref[k, j], NT)

        r_ref[col] = x_ref[col]

        @pl.loop(0, BLOCKS)
        def _(step):
            k = BLOCKS - 1 - step

            @pl.when(k > col)
            def _():
                r_ref[k] = jnp.zeros((TILE, TILE), jnp.bfloat16)

            @pl.when(k < col)
            def _():
                n_ref[...] = jnp.zeros((TILE, TILE), jnp.float32)

                @pl.loop(k + 1, col + 1)
                def _(m):
                    n_ref[...] += mxu(r_ref[m], l_ref[m, k], NN)

                r_ref[k] = (-mxu(n_ref[...], x_ref[k], NN)).astype(jnp.bfloat16)

        for z in range(8):
            for k in range(BLOCKS):
                outs[z][:, k * TILE : (k + 1) * TILE] = r_ref[k, z * 64 : (z + 1) * 64, :]


HBM = pl.BlockSpec(memory_space=pltpu.HBM)


def factor_rows(where, own, tops):
    return pl.pallas_call(
        factor_kernel,
        out_shape=[jax.ShapeDtypeStruct((64, PW), jnp.bfloat16)] * 8,
        in_specs=[pl.BlockSpec(memory_space=pltpu.SMEM)] + [HBM] * 10,
        out_specs=[pl.BlockSpec(memory_space=pltpu.VMEM)] * 8,
        scratch_shapes=[
            pltpu.VMEM((BLOCKS, PW, TILE), jnp.bfloat16),
            pltpu.VMEM((BLOCKS, BLOCKS, TILE, TILE), jnp.float32),
            pltpu.VMEM((BLOCKS, BLOCKS, TILE, TILE), jnp.bfloat16),
            pltpu.VMEM((BLOCKS, TILE, TILE), jnp.bfloat16),
            pltpu.VMEM((BLOCKS, TILE, TILE), jnp.bfloat16),
            pltpu.VMEM((TILE, TILE), jnp.float32),
            pltpu.VMEM((TILE, TILE), jnp.float32),
            pltpu.VMEM((TILE, TILE), jnp.bfloat16),
            pltpu.SemaphoreType.DMA((7,)),
        ],
        compiler_params=pltpu.CompilerParams(vmem_limit_bytes=56 << 20),
        name="factor_rows",
    )(where, own, *tops)


CHUNKS = 9


def apply_kernel(where_ref, own, *refs):
    main, late, tops = refs[:4], refs[4:8], refs[8:17]
    chunks = refs[17 : 17 + CHUNKS]
    out, p_ref, r_ref, acc_ref, psems, rsems = refs[18 + CHUNKS :]
    group, col, z, core = where_ref[0], where_ref[1], where_ref[2], where_ref[3]
    sign = 1 - 2 * core
    copies = []
    for slot in range(CHUNKS):
        size = 64
        if slot <= 3:
            at = lax.rem(z - sign * slot + 8, 8) * 64
        elif slot <= 6:
            at = lax.rem(z + sign * (slot - 3) + 8, 8) * 64
        else:
            size = 32
            at = lax.rem(z + 4, 8) * 64 + (core if slot == 7 else 1 - core) * 32
        rows = pl.ds(pl.multiple_of(at, size), size)
        copies.append(pltpu.make_async_copy(chunks[slot], r_ref.at[rows], rsems.at[slot]))
    copies.append(pltpu.make_async_copy(own, p_ref.at[col], psems.at[6]))
    for copy in copies:
        copy.start()

    @pl.when(group == 0)
    def _():
        fetch_tops(col, tops, p_ref, psems)

    for index, parts in ((1, main), (2, late)):

        @pl.when(group == index)
        def _():
            fetch_rows(col, parts, p_ref, psems)

    for copy in copies:
        copy.wait()

    @pl.loop(0, PW // TILE)
    def _(tile):
        at = pl.ds(pl.multiple_of(tile * TILE, TILE), TILE)
        acc_ref[...] = mxu(r_ref[:, :TILE], p_ref[0, at, :], NT)
        for k in range(1, BLOCKS):

            @pl.when(k <= col)
            def _():
                acc_ref[...] += mxu(r_ref[:, k * TILE : (k + 1) * TILE], p_ref[k, at, :], NT)

        out[:, at] = acc_ref[...].astype(jnp.bfloat16)


def apply_rows(where, own, main, late, tops, chunks, token):
    return pl.pallas_call(
        apply_kernel,
        out_shape=jax.ShapeDtypeStruct((TILE, PW), jnp.bfloat16),
        in_specs=[pl.BlockSpec(memory_space=pltpu.SMEM)] + [HBM] * (19 + CHUNKS),
        out_specs=pl.BlockSpec(memory_space=pltpu.VMEM),
        scratch_shapes=[
            pltpu.VMEM((BLOCKS, PW, TILE), jnp.bfloat16),
            pltpu.VMEM((TILE, PW), jnp.bfloat16),
            pltpu.VMEM((TILE, TILE), jnp.float32),
            pltpu.SemaphoreType.DMA((7,)),
            pltpu.SemaphoreType.DMA((CHUNKS,)),
        ],
        compiler_params=pltpu.CompilerParams(vmem_limit_bytes=40 << 20),
        name="apply_rows",
    )(where, own, *main, *late, *tops, *chunks, token)


def device(child, z, ylo, core, col):
    return (child * 32 + z * 4 + ylo * 2 + core) * 4 + col


def pairs_of(move):
    found = []
    for child in range(2):
        for z in range(8):
            for ylo in range(2):
                for core in range(2):
                    for col in range(4):
                        target = move(child, z, ylo, core, col)
                        if target is not None:
                            found.append((device(child, z, ylo, core, col), device(*target)))
    return found


def owner(core, col):
    return device(0, 0, 0, core, col)


def moves(member, *steps):
    allowed = dict(steps)
    return pairs_of(
        lambda c, z, y, k, j: (c, z, y, k, allowed[j]) if member(c, z, y, k) and j in allowed else None
    )


def is_first(c, z, y, k):
    return (c, z, y, k) == (0, 0, 0, 0)


def is_second(c, z, y, k):
    return (c, z, y, k) == (0, 0, 0, 1)


def is_other(c, z, y, k):
    return (c, z, y) != (0, 0, 0)


def gather_part(part, member):
    wrap = lax.ppermute(part, ALL, moves(member, (0, 3), (1, 0)))
    near = lax.ppermute(part, ALL, moves(member, (0, 1), (1, 2), (2, 3)))
    return near, wrap


def forward_part(near, wrap, member):
    upper = lax.ppermute(near[:HALF], ALL, moves(member, (1, 2), (2, 3)))
    lower = lax.ppermute(wrap[HALF:], ALL, moves(member, (0, 3), (3, 2)))
    return upper, lower


def gather_top(own, column):
    def send(part, *steps):
        return lax.ppermute(part, ALL, moves(is_first, *steps))

    upper, lower = own[:HALF], own[HALF:]
    first = jnp.where(column == 1, lower, upper)
    u0 = send(first, (0, 3), (1, 0))
    u2_u1 = send(upper, (2, 3), (1, 2))
    w0_w1 = send(lower, (0, 3), (1, 2))
    w2 = send(lower, (2, 3))
    w1 = send(u0, (0, 3))
    u1_u0 = send(jnp.where(column == 3, u0, u2_u1), (2, 3), (3, 2))
    w0 = send(w0_w1, (3, 2))
    upper, lower, w1 = lax.optimization_barrier((upper, lower, w1))
    u0_next = send(upper, (0, 1))
    w0_next = send(lower, (0, 1))
    return [u0, u2_u1, w0_w1, w2, w1, u1_u0, w0, u0_next, w0_next]


def spread_rows(chunks, z, y, core, early):
    kept = chunks[0]
    total = None
    for k in range(1, 8):
        pairs = pairs_of(
            lambda c, zz, yy, kk, j: (0, k, 0, 0, j) if (c, zz, yy, kk) == (0, 0, 0, 0) else None
        )
        got = lax.ppermute(chunks[k], ALL, pairs)
        total = got if total is None else total + got
    chunk = jnp.where(z == 0, kept, total)
    chunk, *early = lax.optimization_barrier((chunk, *early))
    total = None
    for to in (1, 3, 2):
        pairs = pairs_of(
            lambda c, zz, yy, kk, j: (to // 2, zz, to % 2, 0, j) if (c, yy, kk) == (0, 0, 0) else None
        )
        got = lax.ppermute(chunk, ALL, pairs)
        total = got if total is None else total + got
    chunk = jnp.where(y == 0, chunk, total)
    got = lax.ppermute(
        chunk, ALL, pairs_of(lambda c, zz, yy, kk, j: (c, zz, yy, 1, j) if kk == 0 else None)
    )
    chunk = jnp.where(core == 0, chunk, got)
    swap = pairs_of(lambda c, zz, yy, kk, j: (c, zz, yy, 1 - kk, j))
    across = pairs_of(lambda c, zz, yy, kk, j: (c, (zz + 4) % 8, yy, kk, j))
    part = lax.dynamic_slice_in_dim(chunk, core * 32, 32, 0)
    half = lax.ppermute(part, ALL, across)
    direct = {}
    for by in (3, 2, 1):
        pairs = pairs_of(lambda c, zz, yy, kk, j: (c, (zz + (1 - 2 * kk) * by) % 8, yy, kk, j))
        direct[by] = lax.ppermute(chunk, ALL, pairs)
    mine = [direct[by] for by in (1, 2, 3)]
    theirs = [lax.ppermute(direct[by], ALL, swap) for by in (1, 2, 3)]
    return [chunk] + mine + theirs + [half, lax.ppermute(half, ALL, swap)], *early


def assemble(front, left, right, got_left, got_right):
    tiles = right.shape[0]
    left = jnp.concatenate([left, got_left], axis=0).reshape(2 * RANK, tiles, TILE)
    right = jnp.concatenate([right, got_right], axis=1)
    update = jnp.einsum("rtk,trn->tkn", left, right, preferred_element_type=jnp.float32)
    update = update.reshape(tiles * TILE, TILE)
    return (front.astype(jnp.float32) - update).astype(jnp.bfloat16)


def shards(front, left_factors, right_factors):
    side = lax.axis_index("child")
    row = lax.axis_index("row")
    column = lax.axis_index("col")
    z, y, core = row // 4, 2 * side + (row // 2) % 2, row % 2
    left_all = left_factors[0, 0]
    right_all = right_factors[0]
    tiles = right_all.shape[0] // 2
    send_left = lax.dynamic_slice_in_dim(left_all, (1 - side) * PW, PW, 1)
    send_right = lax.dynamic_slice_in_dim(right_all, (1 - side) * tiles, tiles, 0)
    own_left = lax.dynamic_slice_in_dim(left_all, side * PW, PW, 1)
    own_right = lax.dynamic_slice_in_dim(right_all, side * tiles, tiles, 0)

    swap = pairs_of(lambda c, zz, yy, kk, j: (1 - c, zz, yy, kk, j))
    got_left = lax.ppermute(send_left, ALL, swap)
    got_right = lax.ppermute(send_right, ALL, swap)
    own = assemble(front, own_left, own_right, got_left, got_right)
    tops = gather_top(own, column)
    near, wrap = gather_part(own, is_other)
    upper, lower = forward_part(near, wrap, is_other)
    token = lax.ppermute(
        near[:8, :128] + wrap[:8, :128],
        ALL,
        [(device(0, 1, 0, 0, j), owner(1, j)) for j in range(4)],
    )
    own_late, token = lax.optimization_barrier((own, token))
    late_near, late_wrap = gather_part(own_late, is_second)
    group = jnp.where(jnp.logical_and(y == 0, z == 0), 2 * core, 1)
    where = jnp.stack([group, column, z, core]).astype(jnp.int32)
    where, near, wrap, late_near = lax.optimization_barrier((where, near, wrap, late_near))
    late_upper, late_lower = forward_part(late_near, late_wrap, is_second)
    chunks = factor_rows(where, own, tops)
    chunks, upper, lower, late_wrap = spread_rows(chunks, z, y, core, (upper, lower, late_wrap))
    main = [near, wrap, upper, lower]
    late = [late_near, late_wrap, late_upper, late_lower]
    return apply_rows(where, own, main, late, tops, chunks, token)


def solution(mesh):
    in_specs = (
        P(("row", "child"), "col"),
        P("child", "col", None, "row"),
        P("child", "row", None, "col"),
    )
    out_specs = P("col", ("row", "child"))
    return jax.shard_map(shards, mesh=mesh, in_specs=in_specs, out_specs=out_specs, check_vma=False)
```

```python
import functools

import jax
import jax.numpy as jnp
from jax import lax
from jax.experimental import pallas as pl
from jax.experimental.pallas import tpu as pltpu
from jax.sharding import PartitionSpec as P

TILE = 512
RANK = 64
PW = 2048
BLOCKS = PW // TILE
ROOT_ITERS = 3
ALL = ("child", "row", "col")
NT = (((1,), (1,)), ((), ()))
NN = (((1,), (0,)), ((), ()))


def mxu(left, right, dims):
    return lax.dot_general(
        left.astype(jnp.bfloat16),
        right.astype(jnp.bfloat16),
        dims,
        preferred_element_type=jnp.float32,
    )


def leaf_inverse(tile_ref, x_ref, g_ref, n_ref, e_ref):
    rows = lax.broadcasted_iota(jnp.int32, (TILE, TILE), 0)
    cols = lax.broadcasted_iota(jnp.int32, (TILE, TILE), 1)
    diag = rows == cols
    tile = tile_ref[...]
    picked = jnp.where(diag, tile, 0.0)
    down = lax.rsqrt(jnp.sum(picked, axis=1, keepdims=True))
    across = lax.rsqrt(jnp.sum(picked, axis=0, keepdims=True))
    gram = tile * down * across - diag.astype(jnp.float32)

    def lower(mat):
        return jnp.where(rows > cols, mat, jnp.where(diag, 0.5 * mat, 0.0))

    g_ref[...] = gram
    n_ref[...] = lower(gram)

    def step(_, carry):
        n = n_ref[...]
        e = g_ref[...] - n - mxu(n, g_ref[...], NN)
        e_ref[...] = e.astype(jnp.bfloat16)
        phi = lower(e - n.T - mxu(e_ref[...], n, NT))
        n_ref[...] = n + phi - mxu(phi, n, NN)
        return carry

    lax.fori_loop(0, ROOT_ITERS, step, 0)
    x_ref[...] = ((diag.astype(jnp.float32) - n_ref[...]) * across).astype(jnp.bfloat16)


HALF = PW // 2
HBM = pl.BlockSpec(memory_space=pltpu.HBM)


def run_copies(found, dest, sems):
    copies = [
        pltpu.make_async_copy(part, dest.at[column, pl.ds(at * HALF, size)], sems.at[slot])
        for slot, (part, column, at, size) in enumerate(found)
    ]
    for copy in copies:
        copy.start()
    for copy in copies:
        copy.wait()


def fetch_tops(col, tops, dest, sems):
    u0, u2_u1, w0_w1, w2, w1, u1_u0, w0, u0_next, w0_next = tops
    found = {
        1: [(u0_next, 0, 0, HALF), (w0_next, 0, 1, HALF)],
        2: [(u2_u1, 1, 0, HALF), (w0_w1, 1, 1, HALF), (u1_u0, 0, 0, HALF), (w0, 0, 1, HALF)],
        3: [
            (u0, 0, 0, HALF),
            (w0_w1, 0, 1, HALF),
            (u2_u1, 2, 0, HALF),
            (w2, 2, 1, HALF),
            (u1_u0, 1, 0, HALF),
            (w1, 1, 1, HALF),
        ],
    }
    for column, parts in found.items():

        @pl.when(col == column)
        def _():
            run_copies(parts, dest, sems)


def fetch_rows(col, parts, dest, sems):
    near, wrap = parts[:2]
    if len(parts) == 4:
        far = [(parts[2], 0, HALF), (parts[3], 1, HALF)]
    else:
        far = [(parts[2], 0, PW)]
    found = {
        1: [(near, 0, 0, PW)],
        2: [(near, 1, 0, PW)] + [(part, 0, at, size) for part, at, size in far],
        3: [(near, 2, 0, PW), (wrap, 0, 0, PW)] + [(part, 1, at, size) for part, at, size in far],
    }
    for column, parts in found.items():

        @pl.when(col == column)
        def _():
            run_copies(parts, dest, sems)


def factor_kernel(where_ref, own, *refs):
    tops, outs = refs[:9], refs[9:17]
    t_ref, s_ref, l_ref, x_ref, r_ref, g_ref, n_ref, e_ref, sems = refs[17:]
    col = where_ref[1]

    @pl.when(where_ref[0] == 0)
    def _():
        mine = pltpu.make_async_copy(own, t_ref.at[col], sems.at[6])
        mine.start()
        fetch_tops(col, tops, t_ref, sems)
        mine.wait()

        def rows_of(i):
            return pl.ds(pl.multiple_of(i * TILE, TILE), TILE)

        @pl.loop(0, col + 1)
        def _(i):
            @pl.loop(0, i + 1)
            def _(j):
                low = t_ref[j, rows_of(i), :].astype(jnp.float32)
                high = t_ref[i, rows_of(j), :].astype(jnp.float32)
                s_ref[i, j] = 0.5 * (low + high.T)

        @pl.loop(0, col + 1)
        def _(j):
            leaf_inverse(s_ref.at[j, j], x_ref.at[j], g_ref, n_ref, e_ref)

            @pl.loop(j + 1, col + 1)
            def _(i):
                l_ref[i, j] = mxu(s_ref[i, j], x_ref[j], NT).astype(jnp.bfloat16)

                @pl.loop(j + 1, i + 1)
                def _(k):
                    s_ref[i, k] = s_ref[i, k] - mxu(l_ref[i, j], l_ref[k, j], NT)

        r_ref[col] = x_ref[col]

        @pl.loop(0, BLOCKS)
        def _(step):
            k = BLOCKS - 1 - step

            @pl.when(k > col)
            def _():
                r_ref[k] = jnp.zeros((TILE, TILE), jnp.bfloat16)

            @pl.when(k < col)
            def _():
                n_ref[...] = jnp.zeros((TILE, TILE), jnp.float32)

                @pl.loop(k + 1, col + 1)
                def _(m):
                    n_ref[...] += mxu(r_ref[m], l_ref[m, k], NN)

                r_ref[k] = (-mxu(n_ref[...], x_ref[k], NN)).astype(jnp.bfloat16)

        for z in range(8):
            for k in range(BLOCKS):
                outs[z][:, k * TILE : (k + 1) * TILE] = r_ref[k, z * 64 : (z + 1) * 64, :]


HBM = pl.BlockSpec(memory_space=pltpu.HBM)


def factor_rows(where, own, tops):
    return pl.pallas_call(
        factor_kernel,
        out_shape=[jax.ShapeDtypeStruct((64, PW), jnp.bfloat16)] * 8,
        in_specs=[pl.BlockSpec(memory_space=pltpu.SMEM)] + [HBM] * 10,
        out_specs=[pl.BlockSpec(memory_space=pltpu.VMEM)] * 8,
        scratch_shapes=[
            pltpu.VMEM((BLOCKS, PW, TILE), jnp.bfloat16),
            pltpu.VMEM((BLOCKS, BLOCKS, TILE, TILE), jnp.float32),
            pltpu.VMEM((BLOCKS, BLOCKS, TILE, TILE), jnp.bfloat16),
            pltpu.VMEM((BLOCKS, TILE, TILE), jnp.bfloat16),
            pltpu.VMEM((BLOCKS, TILE, TILE), jnp.bfloat16),
            pltpu.VMEM((TILE, TILE), jnp.float32),
            pltpu.VMEM((TILE, TILE), jnp.float32),
            pltpu.VMEM((TILE, TILE), jnp.bfloat16),
            pltpu.SemaphoreType.DMA((7,)),
        ],
        compiler_params=pltpu.CompilerParams(vmem_limit_bytes=56 << 20),
        name="factor_rows",
    )(where, own, *tops)


CHUNKS = 6


def apply_kernel(where_ref, own, *refs):
    main, late, tops = refs[:4], refs[4:7], refs[7:16]
    chunks = refs[16 : 16 + CHUNKS]
    out, p_ref, r_ref, acc_ref, psems, rsems = refs[17 + CHUNKS :]
    group, col, z, core = where_ref[0], where_ref[1], where_ref[2], where_ref[3]
    sign = 1 - 2 * core
    copies = []

    def place(part, at, size):
        rows = pl.ds(pl.multiple_of(at, size), size)
        copies.append(pltpu.make_async_copy(part, r_ref.at[rows], rsems.at[len(copies)]))

    swapped = chunks[5]
    place(chunks[0], z * 64, 64)
    for by in range(1, 4):
        place(chunks[by], lax.rem(z - sign * by + 8, 8) * 64, 64)
        place(swapped.at[pl.ds(by * 64 - 64, 64)], lax.rem(z + sign * by + 8, 8) * 64, 64)
    place(chunks[4], lax.rem(z + 4, 8) * 64 + core * 32, 32)
    place(swapped.at[pl.ds(192, 32)], lax.rem(z + 4, 8) * 64 + (1 - core) * 32, 32)
    copies.append(pltpu.make_async_copy(own, p_ref.at[col], psems.at[6]))
    for copy in copies:
        copy.start()

    @pl.when(group == 0)
    def _():
        fetch_tops(col, tops, p_ref, psems)

    for index, parts in ((1, main), (2, late)):

        @pl.when(group == index)
        def _():
            fetch_rows(col, parts, p_ref, psems)

    for copy in copies:
        copy.wait()

    @pl.loop(0, PW // TILE)
    def _(tile):
        at = pl.ds(pl.multiple_of(tile * TILE, TILE), TILE)
        acc_ref[...] = mxu(r_ref[:, :TILE], p_ref[0, at, :], NT)
        for k in range(1, BLOCKS):

            @pl.when(k <= col)
            def _():
                acc_ref[...] += mxu(r_ref[:, k * TILE : (k + 1) * TILE], p_ref[k, at, :], NT)

        out[:, at] = acc_ref[...].astype(jnp.bfloat16)


def apply_rows(where, own, main, late, tops, chunks, token):
    return pl.pallas_call(
        apply_kernel,
        out_shape=jax.ShapeDtypeStruct((TILE, PW), jnp.bfloat16),
        in_specs=[pl.BlockSpec(memory_space=pltpu.SMEM)] + [HBM] * (18 + CHUNKS),
        out_specs=pl.BlockSpec(memory_space=pltpu.VMEM),
        scratch_shapes=[
            pltpu.VMEM((BLOCKS, PW, TILE), jnp.bfloat16),
            pltpu.VMEM((TILE, PW), jnp.bfloat16),
            pltpu.VMEM((TILE, TILE), jnp.float32),
            pltpu.SemaphoreType.DMA((7,)),
            pltpu.SemaphoreType.DMA((9,)),
        ],
        compiler_params=pltpu.CompilerParams(vmem_limit_bytes=40 << 20),
        name="apply_rows",
    )(where, own, *main, *late, *tops, *chunks, token)


def device(child, z, ylo, core, col):
    return (child * 32 + z * 4 + ylo * 2 + core) * 4 + col


def pairs_of(move):
    found = []
    for child in range(2):
        for z in range(8):
            for ylo in range(2):
                for core in range(2):
                    for col in range(4):
                        target = move(child, z, ylo, core, col)
                        if target is not None:
                            found.append((device(child, z, ylo, core, col), device(*target)))
    return found


def owner(core, col):
    return device(0, 0, 0, core, col)


def moves(member, *steps):
    allowed = dict(steps)
    return pairs_of(
        lambda c, z, y, k, j: (c, z, y, k, allowed[j]) if member(c, z, y, k) and j in allowed else None
    )


def is_first(c, z, y, k):
    return (c, z, y, k) == (0, 0, 0, 0)


def is_second(c, z, y, k):
    return (c, z, y, k) == (0, 0, 0, 1)


def is_other(c, z, y, k):
    return (c, z, y) != (0, 0, 0)


def gather_part(part, member):
    wrap = lax.ppermute(part, ALL, moves(member, (0, 3), (1, 0)))
    near = lax.ppermute(part, ALL, moves(member, (0, 1), (1, 2), (2, 3)))
    return near, wrap


def gather_top(own, column):
    def send(part, *steps):
        return lax.ppermute(part, ALL, moves(is_first, *steps))

    upper, lower = own[:HALF], own[HALF:]
    first = jnp.where(column == 1, lower, upper)
    u0 = send(first, (0, 3), (1, 0))
    u2_u1 = send(upper, (2, 3), (1, 2))
    w0_w1 = send(lower, (0, 3), (1, 2))
    w2 = send(lower, (2, 3))
    w1 = send(u0, (0, 3))
    u1_u0 = send(jnp.where(column == 3, u0, u2_u1), (2, 3), (3, 2))
    w0 = send(w0_w1, (3, 2))
    upper, lower, w1 = lax.optimization_barrier((upper, lower, w1))
    u0_next = send(upper, (0, 1))
    w0_next = send(lower, (0, 1))
    return [u0, u2_u1, w0_w1, w2, w1, u1_u0, w0, u0_next, w0_next]


def spread_rows(chunks, z, y, core, early):
    kept = chunks[0]
    total = None
    for k in range(1, 8):
        pairs = pairs_of(
            lambda c, zz, yy, kk, j: (0, k, 0, 0, j) if (c, zz, yy, kk) == (0, 0, 0, 0) else None
        )
        got = lax.ppermute(chunks[k], ALL, pairs)
        total = got if total is None else total + got
    chunk = jnp.where(z == 0, kept, total)
    chunk, *early = lax.optimization_barrier((chunk, *early))
    total = None
    for to in (1, 3, 2):
        pairs = pairs_of(
            lambda c, zz, yy, kk, j: (to // 2, zz, to % 2, 0, j) if (c, yy, kk) == (0, 0, 0) else None
        )
        got = lax.ppermute(chunk, ALL, pairs)
        total = got if total is None else total + got
    chunk = jnp.where(y == 0, chunk, total)
    got = lax.ppermute(
        chunk, ALL, pairs_of(lambda c, zz, yy, kk, j: (c, zz, yy, 1, j) if kk == 0 else None)
    )
    chunk = jnp.where(core == 0, chunk, got)
    swap = pairs_of(lambda c, zz, yy, kk, j: (c, zz, yy, 1 - kk, j))
    across = pairs_of(lambda c, zz, yy, kk, j: (c, (zz + 4) % 8, yy, kk, j))
    part = lax.dynamic_slice_in_dim(chunk, core * 32, 32, 0)
    half = lax.ppermute(part, ALL, across)
    direct = {}
    for by in (3, 2, 1):
        pairs = pairs_of(lambda c, zz, yy, kk, j: (c, (zz + (1 - 2 * kk) * by) % 8, yy, kk, j))
        direct[by] = lax.ppermute(chunk, ALL, pairs)
    mine = [direct[by] for by in (1, 2, 3)] + [half]
    theirs = lax.ppermute(jnp.concatenate(mine, axis=0), ALL, swap)
    return [chunk] + mine + [theirs], *early


def shards(front, left_factors, right_factors):
    side = lax.axis_index("child")
    row = lax.axis_index("row")
    column = lax.axis_index("col")
    z, y, core = row // 4, 2 * side + (row // 2) % 2, row % 2
    tiles = right_factors.shape[1] // 2
    left_all = left_factors[0, 0].reshape(RANK, 2 * tiles, TILE).transpose(1, 0, 2)
    both = jnp.stack([left_all, right_factors[0]])
    sent = lax.dynamic_slice_in_dim(both, (1 - side) * tiles, tiles, 1)
    kept = lax.dynamic_slice_in_dim(both, side * tiles, tiles, 1)
    got = lax.ppermute(
        sent, ALL, pairs_of(lambda c, zz, yy, kk, j: (1 - c, zz, yy, kk, j))
    )
    factors = jnp.concatenate([kept, got], axis=2)
    update = jnp.einsum("trk,trn->tkn", factors[0], factors[1], preferred_element_type=jnp.float32)
    own = (front.astype(jnp.float32) - update.reshape(PW, TILE)).astype(jnp.bfloat16)
    tops = gather_top(own, column)
    near, wrap = gather_part(own, is_other)
    token = lax.ppermute(
        near[:8, :128] + wrap[:8, :128],
        ALL,
        [(device(0, 1, 0, 0, j), owner(1, j)) for j in range(4)],
    )
    own_late, token = lax.optimization_barrier((own, token))
    late_near = lax.ppermute(own_late, ALL, moves(is_second, (0, 1), (1, 2), (2, 3)))
    late_wrap = lax.ppermute(own_late, ALL, moves(is_second, (0, 3)))
    group = jnp.where(jnp.logical_and(y == 0, z == 0), 2 * core, 1)
    where = jnp.stack([group, column, z, core]).astype(jnp.int32)
    where, near, wrap, near_a, wrap_b, late_near = lax.optimization_barrier(
        (where, near, wrap, near[:HALF], wrap[HALF:], late_near)
    )
    upper = lax.ppermute(near_a, ALL, moves(is_other, (1, 2), (2, 3)))
    lower = lax.ppermute(wrap_b, ALL, moves(is_other, (0, 3), (3, 2)))
    late_far = lax.ppermute(late_near, ALL, moves(is_second, (1, 2), (2, 3)))
    chunks = factor_rows(where, own, tops)
    chunks, upper, lower, late_wrap, late_far = spread_rows(
        chunks, z, y, core, (upper, lower, late_wrap, late_far)
    )
    main = [near, wrap, upper, lower]
    late = [late_near, late_wrap, late_far]
    return apply_rows(where, own, main, late, tops, chunks, token)


def solution(mesh):
    in_specs = (
        P(("row", "child"), "col"),
        P("child", "col", None, "row"),
        P("child", "row", None, "col"),
    )
    out_specs = P("col", ("row", "child"))
    return jax.shard_map(shards, mesh=mesh, in_specs=in_specs, out_specs=out_specs, check_vma=False)
```

```python
import functools

import jax
import jax.numpy as jnp
from jax import lax
from jax.experimental import pallas as pl
from jax.experimental.pallas import tpu as pltpu
from jax.sharding import PartitionSpec as P

TILE = 512
RANK = 64
PW = 2048
BLOCKS = PW // TILE
ROOT_ITERS = 3
ALL = ("child", "row", "col")
NT = (((1,), (1,)), ((), ()))
NN = (((1,), (0,)), ((), ()))


def mxu(left, right, dims):
    return lax.dot_general(
        left.astype(jnp.bfloat16),
        right.astype(jnp.bfloat16),
        dims,
        preferred_element_type=jnp.float32,
    )


def leaf_inverse(tile_ref, x_ref, g_ref, n_ref, e_ref):
    rows = lax.broadcasted_iota(jnp.int32, (TILE, TILE), 0)
    cols = lax.broadcasted_iota(jnp.int32, (TILE, TILE), 1)
    diag = rows == cols
    tile = tile_ref[...]
    picked = jnp.where(diag, tile, 0.0)
    down = lax.rsqrt(jnp.sum(picked, axis=1, keepdims=True))
    across = lax.rsqrt(jnp.sum(picked, axis=0, keepdims=True))
    gram = tile * down * across - diag.astype(jnp.float32)

    def lower(mat):
        return jnp.where(rows > cols, mat, jnp.where(diag, 0.5 * mat, 0.0))

    g_ref[...] = gram
    n_ref[...] = lower(gram)

    def step(_, carry):
        n = n_ref[...]
        e = g_ref[...] - n - mxu(n, g_ref[...], NN)
        e_ref[...] = e.astype(jnp.bfloat16)
        phi = lower(e - n.T - mxu(e_ref[...], n, NT))
        n_ref[...] = n + phi - mxu(phi, n, NN)
        return carry

    lax.fori_loop(0, ROOT_ITERS, step, 0)
    x_ref[...] = ((diag.astype(jnp.float32) - n_ref[...]) * across).astype(jnp.bfloat16)


HALF = PW // 2
HBM = pl.BlockSpec(memory_space=pltpu.HBM)


def run_copies(found, dest, sems):
    copies = [
        pltpu.make_async_copy(part, dest.at[column, pl.ds(at * HALF, size)], sems.at[slot])
        for slot, (part, column, at, size) in enumerate(found)
    ]
    for copy in copies:
        copy.start()
    for copy in copies:
        copy.wait()


def fetch_rows(col, parts, dest, sems):
    near, wrap, far = parts
    found = {
        1: [(near, 0, 0, PW)],
        2: [(near, 1, 0, PW), (far, 0, 0, PW)],
        3: [(near, 2, 0, PW), (wrap, 0, 0, PW), (far, 1, 0, PW)],
    }
    for column, copies in found.items():

        @pl.when(col == column)
        def _():
            run_copies(copies, dest, sems)


def factor_kernel(where_ref, own, *refs):
    parts, outs = refs[:3], refs[3:11]
    t_ref, s_ref, l_ref, x_ref, r_ref, g_ref, n_ref, e_ref, sems = refs[11:]
    col = where_ref[2]

    @pl.when(where_ref[0] == 1)
    def _():
        mine = pltpu.make_async_copy(own, t_ref.at[col], sems.at[3])
        mine.start()
        fetch_rows(col, parts, t_ref, sems)
        mine.wait()

        def rows_of(i):
            return pl.ds(pl.multiple_of(i * TILE, TILE), TILE)

        @pl.loop(0, col + 1)
        def _(i):
            @pl.loop(0, i + 1)
            def _(j):
                low = t_ref[j, rows_of(i), :].astype(jnp.float32)
                high = t_ref[i, rows_of(j), :].astype(jnp.float32)
                s_ref[i, j] = 0.5 * (low + high.T)

        @pl.loop(0, col + 1)
        def _(j):
            leaf_inverse(s_ref.at[j, j], x_ref.at[j], g_ref, n_ref, e_ref)

            @pl.loop(j + 1, col + 1)
            def _(i):
                l_ref[i, j] = mxu(s_ref[i, j], x_ref[j], NT).astype(jnp.bfloat16)

                @pl.loop(j + 1, i + 1)
                def _(k):
                    s_ref[i, k] = s_ref[i, k] - mxu(l_ref[i, j], l_ref[k, j], NT)

        r_ref[col] = x_ref[col]

        @pl.loop(0, BLOCKS)
        def _(step):
            k = BLOCKS - 1 - step

            @pl.when(k > col)
            def _():
                r_ref[k] = jnp.zeros((TILE, TILE), jnp.bfloat16)

            @pl.when(k < col)
            def _():
                n_ref[...] = jnp.zeros((TILE, TILE), jnp.float32)

                @pl.loop(k + 1, col + 1)
                def _(m):
                    n_ref[...] += mxu(r_ref[m], l_ref[m, k], NN)

                r_ref[k] = (-mxu(n_ref[...], x_ref[k], NN)).astype(jnp.bfloat16)

        for z in range(8):
            for k in range(BLOCKS):
                outs[z][:, k * TILE : (k + 1) * TILE] = r_ref[k, z * 64 : (z + 1) * 64, :]


HBM = pl.BlockSpec(memory_space=pltpu.HBM)


def factor_rows(where, own, parts):
    return pl.pallas_call(
        factor_kernel,
        out_shape=[jax.ShapeDtypeStruct((64, PW), jnp.bfloat16)] * 8,
        in_specs=[pl.BlockSpec(memory_space=pltpu.SMEM)] + [HBM] * 4,
        out_specs=[pl.BlockSpec(memory_space=pltpu.VMEM)] * 8,
        scratch_shapes=[
            pltpu.VMEM((BLOCKS, PW, TILE), jnp.bfloat16),
            pltpu.VMEM((BLOCKS, BLOCKS, TILE, TILE), jnp.float32),
            pltpu.VMEM((BLOCKS, BLOCKS, TILE, TILE), jnp.bfloat16),
            pltpu.VMEM((BLOCKS, TILE, TILE), jnp.bfloat16),
            pltpu.VMEM((BLOCKS, TILE, TILE), jnp.bfloat16),
            pltpu.VMEM((TILE, TILE), jnp.float32),
            pltpu.VMEM((TILE, TILE), jnp.float32),
            pltpu.VMEM((TILE, TILE), jnp.bfloat16),
            pltpu.SemaphoreType.DMA((4,)),
        ],
        compiler_params=pltpu.CompilerParams(vmem_limit_bytes=56 << 20),
        name="factor_rows",
    )(where, own, *parts)


CHUNKS = 6


def apply_kernel(where_ref, own, *refs):
    main, late = refs[:3], refs[3:6]
    chunks = refs[6 : 6 + CHUNKS]
    out, p_ref, r_ref, psems, rsems = refs[7 + CHUNKS :]
    second, col, z, core = where_ref[1], where_ref[2], where_ref[3], where_ref[4]
    sign = 1 - 2 * core
    copies = []

    def place(part, at, size):
        rows = pl.ds(pl.multiple_of(at, size), size)
        copies.append(pltpu.make_async_copy(part, r_ref.at[rows], rsems.at[len(copies)]))

    swapped = chunks[5]
    place(chunks[0], z * 64, 64)
    for by in range(1, 4):
        place(chunks[by], lax.rem(z - sign * by + 8, 8) * 64, 64)
        place(swapped.at[pl.ds(by * 64 - 64, 64)], lax.rem(z + sign * by + 8, 8) * 64, 64)
    place(chunks[4], lax.rem(z + 4, 8) * 64 + core * 32, 32)
    place(swapped.at[pl.ds(192, 32)], lax.rem(z + 4, 8) * 64 + (1 - core) * 32, 32)
    copies.append(pltpu.make_async_copy(own, p_ref.at[col], psems.at[3]))
    for copy in copies:
        copy.start()

    for index, parts in ((0, main), (1, late)):

        @pl.when(second == index)
        def _():
            fetch_rows(col, parts, p_ref, psems)

    for copy in copies:
        copy.wait()

    for last in range(BLOCKS):

        @pl.when(col == last)
        def _():
            @pl.loop(0, PW // TILE)
            def _(tile):
                at = pl.ds(pl.multiple_of(tile * TILE, TILE), TILE)
                acc = mxu(r_ref[:, :TILE], p_ref[0, at, :], NT)
                for k in range(1, last + 1):
                    acc = acc + mxu(r_ref[:, k * TILE : (k + 1) * TILE], p_ref[k, at, :], NT)
                out[:, at] = acc.astype(jnp.bfloat16)


def apply_rows(where, own, main, late, chunks, token):
    return pl.pallas_call(
        apply_kernel,
        out_shape=jax.ShapeDtypeStruct((TILE, PW), jnp.bfloat16),
        in_specs=[pl.BlockSpec(memory_space=pltpu.SMEM)] + [HBM] * (8 + CHUNKS),
        out_specs=pl.BlockSpec(memory_space=pltpu.VMEM),
        scratch_shapes=[
            pltpu.VMEM((BLOCKS, PW, TILE), jnp.bfloat16),
            pltpu.VMEM((TILE, PW), jnp.bfloat16),
            pltpu.SemaphoreType.DMA((4,)),
            pltpu.SemaphoreType.DMA((9,)),
        ],
        compiler_params=pltpu.CompilerParams(vmem_limit_bytes=40 << 20),
        name="apply_rows",
    )(where, own, *main, *late, *chunks, token)


def device(child, z, ylo, core, col):
    return (child * 32 + z * 4 + ylo * 2 + core) * 4 + col


def pairs_of(move):
    found = []
    for child in range(2):
        for z in range(8):
            for ylo in range(2):
                for core in range(2):
                    for col in range(4):
                        target = move(child, z, ylo, core, col)
                        if target is not None:
                            found.append((device(child, z, ylo, core, col), device(*target)))
    return found


def owner(core, col):
    return device(0, 0, 0, core, col)


def moves(member, *steps):
    allowed = dict(steps)
    return pairs_of(
        lambda c, z, y, k, j: (c, z, y, k, allowed[j]) if member(c, z, y, k) and j in allowed else None
    )


def is_second(c, z, y, k):
    return (c, z, y, k) == (0, 0, 0, 1)


def is_other(c, z, y, k):
    return (c, z, y, k) != (0, 0, 0, 1)


def gather(part, member):
    near = lax.ppermute(part, ALL, moves(member, (0, 1), (1, 2), (2, 3)))
    wrap = lax.ppermute(part, ALL, moves(member, (0, 3)))
    near, wrap = lax.optimization_barrier((near, wrap))
    far = lax.ppermute(near, ALL, moves(member, (1, 2), (2, 3)))
    return [near, wrap, far]


def spread_rows(chunks, z, y, core):
    kept = chunks[0]
    total = None
    for k in range(1, 8):
        pairs = pairs_of(
            lambda c, zz, yy, kk, j: (0, k, 0, 0, j) if (c, zz, yy, kk) == (0, 0, 0, 0) else None
        )
        got = lax.ppermute(chunks[k], ALL, pairs)
        total = got if total is None else total + got
    chunk = jnp.where(z == 0, kept, total)
    total = None
    for to in (1, 3, 2):
        pairs = pairs_of(
            lambda c, zz, yy, kk, j: (to // 2, zz, to % 2, 0, j) if (c, yy, kk) == (0, 0, 0) else None
        )
        got = lax.ppermute(chunk, ALL, pairs)
        total = got if total is None else total + got
    chunk = jnp.where(y == 0, chunk, total)
    got = lax.ppermute(
        chunk, ALL, pairs_of(lambda c, zz, yy, kk, j: (c, zz, yy, 1, j) if kk == 0 else None)
    )
    chunk = jnp.where(core == 0, chunk, got)
    swap = pairs_of(lambda c, zz, yy, kk, j: (c, zz, yy, 1 - kk, j))
    across = pairs_of(lambda c, zz, yy, kk, j: (c, (zz + 4) % 8, yy, kk, j))
    part = lax.dynamic_slice_in_dim(chunk, core * 32, 32, 0)
    half = lax.ppermute(part, ALL, across)
    direct = {}
    for by in (3, 2, 1):
        pairs = pairs_of(lambda c, zz, yy, kk, j: (c, (zz + (1 - 2 * kk) * by) % 8, yy, kk, j))
        direct[by] = lax.ppermute(chunk, ALL, pairs)
    mine = [direct[by] for by in (1, 2, 3)] + [half]
    theirs = lax.ppermute(jnp.concatenate(mine, axis=0), ALL, swap)
    return [chunk] + mine + [theirs]


def shards(front, left_factors, right_factors):
    side = lax.axis_index("child")
    row = lax.axis_index("row")
    column = lax.axis_index("col")
    z, y, core = row // 4, 2 * side + (row // 2) % 2, row % 2
    tiles = right_factors.shape[1] // 2
    left_all = left_factors[0, 0].reshape(RANK, 2 * tiles, TILE).transpose(1, 0, 2)
    both = jnp.stack([left_all, right_factors[0]])
    sent = lax.dynamic_slice_in_dim(both, (1 - side) * tiles, tiles, 1)
    kept = lax.dynamic_slice_in_dim(both, side * tiles, tiles, 1)
    got = lax.ppermute(
        sent, ALL, pairs_of(lambda c, zz, yy, kk, j: (1 - c, zz, yy, kk, j))
    )
    factors = jnp.concatenate([kept, got], axis=2)
    update = jnp.einsum("trk,trn->tkn", factors[0], factors[1], preferred_element_type=jnp.float32)
    own = (front.astype(jnp.float32) - update.reshape(PW, TILE)).astype(jnp.bfloat16)
    main = gather(own, is_other)
    token = lax.ppermute(
        main[0][:8, :128] + main[1][:8, :128],
        ALL,
        [(device(0, 1, 0, 0, j), device(0, 0, 0, 1, j)) for j in range(4)],
    )
    own_late, token = lax.optimization_barrier((own, token))
    late = gather(own_late, is_second)
    second = jnp.logical_and(jnp.logical_and(y == 0, z == 0), core == 1)
    first = jnp.logical_and(jnp.logical_and(y == 0, z == 0), core == 0)
    where = jnp.stack([first, second, column, z, core]).astype(jnp.int32)
    where, *gathered = lax.optimization_barrier((where, *main, *late))
    main, late = gathered[:3], gathered[3:]
    chunks = factor_rows(where, own, main)
    chunks = spread_rows(chunks, z, y, core)
    return apply_rows(where, own, main, late, chunks, token)


def solution(mesh):
    in_specs = (
        P(("row", "child"), "col"),
        P("child", "col", None, "row"),
        P("child", "row", None, "col"),
    )
    out_specs = P("col", ("row", "child"))
    return jax.shard_map(shards, mesh=mesh, in_specs=in_specs, out_specs=out_specs, check_vma=False)
```

```python
import functools

import jax
import jax.numpy as jnp
from jax import lax
from jax.experimental import pallas as pl
from jax.experimental.pallas import tpu as pltpu
from jax.sharding import PartitionSpec as P

TILE = 512
RANK = 64
PW = 2048
BLOCKS = PW // TILE
ROOT_ITERS = 3
ALL = ("child", "row", "col")
NT = (((1,), (1,)), ((), ()))
NN = (((1,), (0,)), ((), ()))


def mxu(left, right, dims):
    return lax.dot_general(
        left.astype(jnp.bfloat16),
        right.astype(jnp.bfloat16),
        dims,
        preferred_element_type=jnp.float32,
    )


def leaf_inverse(tile_ref, x_ref, g_ref, n_ref, e_ref):
    rows = lax.broadcasted_iota(jnp.int32, (TILE, TILE), 0)
    cols = lax.broadcasted_iota(jnp.int32, (TILE, TILE), 1)
    diag = rows == cols
    tile = tile_ref[...]
    picked = jnp.where(diag, tile, 0.0)
    down = lax.rsqrt(jnp.sum(picked, axis=1, keepdims=True))
    across = lax.rsqrt(jnp.sum(picked, axis=0, keepdims=True))
    gram = tile * down * across - diag.astype(jnp.float32)

    def lower(mat):
        return jnp.where(rows > cols, mat, jnp.where(diag, 0.5 * mat, 0.0))

    g_ref[...] = gram
    n_ref[...] = lower(gram)

    def step(_, carry):
        n = n_ref[...]
        e = g_ref[...] - n - mxu(n, g_ref[...], NN)
        e_ref[...] = e.astype(jnp.bfloat16)
        phi = lower(e - n.T - mxu(e_ref[...], n, NT))
        n_ref[...] = n + phi - mxu(phi, n, NN)
        return carry

    lax.fori_loop(0, ROOT_ITERS, step, 0)
    x_ref[...] = ((diag.astype(jnp.float32) - n_ref[...]) * across).astype(jnp.bfloat16)


HALF = PW // 2
HBM = pl.BlockSpec(memory_space=pltpu.HBM)


def run_copies(found, dest, sems):
    copies = [
        pltpu.make_async_copy(part, dest.at[column, pl.ds(at * HALF, size)], sems.at[slot])
        for slot, (part, column, at, size) in enumerate(found)
    ]
    for copy in copies:
        copy.start()
    for copy in copies:
        copy.wait()


def fetch_rows(col, parts, dest, sems):
    near, wrap, far = parts
    found = {
        1: [(near, 0, 0, PW)],
        2: [(near, 1, 0, PW), (far, 0, 0, PW)],
        3: [(near, 2, 0, PW), (wrap, 0, 0, PW), (far, 1, 0, PW)],
    }
    for column, copies in found.items():

        @pl.when(col == column)
        def _():
            run_copies(copies, dest, sems)


def factor_kernel(where_ref, own, *refs):
    parts, outs = refs[:3], refs[3:11]
    t_ref, s_ref, l_ref, x_ref, r_ref, g_ref, n_ref, e_ref, sems = refs[11:]
    col = where_ref[2]

    @pl.when(where_ref[0] == 1)
    def _():
        mine = pltpu.make_async_copy(own, t_ref.at[col], sems.at[3])
        mine.start()
        fetch_rows(col, parts, t_ref, sems)
        mine.wait()

        def rows_of(i):
            return pl.ds(pl.multiple_of(i * TILE, TILE), TILE)

        @pl.loop(0, col + 1)
        def _(i):
            @pl.loop(0, i + 1)
            def _(j):
                low = t_ref[j, rows_of(i), :].astype(jnp.float32)
                high = t_ref[i, rows_of(j), :].astype(jnp.float32)
                s_ref[i, j] = 0.5 * (low + high.T)

        @pl.loop(0, col + 1)
        def _(j):
            leaf_inverse(s_ref.at[j, j], x_ref.at[j], g_ref, n_ref, e_ref)

            @pl.loop(j + 1, col + 1)
            def _(i):
                l_ref[i, j] = mxu(s_ref[i, j], x_ref[j], NT).astype(jnp.bfloat16)

                @pl.loop(j + 1, i + 1)
                def _(k):
                    s_ref[i, k] = s_ref[i, k] - mxu(l_ref[i, j], l_ref[k, j], NT)

        r_ref[col] = x_ref[col]

        @pl.loop(0, BLOCKS)
        def _(step):
            k = BLOCKS - 1 - step

            @pl.when(k > col)
            def _():
                r_ref[k] = jnp.zeros((TILE, TILE), jnp.bfloat16)

            @pl.when(k < col)
            def _():
                n_ref[...] = jnp.zeros((TILE, TILE), jnp.float32)

                @pl.loop(k + 1, col + 1)
                def _(m):
                    n_ref[...] += mxu(r_ref[m], l_ref[m, k], NN)

                r_ref[k] = (-mxu(n_ref[...], x_ref[k], NN)).astype(jnp.bfloat16)

        for z in range(8):
            for k in range(BLOCKS):
                outs[z][:, k * TILE : (k + 1) * TILE] = r_ref[k, z * 64 : (z + 1) * 64, :]


HBM = pl.BlockSpec(memory_space=pltpu.HBM)


def factor_rows(where, own, parts):
    return pl.pallas_call(
        factor_kernel,
        out_shape=[jax.ShapeDtypeStruct((64, PW), jnp.bfloat16)] * 8,
        in_specs=[pl.BlockSpec(memory_space=pltpu.SMEM)] + [HBM] * 4,
        out_specs=[pl.BlockSpec(memory_space=pltpu.VMEM)] * 8,
        scratch_shapes=[
            pltpu.VMEM((BLOCKS, PW, TILE), jnp.bfloat16),
            pltpu.VMEM((BLOCKS, BLOCKS, TILE, TILE), jnp.float32),
            pltpu.VMEM((BLOCKS, BLOCKS, TILE, TILE), jnp.bfloat16),
            pltpu.VMEM((BLOCKS, TILE, TILE), jnp.bfloat16),
            pltpu.VMEM((BLOCKS, TILE, TILE), jnp.bfloat16),
            pltpu.VMEM((TILE, TILE), jnp.float32),
            pltpu.VMEM((TILE, TILE), jnp.float32),
            pltpu.VMEM((TILE, TILE), jnp.bfloat16),
            pltpu.SemaphoreType.DMA((4,)),
        ],
        compiler_params=pltpu.CompilerParams(vmem_limit_bytes=56 << 20),
        name="factor_rows",
    )(where, own, *parts)


CHUNKS = 6


def apply_kernel(where_ref, own, *refs):
    main, late = refs[:3], refs[3:6]
    chunks = refs[6 : 6 + CHUNKS]
    out, p_ref, r_ref, psems, rsems = refs[7 + CHUNKS :]
    second, col, z, core = where_ref[1], where_ref[2], where_ref[3], where_ref[4]
    sign = 1 - 2 * core
    copies = []

    def place(part, at, size):
        rows = pl.ds(pl.multiple_of(at, size), size)
        copies.append(pltpu.make_async_copy(part, r_ref.at[rows], rsems.at[len(copies)]))

    swapped = chunks[5]
    place(chunks[0], z * 64, 64)
    for by in range(1, 4):
        place(chunks[by], lax.rem(z - sign * by + 8, 8) * 64, 64)
        place(swapped.at[pl.ds(by * 64 - 64, 64)], lax.rem(z + sign * by + 8, 8) * 64, 64)
    place(chunks[4], lax.rem(z + 4, 8) * 64 + core * 32, 32)
    place(swapped.at[pl.ds(192, 32)], lax.rem(z + 4, 8) * 64 + (1 - core) * 32, 32)
    copies.append(pltpu.make_async_copy(own, p_ref.at[col], psems.at[3]))
    for copy in copies:
        copy.start()

    for index, parts in ((0, main), (1, late)):

        @pl.when(second == index)
        def _():
            fetch_rows(col, parts, p_ref, psems)

    for copy in copies:
        copy.wait()

    for last in range(BLOCKS):

        @pl.when(col == last)
        def _():
            @pl.loop(0, PW // TILE)
            def _(tile):
                at = pl.ds(pl.multiple_of(tile * TILE, TILE), TILE)
                acc = mxu(r_ref[:, :TILE], p_ref[0, at, :], NT)
                for k in range(1, last + 1):
                    acc = acc + mxu(r_ref[:, k * TILE : (k + 1) * TILE], p_ref[k, at, :], NT)
                out[:, at] = acc.astype(jnp.bfloat16)


def apply_rows(where, own, main, late, chunks, token):
    return pl.pallas_call(
        apply_kernel,
        out_shape=jax.ShapeDtypeStruct((TILE, PW), jnp.bfloat16),
        in_specs=[pl.BlockSpec(memory_space=pltpu.SMEM)] + [HBM] * (8 + CHUNKS),
        out_specs=pl.BlockSpec(memory_space=pltpu.VMEM),
        scratch_shapes=[
            pltpu.VMEM((BLOCKS, PW, TILE), jnp.bfloat16),
            pltpu.VMEM((TILE, PW), jnp.bfloat16),
            pltpu.SemaphoreType.DMA((4,)),
            pltpu.SemaphoreType.DMA((9,)),
        ],
        compiler_params=pltpu.CompilerParams(vmem_limit_bytes=40 << 20),
        name="apply_rows",
    )(where, own, *main, *late, *chunks, token)


def device(child, z, ylo, core, col):
    return (child * 32 + z * 4 + ylo * 2 + core) * 4 + col


def pairs_of(move):
    found = []
    for child in range(2):
        for z in range(8):
            for ylo in range(2):
                for core in range(2):
                    for col in range(4):
                        target = move(child, z, ylo, core, col)
                        if target is not None:
                            found.append((device(child, z, ylo, core, col), device(*target)))
    return found


def moves(member, *steps):
    allowed = dict(steps)
    return pairs_of(
        lambda c, z, y, k, j: (c, z, y, k, allowed[j]) if member(c, z, y, k) and j in allowed else None
    )


def is_second(c, z, y, k):
    return (c, y, k) == (0, 0, 1)


def is_other(c, z, y, k):
    return (c, y, k) != (0, 0, 1)


def gather(part, member):
    near = lax.ppermute(part, ALL, moves(member, (0, 1), (1, 2), (2, 3)))
    wrap = lax.ppermute(part, ALL, moves(member, (0, 3)))
    near, wrap = lax.optimization_barrier((near, wrap))
    far = lax.ppermute(near, ALL, moves(member, (1, 2), (2, 3)))
    return [near, wrap, far]


def spread_rows(chunks, z, y, core):
    kept = chunks[0]
    total = None
    for k in range(1, 8):
        pairs = pairs_of(
            lambda c, zz, yy, kk, j: (0, k, 0, 0, j) if (c, zz, yy, kk) == (0, 0, 0, 0) else None
        )
        got = lax.ppermute(chunks[k], ALL, pairs)
        total = got if total is None else total + got
    chunk = jnp.where(z == 0, kept, total)
    total = None
    for to in (1, 3, 2):
        pairs = pairs_of(
            lambda c, zz, yy, kk, j: (to // 2, zz, to % 2, 0, j) if (c, yy, kk) == (0, 0, 0) else None
        )
        got = lax.ppermute(chunk, ALL, pairs)
        total = got if total is None else total + got
    chunk = jnp.where(y == 0, chunk, total)
    got = lax.ppermute(
        chunk, ALL, pairs_of(lambda c, zz, yy, kk, j: (c, zz, yy, 1, j) if kk == 0 else None)
    )
    chunk = jnp.where(core == 0, chunk, got)
    swap = pairs_of(lambda c, zz, yy, kk, j: (c, zz, yy, 1 - kk, j))
    across = pairs_of(lambda c, zz, yy, kk, j: (c, (zz + 4) % 8, yy, kk, j))
    part = lax.dynamic_slice_in_dim(chunk, core * 32, 32, 0)
    half = lax.ppermute(part, ALL, across)
    direct = {}
    for by in (3, 2, 1):
        pairs = pairs_of(lambda c, zz, yy, kk, j: (c, (zz + (1 - 2 * kk) * by) % 8, yy, kk, j))
        direct[by] = lax.ppermute(chunk, ALL, pairs)
    mine = [direct[by] for by in (1, 2, 3)] + [half]
    theirs = lax.ppermute(jnp.concatenate(mine, axis=0), ALL, swap)
    return [chunk] + mine + [theirs]


def shards(front, left_factors, right_factors):
    side = lax.axis_index("child")
    row = lax.axis_index("row")
    column = lax.axis_index("col")
    z, y, core = row // 4, 2 * side + (row // 2) % 2, row % 2
    tiles = right_factors.shape[1] // 2
    left_all = left_factors[0, 0].reshape(RANK, 2 * tiles, TILE).transpose(1, 0, 2)
    both = jnp.stack([left_all, right_factors[0]])
    sent = lax.dynamic_slice_in_dim(both, (1 - side) * tiles, tiles, 1)
    kept = lax.dynamic_slice_in_dim(both, side * tiles, tiles, 1)
    got = lax.ppermute(
        sent, ALL, pairs_of(lambda c, zz, yy, kk, j: (1 - c, zz, yy, kk, j))
    )
    factors = jnp.concatenate([kept, got], axis=2)
    update = jnp.einsum("trk,trn->tkn", factors[0], factors[1], preferred_element_type=jnp.float32)
    own = (front.astype(jnp.float32) - update.reshape(PW, TILE)).astype(jnp.bfloat16)
    main = gather(own, is_other)
    token = lax.ppermute(
        main[0][:8, :128] + main[1][:8, :128],
        ALL,
        pairs_of(lambda c, zz, yy, kk, j: (0, zz, 0, 1, j) if (c, yy, kk) == (0, 1, 0) else None),
    )
    own_late, token = lax.optimization_barrier((own, token))
    late = gather(own_late, is_second)
    second = jnp.logical_and(y == 0, core == 1)
    first = jnp.logical_and(jnp.logical_and(y == 0, z == 0), core == 0)
    where = jnp.stack([first, second, column, z, core]).astype(jnp.int32)
    where, *gathered = lax.optimization_barrier((where, *main, *late))
    main, late = gathered[:3], gathered[3:]
    chunks = factor_rows(where, own, main)
    chunks = spread_rows(chunks, z, y, core)
    return apply_rows(where, own, main, late, chunks, token)


def solution(mesh):
    in_specs = (
        P(("row", "child"), "col"),
        P("child", "col", None, "row"),
        P("child", "row", None, "col"),
    )
    out_specs = P("col", ("row", "child"))
    return jax.shard_map(shards, mesh=mesh, in_specs=in_specs, out_specs=out_specs, check_vma=False)
```

```python
import functools

import jax
import jax.numpy as jnp
from jax import lax
from jax.experimental import pallas as pl
from jax.experimental.pallas import tpu as pltpu
from jax.sharding import PartitionSpec as P

TILE = 512
RANK = 64
PW = 2048
BLOCKS = PW // TILE
ROOT_ITERS = 3
ALL = ("child", "row", "col")
NT = (((1,), (1,)), ((), ()))
NN = (((1,), (0,)), ((), ()))


def mxu(left, right, dims):
    return lax.dot_general(
        left.astype(jnp.bfloat16),
        right.astype(jnp.bfloat16),
        dims,
        preferred_element_type=jnp.float32,
    )


def leaf_inverse(tile_ref, x_ref, g_ref, n_ref, nb_ref):
    part = TILE // 2
    top, low = slice(0, part), slice(part, TILE)
    diag = lax.broadcasted_iota(jnp.int32, (part, part), 0) == lax.broadcasted_iota(
        jnp.int32, (part, part), 1
    )
    under = lax.broadcasted_iota(jnp.int32, (part, part), 0) > lax.broadcasted_iota(
        jnp.int32, (part, part), 1
    )

    def lower(mat):
        return jnp.where(under, mat, jnp.where(diag, 0.5 * mat, 0.0))

    def scales(block):
        picked = jnp.where(diag, tile_ref[block, block], 0.0)
        return (
            lax.rsqrt(jnp.sum(picked, axis=1, keepdims=True)),
            lax.rsqrt(jnp.sum(picked, axis=0, keepdims=True)),
        )

    (down0, across0), (down1, across1) = scales(top), scales(low)
    eye = diag.astype(jnp.float32)
    g00 = tile_ref[top, top] * down0 * across0 - eye
    g10 = tile_ref[low, top] * down1 * across0
    g01 = tile_ref[top, low] * down0 * across1
    g11 = tile_ref[low, low] * down1 * across1 - eye
    g_ref[top, top] = g00.astype(jnp.bfloat16)
    g_ref[low, top] = g10.astype(jnp.bfloat16)
    g_ref[top, low] = g01.astype(jnp.bfloat16)
    g_ref[low, low] = g11.astype(jnp.bfloat16)
    n_ref[top, top] = lower(g00)
    n_ref[low, top] = g10
    n_ref[low, low] = lower(g11)
    nb_ref[top, top] = lower(g00).astype(jnp.bfloat16)
    nb_ref[low, top] = g10.astype(jnp.bfloat16)
    nb_ref[low, low] = lower(g11).astype(jnp.bfloat16)

    def step(_, carry):
        n00, n10, n11 = n_ref[top, top], n_ref[low, top], n_ref[low, low]
        b00, b10, b11 = nb_ref[top, top], nb_ref[low, top], nb_ref[low, low]
        scaled00 = tile_ref[top, top] * down0 * across0 - eye
        scaled10 = tile_ref[low, top] * down1 * across0
        scaled11 = tile_ref[low, low] * down1 * across1 - eye
        e00 = scaled00 - n00 - mxu(b00, g_ref[top, top], NN)
        e10 = scaled10 - n10 - mxu(nb_ref[low, :], g_ref[:, top], NN)
        e11 = scaled11 - n11 - mxu(nb_ref[low, :], g_ref[:, low], NN)
        c00, c10, c11 = e00.astype(jnp.bfloat16), e10.astype(jnp.bfloat16), e11.astype(jnp.bfloat16)
        p00 = lower(e00 - jnp.where(diag, n00, 0.0) - mxu(c00, b00, NT))
        p10 = e10 - mxu(c10, b00, NT)
        p11 = lower(
            e11 - jnp.where(diag, n11, 0.0) - mxu(c10, b10, NT) - mxu(c11, b11, NT)
        )
        f00, f10, f11 = p00.astype(jnp.bfloat16), p10.astype(jnp.bfloat16), p11.astype(jnp.bfloat16)
        n00 = n00 + p00 - mxu(f00, b00, NN)
        n10 = n10 + p10 - mxu(f10, b00, NN) - mxu(f11, b10, NN)
        n11 = n11 + p11 - mxu(f11, b11, NN)
        n_ref[top, top], n_ref[low, top], n_ref[low, low] = n00, n10, n11
        nb_ref[top, top] = n00.astype(jnp.bfloat16)
        nb_ref[low, top] = n10.astype(jnp.bfloat16)
        nb_ref[low, low] = n11.astype(jnp.bfloat16)
        return carry

    lax.fori_loop(0, ROOT_ITERS, step, 0)
    x_ref[top, top] = ((eye - n_ref[top, top]) * across0).astype(jnp.bfloat16)
    x_ref[top, low] = jnp.zeros((part, part), jnp.bfloat16)
    x_ref[low, top] = (-n_ref[low, top] * across0).astype(jnp.bfloat16)
    x_ref[low, low] = ((eye - n_ref[low, low]) * across1).astype(jnp.bfloat16)


HALF = PW // 2


def run_copies(found, dest, sems):
    copies = [
        pltpu.make_async_copy(part, dest.at[column, pl.ds(at * HALF, size)], sems.at[slot])
        for slot, (part, column, at, size) in enumerate(found)
    ]
    for copy in copies:
        copy.start()
    for copy in copies:
        copy.wait()


def fetch_rows(col, parts, dest, sems):
    near, wrap, upper, lower = parts
    found = {
        1: [(near, 0, 0, PW)],
        2: [(near, 1, 0, PW), (upper, 0, 0, HALF), (lower, 0, 1, HALF)],
        3: [(near, 2, 0, PW), (wrap, 0, 0, PW), (upper, 1, 0, HALF), (lower, 1, 1, HALF)],
    }
    for column, copies in found.items():

        @pl.when(col == column)
        def _():
            run_copies(copies, dest, sems)


def factor_kernel(where_ref, own, *refs):
    parts, outs = refs[:4], refs[4:12]
    t_ref, s_ref, l_ref, x_ref, r_ref, g_ref, n_ref, e_ref, sems = refs[12:]
    col = where_ref[2]

    @pl.when(where_ref[0] == 1)
    def _():
        mine = pltpu.make_async_copy(own, t_ref.at[col], sems.at[4])
        mine.start()
        fetch_rows(col, parts, t_ref, sems)
        mine.wait()

        def rows_of(i):
            return pl.ds(pl.multiple_of(i * TILE, TILE), TILE)

        @pl.loop(0, col + 1)
        def _(i):
            @pl.loop(0, i + 1)
            def _(j):
                low = t_ref[j, rows_of(i), :].astype(jnp.float32)
                high = t_ref[i, rows_of(j), :].astype(jnp.float32)
                s_ref[i, j] = 0.5 * (low + high.T)

        @pl.loop(0, col + 1)
        def _(j):
            leaf_inverse(s_ref.at[j, j], x_ref.at[j], g_ref, n_ref, e_ref)

            @pl.loop(j + 1, col + 1)
            def _(i):
                l_ref[i, j] = mxu(s_ref[i, j], x_ref[j], NT).astype(jnp.bfloat16)

                @pl.loop(j + 1, i + 1)
                def _(k):
                    s_ref[i, k] = s_ref[i, k] - mxu(l_ref[i, j], l_ref[k, j], NT)

        r_ref[col] = x_ref[col]

        @pl.loop(0, BLOCKS)
        def _(step):
            k = BLOCKS - 1 - step

            @pl.when(k > col)
            def _():
                r_ref[k] = jnp.zeros((TILE, TILE), jnp.bfloat16)

            @pl.when(k < col)
            def _():
                n_ref[...] = jnp.zeros((TILE, TILE), jnp.float32)

                @pl.loop(k + 1, col + 1)
                def _(m):
                    n_ref[...] += mxu(r_ref[m], l_ref[m, k], NN)

                r_ref[k] = (-mxu(n_ref[...], x_ref[k], NN)).astype(jnp.bfloat16)

        for z in range(8):
            for k in range(BLOCKS):
                outs[z][:, k * TILE : (k + 1) * TILE] = r_ref[k, z * 64 : (z + 1) * 64, :]


HBM = pl.BlockSpec(memory_space=pltpu.HBM)


def factor_rows(where, own, parts):
    return pl.pallas_call(
        factor_kernel,
        out_shape=[jax.ShapeDtypeStruct((64, PW), jnp.bfloat16)] * 8,
        in_specs=[pl.BlockSpec(memory_space=pltpu.SMEM)] + [HBM] * 5,
        out_specs=[pl.BlockSpec(memory_space=pltpu.VMEM)] * 8,
        scratch_shapes=[
            pltpu.VMEM((BLOCKS, PW, TILE), jnp.bfloat16),
            pltpu.VMEM((BLOCKS, BLOCKS, TILE, TILE), jnp.float32),
            pltpu.VMEM((BLOCKS, BLOCKS, TILE, TILE), jnp.bfloat16),
            pltpu.VMEM((BLOCKS, TILE, TILE), jnp.bfloat16),
            pltpu.VMEM((BLOCKS, TILE, TILE), jnp.bfloat16),
            pltpu.VMEM((TILE, TILE), jnp.bfloat16),
            pltpu.VMEM((TILE, TILE), jnp.float32),
            pltpu.VMEM((TILE, TILE), jnp.bfloat16),
            pltpu.SemaphoreType.DMA((5,)),
        ],
        compiler_params=pltpu.CompilerParams(vmem_limit_bytes=56 << 20),
        name="factor_rows",
    )(where, own, *parts)


CHUNKS = 6


def apply_kernel(where_ref, own, *refs):
    main, late = refs[:4], refs[4:8]
    chunks = refs[8 : 8 + CHUNKS]
    out, p_ref, r_ref, psems, rsems = refs[9 + CHUNKS :]
    second, col, z, core = where_ref[1], where_ref[2], where_ref[3], where_ref[4]
    sign = 1 - 2 * core
    copies = []

    def place(part, at, size):
        rows = pl.ds(pl.multiple_of(at, size), size)
        copies.append(pltpu.make_async_copy(part, r_ref.at[rows], rsems.at[len(copies)]))

    swapped = chunks[5]
    place(chunks[0], z * 64, 64)
    for by in range(1, 4):
        place(chunks[by], lax.rem(z - sign * by + 8, 8) * 64, 64)
        place(swapped.at[pl.ds(by * 64 - 64, 64)], lax.rem(z + sign * by + 8, 8) * 64, 64)
    place(chunks[4], lax.rem(z + 4, 8) * 64 + core * 32, 32)
    place(swapped.at[pl.ds(192, 32)], lax.rem(z + 4, 8) * 64 + (1 - core) * 32, 32)
    copies.append(pltpu.make_async_copy(own, p_ref.at[col], psems.at[4]))
    for copy in copies:
        copy.start()

    for index, parts in ((0, main), (1, late)):

        @pl.when(second == index)
        def _():
            fetch_rows(col, parts, p_ref, psems)

    for copy in copies:
        copy.wait()

    for last in range(BLOCKS):

        @pl.when(col == last)
        def _():
            @pl.loop(0, PW // TILE)
            def _(tile):
                at = pl.ds(pl.multiple_of(tile * TILE, TILE), TILE)
                acc = mxu(r_ref[:, :TILE], p_ref[0, at, :], NT)
                for k in range(1, last + 1):
                    acc = acc + mxu(r_ref[:, k * TILE : (k + 1) * TILE], p_ref[k, at, :], NT)
                out[:, at] = acc.astype(jnp.bfloat16)


def apply_rows(where, own, main, late, chunks, token):
    return pl.pallas_call(
        apply_kernel,
        out_shape=jax.ShapeDtypeStruct((TILE, PW), jnp.bfloat16),
        in_specs=[pl.BlockSpec(memory_space=pltpu.SMEM)] + [HBM] * (10 + CHUNKS),
        out_specs=pl.BlockSpec(memory_space=pltpu.VMEM),
        scratch_shapes=[
            pltpu.VMEM((BLOCKS, PW, TILE), jnp.bfloat16),
            pltpu.VMEM((TILE, PW), jnp.bfloat16),
            pltpu.SemaphoreType.DMA((5,)),
            pltpu.SemaphoreType.DMA((9,)),
        ],
        compiler_params=pltpu.CompilerParams(vmem_limit_bytes=40 << 20),
        name="apply_rows",
    )(where, own, *main, *late, *chunks, token)


def device(child, z, ylo, core, col):
    return (child * 32 + z * 4 + ylo * 2 + core) * 4 + col


def pairs_of(move):
    found = []
    for child in range(2):
        for z in range(8):
            for ylo in range(2):
                for core in range(2):
                    for col in range(4):
                        target = move(child, z, ylo, core, col)
                        if target is not None:
                            found.append((device(child, z, ylo, core, col), device(*target)))
    return found


def moves(member, *steps):
    allowed = dict(steps)
    return pairs_of(
        lambda c, z, y, k, j: (c, z, y, k, allowed[j]) if member(c, z, y, k) and j in allowed else None
    )


def is_second(c, z, y, k):
    return (c, y, k) == (0, 0, 1)


def is_other(c, z, y, k):
    return (c, y, k) != (0, 0, 1)


def gather(part, member, column):
    near = lax.ppermute(part, ALL, moves(member, (0, 1), (1, 2), (2, 3)))
    wrap = lax.ppermute(part, ALL, moves(member, (0, 3)))
    back = lax.ppermute(part[HALF:], ALL, moves(member, (1, 0)))
    near, wrap, back = lax.optimization_barrier((near, wrap, back))
    upper = lax.ppermute(near[:HALF], ALL, moves(member, (1, 2), (2, 3)))
    mixed = jnp.where(column == 0, back, wrap[HALF:])
    lower = lax.ppermute(mixed, ALL, moves(member, (0, 3), (3, 2)))
    return [near, wrap, upper, lower]


def spread_rows(chunks, z, y, core):
    kept = chunks[0]
    total = None
    for k in range(1, 8):
        pairs = pairs_of(
            lambda c, zz, yy, kk, j: (0, k, 0, 0, j) if (c, zz, yy, kk) == (0, 0, 0, 0) else None
        )
        got = lax.ppermute(chunks[k], ALL, pairs)
        total = got if total is None else total + got
    chunk = jnp.where(z == 0, kept, total)
    total = None
    for to in (1, 3, 2):
        pairs = pairs_of(
            lambda c, zz, yy, kk, j: (to // 2, zz, to % 2, 0, j) if (c, yy, kk) == (0, 0, 0) else None
        )
        got = lax.ppermute(chunk, ALL, pairs)
        total = got if total is None else total + got
    chunk = jnp.where(y == 0, chunk, total)
    got = lax.ppermute(
        chunk, ALL, pairs_of(lambda c, zz, yy, kk, j: (c, zz, yy, 1, j) if kk == 0 else None)
    )
    chunk = jnp.where(core == 0, chunk, got)
    swap = pairs_of(lambda c, zz, yy, kk, j: (c, zz, yy, 1 - kk, j))
    across = pairs_of(lambda c, zz, yy, kk, j: (c, (zz + 4) % 8, yy, kk, j))
    part = lax.dynamic_slice_in_dim(chunk, core * 32, 32, 0)
    half = lax.ppermute(part, ALL, across)
    direct = {}
    for by in (3, 2, 1):
        pairs = pairs_of(lambda c, zz, yy, kk, j: (c, (zz + (1 - 2 * kk) * by) % 8, yy, kk, j))
        direct[by] = lax.ppermute(chunk, ALL, pairs)
    mine = [direct[by] for by in (1, 2, 3)] + [half]
    theirs = lax.ppermute(jnp.concatenate(mine, axis=0), ALL, swap)
    return [chunk] + mine + [theirs]


def shards(front, left_factors, right_factors):
    side = lax.axis_index("child")
    row = lax.axis_index("row")
    column = lax.axis_index("col")
    z, y, core = row // 4, 2 * side + (row // 2) % 2, row % 2
    tiles = right_factors.shape[1] // 2
    left_all = left_factors[0, 0].reshape(RANK, 2 * tiles, TILE).transpose(1, 0, 2)
    both = jnp.stack([left_all, right_factors[0]])
    sent = lax.dynamic_slice_in_dim(both, (1 - side) * tiles, tiles, 1)
    kept = lax.dynamic_slice_in_dim(both, side * tiles, tiles, 1)
    got = lax.ppermute(
        sent, ALL, pairs_of(lambda c, zz, yy, kk, j: (1 - c, zz, yy, kk, j))
    )
    factors = jnp.concatenate([kept, got], axis=2)
    update = jnp.einsum("trk,trn->tkn", factors[0], factors[1], preferred_element_type=jnp.float32)
    own = (front.astype(jnp.float32) - update.reshape(PW, TILE)).astype(jnp.bfloat16)
    main = gather(own, is_other, column)
    token = lax.ppermute(
        main[0][:8, :128] + main[1][:8, :128],
        ALL,
        pairs_of(lambda c, zz, yy, kk, j: (0, zz, 0, 1, j) if (c, yy, kk) == (0, 1, 0) else None),
    )
    own_late, token = lax.optimization_barrier((own, token))
    late = gather(own_late, is_second, column)
    second = jnp.logical_and(y == 0, core == 1)
    first = jnp.logical_and(jnp.logical_and(y == 0, z == 0), core == 0)
    where = jnp.stack([first, second, column, z, core]).astype(jnp.int32)
    where, *gathered = lax.optimization_barrier((where, *main, *late))
    main, late = gathered[:4], gathered[4:]
    chunks = factor_rows(where, own, main)
    chunks = spread_rows(chunks, z, y, core)
    return apply_rows(where, own, main, late, chunks, token)


def solution(mesh):
    in_specs = (
        P(("row", "child"), "col"),
        P("child", "col", None, "row"),
        P("child", "row", None, "col"),
    )
    out_specs = P("col", ("row", "child"))
    return jax.shard_map(shards, mesh=mesh, in_specs=in_specs, out_specs=out_specs, check_vma=False)
```

```python
import functools

import jax
import jax.numpy as jnp
from jax import lax
from jax.experimental import pallas as pl
from jax.experimental.pallas import tpu as pltpu
from jax.sharding import PartitionSpec as P

TILE = 512
RANK = 64
PW = 2048
BLOCKS = PW // TILE
ROOT_ITERS = 3
ALL = ("child", "row", "col")
NT = (((1,), (1,)), ((), ()))
NN = (((1,), (0,)), ((), ()))


def mxu(left, right, dims):
    return lax.dot_general(
        left.astype(jnp.bfloat16),
        right.astype(jnp.bfloat16),
        dims,
        preferred_element_type=jnp.float32,
    )


def leaf_inverse(tile_ref, x_ref, g_ref, n_ref, nb_ref):
    part = TILE // 2
    top, low = slice(0, part), slice(part, TILE)
    diag = lax.broadcasted_iota(jnp.int32, (part, part), 0) == lax.broadcasted_iota(
        jnp.int32, (part, part), 1
    )
    under = lax.broadcasted_iota(jnp.int32, (part, part), 0) > lax.broadcasted_iota(
        jnp.int32, (part, part), 1
    )

    def lower(mat):
        return jnp.where(under, mat, jnp.where(diag, 0.5 * mat, 0.0))

    def scales(block):
        picked = jnp.where(diag, tile_ref[block, block], 0.0)
        return (
            lax.rsqrt(jnp.sum(picked, axis=1, keepdims=True)),
            lax.rsqrt(jnp.sum(picked, axis=0, keepdims=True)),
        )

    (down0, across0), (down1, across1) = scales(top), scales(low)
    eye = diag.astype(jnp.float32)
    g00 = tile_ref[top, top] * down0 * across0 - eye
    g10 = tile_ref[low, top] * down1 * across0
    g01 = tile_ref[top, low] * down0 * across1
    g11 = tile_ref[low, low] * down1 * across1 - eye
    g_ref[top, top] = g00.astype(jnp.bfloat16)
    g_ref[low, top] = g10.astype(jnp.bfloat16)
    g_ref[top, low] = g01.astype(jnp.bfloat16)
    g_ref[low, low] = g11.astype(jnp.bfloat16)
    n_ref[top, top] = lower(g00)
    n_ref[low, top] = g10
    n_ref[low, low] = lower(g11)
    nb_ref[top, top] = lower(g00).astype(jnp.bfloat16)
    nb_ref[low, top] = g10.astype(jnp.bfloat16)
    nb_ref[low, low] = lower(g11).astype(jnp.bfloat16)

    def step(_, carry):
        n00, n10, n11 = n_ref[top, top], n_ref[low, top], n_ref[low, low]
        b00, b10, b11 = nb_ref[top, top], nb_ref[low, top], nb_ref[low, low]
        scaled00 = tile_ref[top, top] * down0 * across0 - eye
        scaled10 = tile_ref[low, top] * down1 * across0
        scaled11 = tile_ref[low, low] * down1 * across1 - eye
        e00 = scaled00 - n00 - mxu(b00, g_ref[top, top], NN)
        e10 = scaled10 - n10 - mxu(nb_ref[low, :], g_ref[:, top], NN)
        e11 = scaled11 - n11 - mxu(nb_ref[low, :], g_ref[:, low], NN)
        c00, c10, c11 = e00.astype(jnp.bfloat16), e10.astype(jnp.bfloat16), e11.astype(jnp.bfloat16)
        p00 = lower(e00 - jnp.where(diag, n00, 0.0) - mxu(c00, b00, NT))
        p10 = e10 - mxu(c10, b00, NT)
        p11 = lower(
            e11 - jnp.where(diag, n11, 0.0) - mxu(c10, b10, NT) - mxu(c11, b11, NT)
        )
        f00, f10, f11 = p00.astype(jnp.bfloat16), p10.astype(jnp.bfloat16), p11.astype(jnp.bfloat16)
        n00 = n00 + p00 - mxu(f00, b00, NN)
        n10 = n10 + p10 - mxu(f10, b00, NN) - mxu(f11, b10, NN)
        n11 = n11 + p11 - mxu(f11, b11, NN)
        n_ref[top, top], n_ref[low, top], n_ref[low, low] = n00, n10, n11
        nb_ref[top, top] = n00.astype(jnp.bfloat16)
        nb_ref[low, top] = n10.astype(jnp.bfloat16)
        nb_ref[low, low] = n11.astype(jnp.bfloat16)
        return carry

    lax.fori_loop(0, ROOT_ITERS, step, 0)
    x_ref[top, top] = ((eye - n_ref[top, top]) * across0).astype(jnp.bfloat16)
    x_ref[top, low] = jnp.zeros((part, part), jnp.bfloat16)
    x_ref[low, top] = (-n_ref[low, top] * across0).astype(jnp.bfloat16)
    x_ref[low, low] = ((eye - n_ref[low, low]) * across1).astype(jnp.bfloat16)


HALF = PW // 2


def run_copies(found, dest, sems):
    copies = [
        pltpu.make_async_copy(part, dest.at[column, pl.ds(at * HALF, size)], sems.at[slot])
        for slot, (part, column, at, size) in enumerate(found)
    ]
    for copy in copies:
        copy.start()
    for copy in copies:
        copy.wait()


def fetch_rows(col, parts, dest, sems):
    near, wrap, upper, lower = parts
    found = {
        1: [(near, 0, 0, PW)],
        2: [(near, 1, 0, PW), (upper, 0, 0, HALF), (lower, 0, 1, HALF)],
        3: [(near, 2, 0, PW), (wrap, 0, 0, PW), (upper, 1, 0, HALF), (lower, 1, 1, HALF)],
    }
    for column, copies in found.items():

        @pl.when(col == column)
        def _():
            run_copies(copies, dest, sems)


def factor_kernel(where_ref, own, *refs):
    parts, outs = refs[:4], refs[4:12]
    t_ref, s_ref, l_ref, x_ref, r_ref, g_ref, n_ref, e_ref, sems = refs[12:]
    col = where_ref[2]

    @pl.when(where_ref[0] == 1)
    def _():
        mine = pltpu.make_async_copy(own, t_ref.at[col], sems.at[4])
        mine.start()
        fetch_rows(col, parts, t_ref, sems)
        mine.wait()

        def rows_of(i):
            return pl.ds(pl.multiple_of(i * TILE, TILE), TILE)

        @pl.loop(0, col + 1)
        def _(i):
            @pl.loop(0, i + 1)
            def _(j):
                low = t_ref[j, rows_of(i), :].astype(jnp.float32)
                high = t_ref[i, rows_of(j), :].astype(jnp.float32)
                s_ref[i, j] = 0.5 * (low + high.T)

        @pl.loop(0, col + 1)
        def _(j):
            leaf_inverse(s_ref.at[j, j], x_ref.at[j], g_ref, n_ref, e_ref)

            @pl.loop(j + 1, col + 1)
            def _(i):
                l_ref[i, j] = mxu(s_ref[i, j], x_ref[j], NT).astype(jnp.bfloat16)

                @pl.loop(j + 1, i + 1)
                def _(k):
                    s_ref[i, k] = s_ref[i, k] - mxu(l_ref[i, j], l_ref[k, j], NT)

        r_ref[col] = x_ref[col]

        @pl.loop(0, BLOCKS)
        def _(step):
            k = BLOCKS - 1 - step

            @pl.when(k > col)
            def _():
                r_ref[k] = jnp.zeros((TILE, TILE), jnp.bfloat16)

            @pl.when(k < col)
            def _():
                n_ref[...] = jnp.zeros((TILE, TILE), jnp.float32)

                @pl.loop(k + 1, col + 1)
                def _(m):
                    n_ref[...] += mxu(r_ref[m], l_ref[m, k], NN)

                r_ref[k] = (-mxu(n_ref[...], x_ref[k], NN)).astype(jnp.bfloat16)

        for z in range(8):
            for k in range(BLOCKS):
                outs[z][:, k * TILE : (k + 1) * TILE] = r_ref[k, z * 64 : (z + 1) * 64, :]


HBM = pl.BlockSpec(memory_space=pltpu.HBM)


def factor_rows(where, own, parts):
    return pl.pallas_call(
        factor_kernel,
        out_shape=[jax.ShapeDtypeStruct((64, PW), jnp.bfloat16)] * 8,
        in_specs=[pl.BlockSpec(memory_space=pltpu.SMEM)] + [HBM] * 5,
        out_specs=[pl.BlockSpec(memory_space=pltpu.VMEM)] * 8,
        scratch_shapes=[
            pltpu.VMEM((BLOCKS, PW, TILE), jnp.bfloat16),
            pltpu.VMEM((BLOCKS, BLOCKS, TILE, TILE), jnp.float32),
            pltpu.VMEM((BLOCKS, BLOCKS, TILE, TILE), jnp.bfloat16),
            pltpu.VMEM((BLOCKS, TILE, TILE), jnp.bfloat16),
            pltpu.VMEM((BLOCKS, TILE, TILE), jnp.bfloat16),
            pltpu.VMEM((TILE, TILE), jnp.bfloat16),
            pltpu.VMEM((TILE, TILE), jnp.float32),
            pltpu.VMEM((TILE, TILE), jnp.bfloat16),
            pltpu.SemaphoreType.DMA((5,)),
        ],
        compiler_params=pltpu.CompilerParams(vmem_limit_bytes=56 << 20),
        name="factor_rows",
    )(where, own, *parts)


CHUNKS = 6


def apply_kernel(where_ref, own, *refs):
    near, wrap, upper, lower, late_wrap, late_upper, late_lower = refs[:7]
    chunks = refs[7 : 7 + CHUNKS]
    out, p_ref, r_ref, psems, rsems = refs[8 + CHUNKS :]
    second, col, z, core = where_ref[1], where_ref[2], where_ref[3], where_ref[4]
    sign = 1 - 2 * core
    copies = []

    def place(part, at, size):
        rows = pl.ds(pl.multiple_of(at, size), size)
        copies.append(pltpu.make_async_copy(part, r_ref.at[rows], rsems.at[len(copies)]))

    swapped = chunks[5]
    place(chunks[0], z * 64, 64)
    for by in range(1, 4):
        place(chunks[by], lax.rem(z - sign * by + 8, 8) * 64, 64)
        place(swapped.at[pl.ds(by * 64 - 64, 64)], lax.rem(z + sign * by + 8, 8) * 64, 64)
    place(chunks[4], lax.rem(z + 4, 8) * 64 + core * 32, 32)
    place(swapped.at[pl.ds(192, 32)], lax.rem(z + 4, 8) * 64 + (1 - core) * 32, 32)
    copies.append(pltpu.make_async_copy(own, p_ref.at[col], psems.at[5]))
    for copy in copies:
        copy.start()

    @pl.when(second == 0)
    def _():
        fetch_rows(col, (near, wrap, upper, lower), p_ref, psems)

    for last in range(1, BLOCKS):
        sources = [(upper, last - 1, 0, HALF), (lower, last - 1, 1, HALF)]
        if last >= 2:
            sources += [(late_upper, last - 2, 0, HALF), (late_lower, last - 2, 1, HALF)]
        if last == 3:
            sources += [(late_wrap, 0, 0, PW)]

        @pl.when(jnp.logical_and(second == 1, col == last))
        def _():
            run_copies(sources, p_ref, psems)

    for copy in copies:
        copy.wait()

    for last in range(BLOCKS):

        @pl.when(col == last)
        def _():
            @pl.loop(0, PW // TILE)
            def _(tile):
                at = pl.ds(pl.multiple_of(tile * TILE, TILE), TILE)
                acc = mxu(r_ref[:, :TILE], p_ref[0, at, :], NT)
                for k in range(1, last + 1):
                    acc = acc + mxu(r_ref[:, k * TILE : (k + 1) * TILE], p_ref[k, at, :], NT)
                out[:, at] = acc.astype(jnp.bfloat16)


def apply_rows(where, own, gathered, chunks, token):
    return pl.pallas_call(
        apply_kernel,
        out_shape=jax.ShapeDtypeStruct((TILE, PW), jnp.bfloat16),
        in_specs=[pl.BlockSpec(memory_space=pltpu.SMEM)] + [HBM] * (9 + CHUNKS),
        out_specs=pl.BlockSpec(memory_space=pltpu.VMEM),
        scratch_shapes=[
            pltpu.VMEM((BLOCKS, PW, TILE), jnp.bfloat16),
            pltpu.VMEM((TILE, PW), jnp.bfloat16),
            pltpu.SemaphoreType.DMA((6,)),
            pltpu.SemaphoreType.DMA((9,)),
        ],
        compiler_params=pltpu.CompilerParams(vmem_limit_bytes=60 << 20),
        name="apply_rows",
    )(where, own, *gathered, *chunks, token)


def device(child, z, ylo, core, col):
    return (child * 32 + z * 4 + ylo * 2 + core) * 4 + col


def pairs_of(move):
    found = []
    for child in range(2):
        for z in range(8):
            for ylo in range(2):
                for core in range(2):
                    for col in range(4):
                        target = move(child, z, ylo, core, col)
                        if target is not None:
                            found.append((device(child, z, ylo, core, col), device(*target)))
    return found


def moves(member, *steps):
    allowed = dict(steps)
    return pairs_of(
        lambda c, z, y, k, j: (c, z, y, k, allowed[j]) if member(c, z, y, k) and j in allowed else None
    )


def is_second(c, z, y, k):
    return (c, y, k) == (0, 0, 1)


def is_other(c, z, y, k):
    return (c, y, k) != (0, 0, 1)


def spread_rows(chunks, z, y, core):
    kept = chunks[0]
    total = None
    for k in range(1, 8):
        pairs = pairs_of(
            lambda c, zz, yy, kk, j: (0, k, 0, 0, j) if (c, zz, yy, kk) == (0, 0, 0, 0) else None
        )
        got = lax.ppermute(chunks[k], ALL, pairs)
        total = got if total is None else total + got
    chunk = jnp.where(z == 0, kept, total)
    total = None
    for to in (1, 3, 2):
        pairs = pairs_of(
            lambda c, zz, yy, kk, j: (to // 2, zz, to % 2, 0, j) if (c, yy, kk) == (0, 0, 0) else None
        )
        got = lax.ppermute(chunk, ALL, pairs)
        total = got if total is None else total + got
    chunk = jnp.where(y == 0, chunk, total)
    got = lax.ppermute(
        chunk, ALL, pairs_of(lambda c, zz, yy, kk, j: (c, zz, yy, 1, j) if kk == 0 else None)
    )
    chunk = jnp.where(core == 0, chunk, got)
    swap = pairs_of(lambda c, zz, yy, kk, j: (c, zz, yy, 1 - kk, j))
    across = pairs_of(lambda c, zz, yy, kk, j: (c, (zz + 4) % 8, yy, kk, j))
    part = lax.dynamic_slice_in_dim(chunk, core * 32, 32, 0)
    half = lax.ppermute(part, ALL, across)
    direct = {}
    for by in (3, 2, 1):
        pairs = pairs_of(lambda c, zz, yy, kk, j: (c, (zz + (1 - 2 * kk) * by) % 8, yy, kk, j))
        direct[by] = lax.ppermute(chunk, ALL, pairs)
    mine = [direct[by] for by in (1, 2, 3)] + [half]
    theirs = lax.ppermute(jnp.concatenate(mine, axis=0), ALL, swap)
    return [chunk] + mine + [theirs]


def shards(front, left_factors, right_factors):
    side = lax.axis_index("child")
    row = lax.axis_index("row")
    column = lax.axis_index("col")
    z, y, core = row // 4, 2 * side + (row // 2) % 2, row % 2
    tiles = right_factors.shape[1] // 2
    left_all = left_factors[0, 0].reshape(RANK, 2 * tiles, TILE).transpose(1, 0, 2)
    both = jnp.stack([left_all, right_factors[0]])
    sent = lax.dynamic_slice_in_dim(both, (1 - side) * tiles, tiles, 1)
    kept = lax.dynamic_slice_in_dim(both, side * tiles, tiles, 1)
    got = lax.ppermute(
        sent, ALL, pairs_of(lambda c, zz, yy, kk, j: (1 - c, zz, yy, kk, j))
    )
    factors = jnp.concatenate([kept, got], axis=2)
    update = jnp.einsum("trk,trn->tkn", factors[0], factors[1], preferred_element_type=jnp.float32)
    own = (front.astype(jnp.float32) - update.reshape(PW, TILE)).astype(jnp.bfloat16)
    second = jnp.logical_and(y == 0, core == 1)
    first = jnp.logical_and(jnp.logical_and(y == 0, z == 0), core == 0)
    near = lax.ppermute(own, ALL, moves(is_other, (0, 1), (1, 2), (2, 3)))
    wrap = lax.ppermute(own, ALL, moves(is_other, (0, 3)))
    back = lax.ppermute(own[HALF:], ALL, moves(is_other, (1, 0)))
    near, wrap, back = lax.optimization_barrier((near, wrap, back))
    token = lax.ppermute(
        near[:8, :128] + wrap[:8, :128],
        ALL,
        pairs_of(lambda c, zz, yy, kk, j: (0, zz, 0, 1, j) if (c, yy, kk) == (0, 1, 0) else None),
    )
    held, token = lax.optimization_barrier((own, token))
    along = moves(is_second, (0, 1), (1, 2), (2, 3))
    upper = lax.ppermute(
        jnp.where(second, held[:HALF], near[:HALF]), ALL, moves(is_other, (1, 2), (2, 3)) + along
    )
    mixed = jnp.where(column == 0, back, wrap[HALF:])
    lower = lax.ppermute(
        jnp.where(second, held[HALF:], mixed), ALL, moves(is_other, (0, 3), (3, 2)) + along
    )
    late_wrap = lax.ppermute(held, ALL, moves(is_second, (0, 3)))
    late_upper = lax.ppermute(upper, ALL, moves(is_second, (1, 2), (2, 3)))
    late_lower = lax.ppermute(lower, ALL, moves(is_second, (1, 2), (2, 3)))
    where = jnp.stack([first, second, column, z, core]).astype(jnp.int32)
    where, *gathered = lax.optimization_barrier(
        (where, near, wrap, upper, lower, late_wrap, late_upper, late_lower)
    )
    chunks = factor_rows(where, own, gathered[:4])
    chunks = spread_rows(chunks, z, y, core)
    return apply_rows(where, own, gathered, chunks, token)


def solution(mesh):
    in_specs = (
        P(("row", "child"), "col"),
        P("child", "col", None, "row"),
        P("child", "row", None, "col"),
    )
    out_specs = P("col", ("row", "child"))
    return jax.shard_map(shards, mesh=mesh, in_specs=in_specs, out_specs=out_specs, check_vma=False)
```

```python
import functools

import jax
import jax.numpy as jnp
from jax import lax
from jax.experimental import pallas as pl
from jax.experimental.pallas import tpu as pltpu
from jax.sharding import PartitionSpec as P

TILE = 512
RANK = 64
PW = 2048
BLOCKS = PW // TILE
ROOT_ITERS = 3
ALL = ("child", "row", "col")
NT = (((1,), (1,)), ((), ()))
NN = (((1,), (0,)), ((), ()))


def mxu(left, right, dims):
    return lax.dot_general(
        left.astype(jnp.bfloat16),
        right.astype(jnp.bfloat16),
        dims,
        preferred_element_type=jnp.float32,
    )


def leaf_inverse(tile_ref, x_ref, g_ref, n_ref, nb_ref):
    part = TILE // 2
    top, low = slice(0, part), slice(part, TILE)
    diag = lax.broadcasted_iota(jnp.int32, (part, part), 0) == lax.broadcasted_iota(
        jnp.int32, (part, part), 1
    )
    under = lax.broadcasted_iota(jnp.int32, (part, part), 0) > lax.broadcasted_iota(
        jnp.int32, (part, part), 1
    )

    def lower(mat):
        return jnp.where(under, mat, jnp.where(diag, 0.5 * mat, 0.0))

    def scales(block):
        picked = jnp.where(diag, tile_ref[block, block], 0.0)
        return (
            lax.rsqrt(jnp.sum(picked, axis=1, keepdims=True)),
            lax.rsqrt(jnp.sum(picked, axis=0, keepdims=True)),
        )

    (down0, across0), (down1, across1) = scales(top), scales(low)
    eye = diag.astype(jnp.float32)
    g00 = tile_ref[top, top] * down0 * across0 - eye
    g10 = tile_ref[low, top] * down1 * across0
    g01 = tile_ref[top, low] * down0 * across1
    g11 = tile_ref[low, low] * down1 * across1 - eye
    g_ref[top, top] = g00.astype(jnp.bfloat16)
    g_ref[low, top] = g10.astype(jnp.bfloat16)
    g_ref[top, low] = g01.astype(jnp.bfloat16)
    g_ref[low, low] = g11.astype(jnp.bfloat16)
    n_ref[top, top] = lower(g00)
    n_ref[low, top] = g10
    n_ref[low, low] = lower(g11)
    nb_ref[top, top] = lower(g00).astype(jnp.bfloat16)
    nb_ref[low, top] = g10.astype(jnp.bfloat16)
    nb_ref[low, low] = lower(g11).astype(jnp.bfloat16)

    def step(_, carry):
        n00, n10, n11 = n_ref[top, top], n_ref[low, top], n_ref[low, low]
        b00, b10, b11 = nb_ref[top, top], nb_ref[low, top], nb_ref[low, low]
        scaled00 = tile_ref[top, top] * down0 * across0 - eye
        scaled10 = tile_ref[low, top] * down1 * across0
        scaled11 = tile_ref[low, low] * down1 * across1 - eye
        e00 = scaled00 - n00 - mxu(b00, g_ref[top, top], NN)
        e10 = scaled10 - n10 - mxu(nb_ref[low, :], g_ref[:, top], NN)
        e11 = scaled11 - n11 - mxu(nb_ref[low, :], g_ref[:, low], NN)
        c00, c10, c11 = e00.astype(jnp.bfloat16), e10.astype(jnp.bfloat16), e11.astype(jnp.bfloat16)
        p00 = lower(e00 - jnp.where(diag, n00, 0.0) - mxu(c00, b00, NT))
        p10 = e10 - mxu(c10, b00, NT)
        p11 = lower(
            e11 - jnp.where(diag, n11, 0.0) - mxu(c10, b10, NT) - mxu(c11, b11, NT)
        )
        f00, f10, f11 = p00.astype(jnp.bfloat16), p10.astype(jnp.bfloat16), p11.astype(jnp.bfloat16)
        n00 = n00 + p00 - mxu(f00, b00, NN)
        n10 = n10 + p10 - mxu(f10, b00, NN) - mxu(f11, b10, NN)
        n11 = n11 + p11 - mxu(f11, b11, NN)
        n_ref[top, top], n_ref[low, top], n_ref[low, low] = n00, n10, n11
        nb_ref[top, top] = n00.astype(jnp.bfloat16)
        nb_ref[low, top] = n10.astype(jnp.bfloat16)
        nb_ref[low, low] = n11.astype(jnp.bfloat16)
        return carry

    lax.fori_loop(0, ROOT_ITERS, step, 0)
    x_ref[top, top] = ((eye - n_ref[top, top]) * across0).astype(jnp.bfloat16)
    x_ref[top, low] = jnp.zeros((part, part), jnp.bfloat16)
    x_ref[low, top] = (-n_ref[low, top] * across0).astype(jnp.bfloat16)
    x_ref[low, low] = ((eye - n_ref[low, low]) * across1).astype(jnp.bfloat16)


HALF = PW // 2


def run_copies(found, dest, sems):
    copies = [
        pltpu.make_async_copy(part, dest.at[column, pl.ds(at * HALF, size)], sems.at[slot])
        for slot, (part, column, at, size) in enumerate(found)
    ]
    for copy in copies:
        copy.start()
    for copy in copies:
        copy.wait()


def fetch_rows(col, parts, dest, sems):
    near, wrap, upper, lower = parts
    found = {
        1: [(near, 0, 0, PW)],
        2: [(near, 1, 0, PW), (upper, 0, 0, HALF), (lower, 0, 1, HALF)],
        3: [(near, 2, 0, PW), (wrap, 0, 0, PW), (upper, 1, 0, HALF), (lower, 1, 1, HALF)],
    }
    for column, copies in found.items():

        @pl.when(col == column)
        def _():
            run_copies(copies, dest, sems)


def factor_kernel(where_ref, own, *refs):
    parts, outs = refs[:4], refs[4:12]
    t_ref, s_ref, l_ref, x_ref, r_ref, g_ref, n_ref, e_ref, sems = refs[12:]
    col = where_ref[2]

    @pl.when(where_ref[0] == 1)
    def _():
        mine = pltpu.make_async_copy(own, t_ref.at[col], sems.at[4])
        mine.start()
        fetch_rows(col, parts, t_ref, sems)
        mine.wait()

        def rows_of(i):
            return pl.ds(pl.multiple_of(i * TILE, TILE), TILE)

        @pl.loop(0, col + 1)
        def _(i):
            @pl.loop(0, i + 1)
            def _(j):
                low = t_ref[j, rows_of(i), :].astype(jnp.float32)
                high = t_ref[i, rows_of(j), :].astype(jnp.float32)
                s_ref[i, j] = 0.5 * (low + high.T)

        @pl.loop(0, col + 1)
        def _(j):
            leaf_inverse(s_ref.at[j, j], x_ref.at[j], g_ref, n_ref, e_ref)

            @pl.loop(j + 1, col + 1)
            def _(i):
                l_ref[i, j] = mxu(s_ref[i, j], x_ref[j], NT).astype(jnp.bfloat16)

                @pl.loop(j + 1, i + 1)
                def _(k):
                    s_ref[i, k] = s_ref[i, k] - mxu(l_ref[i, j], l_ref[k, j], NT)

        r_ref[col] = x_ref[col]

        @pl.loop(0, BLOCKS)
        def _(step):
            k = BLOCKS - 1 - step

            @pl.when(k > col)
            def _():
                r_ref[k] = jnp.zeros((TILE, TILE), jnp.bfloat16)

            @pl.when(k < col)
            def _():
                n_ref[...] = jnp.zeros((TILE, TILE), jnp.float32)

                @pl.loop(k + 1, col + 1)
                def _(m):
                    n_ref[...] += mxu(r_ref[m], l_ref[m, k], NN)

                r_ref[k] = (-mxu(n_ref[...], x_ref[k], NN)).astype(jnp.bfloat16)

        for z in range(8):
            for k in range(BLOCKS):
                outs[z][:, k * TILE : (k + 1) * TILE] = r_ref[k, z * 64 : (z + 1) * 64, :]


HBM = pl.BlockSpec(memory_space=pltpu.HBM)


def factor_rows(where, own, parts):
    return pl.pallas_call(
        factor_kernel,
        out_shape=[jax.ShapeDtypeStruct((64, PW), jnp.bfloat16)] * 8,
        in_specs=[pl.BlockSpec(memory_space=pltpu.SMEM)] + [HBM] * 5,
        out_specs=[pl.BlockSpec(memory_space=pltpu.VMEM)] * 8,
        scratch_shapes=[
            pltpu.VMEM((BLOCKS, PW, TILE), jnp.bfloat16),
            pltpu.VMEM((BLOCKS, BLOCKS, TILE, TILE), jnp.float32),
            pltpu.VMEM((BLOCKS, BLOCKS, TILE, TILE), jnp.bfloat16),
            pltpu.VMEM((BLOCKS, TILE, TILE), jnp.bfloat16),
            pltpu.VMEM((BLOCKS, TILE, TILE), jnp.bfloat16),
            pltpu.VMEM((TILE, TILE), jnp.bfloat16),
            pltpu.VMEM((TILE, TILE), jnp.float32),
            pltpu.VMEM((TILE, TILE), jnp.bfloat16),
            pltpu.SemaphoreType.DMA((5,)),
        ],
        compiler_params=pltpu.CompilerParams(vmem_limit_bytes=56 << 20),
        name="factor_rows",
    )(where, own, *parts)


CHUNKS = 10
OFFSETS = (4, 3, 5, 6, 2, 7, 1)


def apply_kernel(where_ref, own, *refs):
    near, wrap, upper, lower, late_wrap, late_upper, late_lower = refs[:7]
    chunks = refs[7 : 7 + CHUNKS]
    out, p_ref, r_ref, psems, rsems = refs[8 + CHUNKS :]
    second, col, z, core = where_ref[1], where_ref[2], where_ref[3], where_ref[4]
    parts, early, late = chunks[:8], chunks[8], chunks[9]

    def piece(slot, part):
        by = (OFFSETS + (0,))[slot]
        rows = pl.ds(pl.multiple_of(lax.rem(z - by + 8, 8) * 64, 64), 64)
        return pltpu.make_async_copy(part, r_ref.at[rows], rsems.at[slot])

    @pl.when(core == 0)
    def _():
        for slot in range(8):
            piece(slot, parts[slot]).start()

    @pl.when(core == 1)
    def _():
        for slot in range(8):
            source = early if slot >= 4 else late
            piece(slot, source.at[pl.ds(slot % 4 * 64, 64)]).start()

    def rows_of(at):
        return pl.ds(at * HALF, HALF)

    def load(at, column, part):
        source = part[at] if isinstance(part, tuple) else part.at[rows_of(at)]
        return pltpu.make_async_copy(source, p_ref.at[column, rows_of(at)], psems.at[at, column])

    both, late_both = (upper, lower), (late_upper, late_lower)
    for flag in range(2):
        for last in range(BLOCKS):
            sources = {last: own}
            if last >= 1:
                sources[last - 1] = both if flag else near
            if last >= 2:
                sources[last - 2] = late_both if flag else both
            if last == 3:
                sources[0] = late_wrap if flag else wrap

            @pl.when(jnp.logical_and(second == flag, col == last))
            def _():
                for at in range(2):
                    for column, part in sources.items():
                        load(at, column, part).start()

    for slot in range(8):
        piece(slot, parts[slot]).wait()
    for last in range(BLOCKS):

        @pl.when(col == last)
        def _():
            @pl.loop(0, 2)
            def _(at):
                for column in range(last + 1):
                    rows = pl.ds(pl.multiple_of(at * HALF, HALF), HALF)
                    pltpu.make_async_copy(
                        near.at[pl.ds(0, HALF)], p_ref.at[column, rows], psems.at[at, column]
                    ).wait()

                @pl.loop(0, HALF // TILE)
                def _(tile):
                    rows = pl.ds(pl.multiple_of(at * HALF + tile * TILE, TILE), TILE)
                    acc = mxu(r_ref[:, :TILE], p_ref[0, rows, :], NT)
                    for k in range(1, last + 1):
                        acc = acc + mxu(
                            r_ref[:, k * TILE : (k + 1) * TILE], p_ref[k, rows, :], NT
                        )
                    out[:, rows] = acc.astype(jnp.bfloat16)


def apply_rows(where, own, gathered, chunks, token):
    return pl.pallas_call(
        apply_kernel,
        out_shape=jax.ShapeDtypeStruct((TILE, PW), jnp.bfloat16),
        in_specs=[pl.BlockSpec(memory_space=pltpu.SMEM)] + [HBM] * (9 + CHUNKS),
        out_specs=pl.BlockSpec(memory_space=pltpu.VMEM),
        scratch_shapes=[
            pltpu.VMEM((BLOCKS, PW, TILE), jnp.bfloat16),
            pltpu.VMEM((TILE, PW), jnp.bfloat16),
            pltpu.SemaphoreType.DMA((2, BLOCKS)),
            pltpu.SemaphoreType.DMA((8,)),
        ],
        compiler_params=pltpu.CompilerParams(vmem_limit_bytes=60 << 20),
        name="apply_rows",
    )(where, own, *gathered, *chunks, token)


def device(child, z, ylo, core, col):
    return (child * 32 + z * 4 + ylo * 2 + core) * 4 + col


def pairs_of(move):
    found = []
    for child in range(2):
        for z in range(8):
            for ylo in range(2):
                for core in range(2):
                    for col in range(4):
                        target = move(child, z, ylo, core, col)
                        if target is not None:
                            found.append((device(child, z, ylo, core, col), device(*target)))
    return found


def moves(member, *steps):
    allowed = dict(steps)
    return pairs_of(
        lambda c, z, y, k, j: (c, z, y, k, allowed[j]) if member(c, z, y, k) and j in allowed else None
    )


def is_second(c, z, y, k):
    return (c, y, k) == (0, 0, 1)


def is_other(c, z, y, k):
    return (c, y, k) != (0, 0, 1)


def spread_rows(chunks, z, y):
    kept = chunks[0]
    total = None
    for k in range(1, 8):
        pairs = pairs_of(
            lambda c, zz, yy, kk, j: (0, k, 0, 0, j) if (c, zz, yy, kk) == (0, 0, 0, 0) else None
        )
        got = lax.ppermute(chunks[k], ALL, pairs)
        total = got if total is None else total + got
    chunk = jnp.where(z == 0, kept, total)
    total = None
    for to in (1, 3, 2):
        pairs = pairs_of(
            lambda c, zz, yy, kk, j: (to // 2, zz, to % 2, 0, j) if (c, yy, kk) == (0, 0, 0) else None
        )
        got = lax.ppermute(chunk, ALL, pairs)
        total = got if total is None else total + got
    chunk = jnp.where(y == 0, chunk, total)
    direct = {}
    for by in (6, 2, 5, 3, 4, 7, 1):
        pairs = pairs_of(
            lambda c, zz, yy, kk, j: (c, (zz + by) % 8, yy, kk, j) if kk == 0 else None
        )
        direct[by] = lax.ppermute(chunk, ALL, pairs)
    parts = [direct[by] for by in OFFSETS] + [chunk]
    across = pairs_of(lambda c, zz, yy, kk, j: (c, zz, yy, 1, j) if kk == 0 else None)
    early = lax.ppermute(jnp.concatenate(parts[4:], axis=0), ALL, across)
    last = lax.ppermute(jnp.concatenate(parts[:4], axis=0), ALL, across)
    return parts + [early, last]


def shards(front, left_factors, right_factors):
    side = lax.axis_index("child")
    row = lax.axis_index("row")
    column = lax.axis_index("col")
    z, y, core = row // 4, 2 * side + (row // 2) % 2, row % 2
    tiles = right_factors.shape[1] // 2
    left_all = left_factors[0, 0].reshape(RANK, 2 * tiles, TILE).transpose(1, 0, 2)
    both = jnp.stack([left_all, right_factors[0]])
    sent = lax.dynamic_slice_in_dim(both, (1 - side) * tiles, tiles, 1)
    kept = lax.dynamic_slice_in_dim(both, side * tiles, tiles, 1)
    got = lax.ppermute(
        sent, ALL, pairs_of(lambda c, zz, yy, kk, j: (1 - c, zz, yy, kk, j))
    )
    factors = jnp.concatenate([kept, got], axis=2)
    update = jnp.einsum("trk,trn->tkn", factors[0], factors[1], preferred_element_type=jnp.float32)
    own = (front.astype(jnp.float32) - update.reshape(PW, TILE)).astype(jnp.bfloat16)
    second = jnp.logical_and(y == 0, core == 1)
    first = jnp.logical_and(jnp.logical_and(y == 0, z == 0), core == 0)
    near = lax.ppermute(own, ALL, moves(is_other, (0, 1), (1, 2), (2, 3)))
    wrap = lax.ppermute(own, ALL, moves(is_other, (0, 3)))
    back = lax.ppermute(own[HALF:], ALL, moves(is_other, (1, 0)))
    near, wrap, back = lax.optimization_barrier((near, wrap, back))
    token = lax.ppermute(
        near[:8, :128] + wrap[:8, :128],
        ALL,
        pairs_of(lambda c, zz, yy, kk, j: (0, zz, 0, 1, j) if (c, yy, kk) == (0, 1, 0) else None),
    )
    held, token = lax.optimization_barrier((own, token))
    along = moves(is_second, (0, 1), (1, 2), (2, 3))
    upper = lax.ppermute(
        jnp.where(second, held[:HALF], near[:HALF]), ALL, moves(is_other, (1, 2), (2, 3)) + along
    )
    mixed = jnp.where(column == 0, back, wrap[HALF:])
    lower = lax.ppermute(
        jnp.where(second, held[HALF:], mixed), ALL, moves(is_other, (0, 3), (3, 2)) + along
    )
    late_wrap = lax.ppermute(held, ALL, moves(is_second, (0, 3)))
    late_upper = lax.ppermute(upper, ALL, moves(is_second, (1, 2), (2, 3)))
    late_lower = lax.ppermute(lower, ALL, moves(is_second, (1, 2), (2, 3)))
    where = jnp.stack([first, second, column, z, core]).astype(jnp.int32)
    where, *gathered = lax.optimization_barrier(
        (where, near, wrap, upper, lower, late_wrap, late_upper, late_lower)
    )
    chunks = factor_rows(where, own, gathered[:4])
    chunks = spread_rows(chunks, z, y)
    return apply_rows(where, own, gathered, chunks, token)


def solution(mesh):
    in_specs = (
        P(("row", "child"), "col"),
        P("child", "col", None, "row"),
        P("child", "row", None, "col"),
    )
    out_specs = P("col", ("row", "child"))
    return jax.shard_map(shards, mesh=mesh, in_specs=in_specs, out_specs=out_specs, check_vma=False)
```

```python
import functools

import jax
import jax.numpy as jnp
from jax import lax
from jax.experimental import pallas as pl
from jax.experimental.pallas import tpu as pltpu
from jax.sharding import PartitionSpec as P

TILE = 512
RANK = 64
PW = 2048
BLOCKS = PW // TILE
ROOT_ITERS = 3
ALL = ("child", "row", "col")
NT = (((1,), (1,)), ((), ()))
NN = (((1,), (0,)), ((), ()))


def mxu(left, right, dims):
    return lax.dot_general(
        left.astype(jnp.bfloat16),
        right.astype(jnp.bfloat16),
        dims,
        preferred_element_type=jnp.float32,
    )


def leaf_inverse(tile_ref, x_ref, g_ref, n_ref, nb_ref):
    part = TILE // 2
    top, low = slice(0, part), slice(part, TILE)
    diag = lax.broadcasted_iota(jnp.int32, (part, part), 0) == lax.broadcasted_iota(
        jnp.int32, (part, part), 1
    )
    under = lax.broadcasted_iota(jnp.int32, (part, part), 0) > lax.broadcasted_iota(
        jnp.int32, (part, part), 1
    )

    def lower(mat):
        return jnp.where(under, mat, jnp.where(diag, 0.5 * mat, 0.0))

    def scales(block):
        picked = jnp.where(diag, tile_ref[block, block], 0.0)
        return (
            lax.rsqrt(jnp.sum(picked, axis=1, keepdims=True)),
            lax.rsqrt(jnp.sum(picked, axis=0, keepdims=True)),
        )

    (down0, across0), (down1, across1) = scales(top), scales(low)
    eye = diag.astype(jnp.float32)
    g00 = tile_ref[top, top] * down0 * across0 - eye
    g10 = tile_ref[low, top] * down1 * across0
    g01 = tile_ref[top, low] * down0 * across1
    g11 = tile_ref[low, low] * down1 * across1 - eye
    g_ref[top, top] = g00.astype(jnp.bfloat16)
    g_ref[low, top] = g10.astype(jnp.bfloat16)
    g_ref[top, low] = g01.astype(jnp.bfloat16)
    g_ref[low, low] = g11.astype(jnp.bfloat16)
    n_ref[top, top] = lower(g00)
    n_ref[low, top] = g10
    n_ref[low, low] = lower(g11)
    nb_ref[top, top] = lower(g00).astype(jnp.bfloat16)
    nb_ref[low, top] = g10.astype(jnp.bfloat16)
    nb_ref[low, low] = lower(g11).astype(jnp.bfloat16)

    def step(_, carry):
        n00, n10, n11 = n_ref[top, top], n_ref[low, top], n_ref[low, low]
        b00, b10, b11 = nb_ref[top, top], nb_ref[low, top], nb_ref[low, low]
        scaled00 = tile_ref[top, top] * down0 * across0 - eye
        scaled10 = tile_ref[low, top] * down1 * across0
        scaled11 = tile_ref[low, low] * down1 * across1 - eye
        e00 = scaled00 - n00 - mxu(b00, g_ref[top, top], NN)
        e10 = scaled10 - n10 - mxu(nb_ref[low, :], g_ref[:, top], NN)
        e11 = scaled11 - n11 - mxu(nb_ref[low, :], g_ref[:, low], NN)
        c00, c10, c11 = e00.astype(jnp.bfloat16), e10.astype(jnp.bfloat16), e11.astype(jnp.bfloat16)
        p00 = lower(e00 - jnp.where(diag, n00, 0.0) - mxu(c00, b00, NT))
        p10 = e10 - mxu(c10, b00, NT)
        p11 = lower(
            e11 - jnp.where(diag, n11, 0.0) - mxu(c10, b10, NT) - mxu(c11, b11, NT)
        )
        f00, f10, f11 = p00.astype(jnp.bfloat16), p10.astype(jnp.bfloat16), p11.astype(jnp.bfloat16)
        n00 = n00 + p00 - mxu(f00, b00, NN)
        n10 = n10 + p10 - mxu(f10, b00, NN) - mxu(f11, b10, NN)
        n11 = n11 + p11 - mxu(f11, b11, NN)
        n_ref[top, top], n_ref[low, top], n_ref[low, low] = n00, n10, n11
        nb_ref[top, top] = n00.astype(jnp.bfloat16)
        nb_ref[low, top] = n10.astype(jnp.bfloat16)
        nb_ref[low, low] = n11.astype(jnp.bfloat16)
        return carry

    lax.fori_loop(0, ROOT_ITERS, step, 0)
    x_ref[top, top] = ((eye - n_ref[top, top]) * across0).astype(jnp.bfloat16)
    x_ref[top, low] = jnp.zeros((part, part), jnp.bfloat16)
    x_ref[low, top] = (-n_ref[low, top] * across0).astype(jnp.bfloat16)
    x_ref[low, low] = ((eye - n_ref[low, low]) * across1).astype(jnp.bfloat16)


HALF = PW // 2


def start_columns(col, own, near, far, wrap, dest, sems):
    for last in range(BLOCKS):
        sources = {0: wrap} if last == 3 else {}
        if last >= 2:
            sources[last - 2] = far
        if last >= 1:
            sources[last - 1] = near
        sources[last] = own

        @pl.when(col == last)
        def _():
            for column, part in sources.items():
                for at in range(2):
                    rows = pl.ds(at * HALF, HALF)
                    source = part[at] if isinstance(part, tuple) else part.at[rows]
                    pltpu.make_async_copy(
                        source, dest.at[column, rows], sems.at[at, column]
                    ).start()


def wait_column(like, column, at, dest, sems):
    rows = pl.ds(pl.multiple_of(at * HALF, HALF), HALF)
    pltpu.make_async_copy(
        like.at[pl.ds(0, HALF)], dest.at[column, rows], sems.at[at, column]
    ).wait()


def factor_kernel(where_ref, own, *refs):
    parts, outs = tuple(refs[:4]), refs[4:12]
    t_ref, s_ref, l_ref, x_ref, r_ref, g_ref, n_ref, e_ref, sems = refs[12:]
    col = where_ref[2]

    @pl.when(where_ref[0] == 1)
    def _():
        start_columns(col, own, parts[0], parts[2:4], parts[1], t_ref, sems)

        def rows_of(i):
            return pl.ds(pl.multiple_of(i * TILE, TILE), TILE)

        def symmetric(i, j):
            low = t_ref[j, rows_of(i), :].astype(jnp.float32)
            high = t_ref[i, rows_of(j), :].astype(jnp.float32)
            s_ref[i, j] = 0.5 * (low + high.T)

        wait_column(own, 0, 0, t_ref, sems)
        symmetric(0, 0)

        @pl.loop(0, col + 1)
        def _(j):
            leaf_inverse(s_ref.at[j, j], x_ref.at[j], g_ref, n_ref, e_ref)

            @pl.when(j == 0)
            def _():
                wait_column(own, 0, 1, t_ref, sems)

                @pl.loop(1, col + 1)
                def _(i):
                    for at in range(2):
                        wait_column(own, i, at, t_ref, sems)

                @pl.loop(1, col + 1)
                def _(i):
                    @pl.loop(0, i + 1)
                    def _(k):
                        symmetric(i, k)

            @pl.loop(j + 1, col + 1)
            def _(i):
                l_ref[i, j] = mxu(s_ref[i, j], x_ref[j], NT).astype(jnp.bfloat16)

                @pl.loop(j + 1, i + 1)
                def _(k):
                    s_ref[i, k] = s_ref[i, k] - mxu(l_ref[i, j], l_ref[k, j], NT)

        r_ref[col] = x_ref[col]

        @pl.loop(0, BLOCKS)
        def _(step):
            k = BLOCKS - 1 - step

            @pl.when(k > col)
            def _():
                r_ref[k] = jnp.zeros((TILE, TILE), jnp.bfloat16)

            @pl.when(k < col)
            def _():
                n_ref[...] = jnp.zeros((TILE, TILE), jnp.float32)

                @pl.loop(k + 1, col + 1)
                def _(m):
                    n_ref[...] += mxu(r_ref[m], l_ref[m, k], NN)

                r_ref[k] = (-mxu(n_ref[...], x_ref[k], NN)).astype(jnp.bfloat16)

        for z in range(8):
            for k in range(BLOCKS):
                outs[z][:, k * TILE : (k + 1) * TILE] = r_ref[k, z * 64 : (z + 1) * 64, :]


HBM = pl.BlockSpec(memory_space=pltpu.HBM)


def factor_rows(where, own, parts):
    return pl.pallas_call(
        factor_kernel,
        out_shape=[jax.ShapeDtypeStruct((64, PW), jnp.bfloat16)] * 8,
        in_specs=[pl.BlockSpec(memory_space=pltpu.SMEM)] + [HBM] * 5,
        out_specs=[pl.BlockSpec(memory_space=pltpu.VMEM)] * 8,
        scratch_shapes=[
            pltpu.VMEM((BLOCKS, PW, TILE), jnp.bfloat16),
            pltpu.VMEM((BLOCKS, BLOCKS, TILE, TILE), jnp.float32),
            pltpu.VMEM((BLOCKS, BLOCKS, TILE, TILE), jnp.bfloat16),
            pltpu.VMEM((BLOCKS, TILE, TILE), jnp.bfloat16),
            pltpu.VMEM((BLOCKS, TILE, TILE), jnp.bfloat16),
            pltpu.VMEM((TILE, TILE), jnp.bfloat16),
            pltpu.VMEM((TILE, TILE), jnp.float32),
            pltpu.VMEM((TILE, TILE), jnp.bfloat16),
            pltpu.SemaphoreType.DMA((2, BLOCKS)),
        ],
        compiler_params=pltpu.CompilerParams(vmem_limit_bytes=56 << 20),
        name="factor_rows",
    )(where, own, *parts)


CHUNKS = 3


def apply_kernel(where_ref, own, *refs):
    near, wrap, upper, lower, late_wrap, late_upper, late_lower = refs[:7]
    chunks = refs[7 : 7 + CHUNKS]
    out, p_ref, r_ref, psems, rsems = refs[8 + CHUNKS :]
    second, col, z, core = where_ref[1], where_ref[2], where_ref[3], where_ref[4]
    chunk, local, other = chunks

    def piece(slot, part, by):
        rows = pl.ds(pl.multiple_of(lax.rem(z + by + 8, 8) * 64, 64), 64)
        return pltpu.make_async_copy(part, r_ref.at[rows], rsems.at[slot])

    piece(7, chunk, 0).start()
    for here, (low, high) in enumerate(((local, other), (other, local))):

        @pl.when(core == here)
        def _():
            for slot, by in enumerate((-3, -4, -1, -2)):
                piece(slot, low.at[pl.ds(slot * 64, 64)], by).start()
            for slot, by in enumerate((1, 2, 3)):
                piece(slot + 4, high.at[pl.ds(slot * 64, 64)], by).start()

    for flag, (last_near, last_far, last_wrap) in enumerate(
        ((near, (upper, lower), wrap), ((upper, lower), (late_upper, late_lower), late_wrap))
    ):

        @pl.when(second == flag)
        def _():
            start_columns(col, own, last_near, last_far, last_wrap, p_ref, psems)

    for slot in range(8):
        piece(slot, chunk, 0).wait()
    for last in range(BLOCKS):

        @pl.when(col == last)
        def _():
            @pl.loop(0, 2)
            def _(at):
                for column in range(last + 1):
                    wait_column(near, column, at, p_ref, psems)

                @pl.loop(0, HALF // TILE)
                def _(tile):
                    rows = pl.ds(pl.multiple_of(at * HALF + tile * TILE, TILE), TILE)
                    acc = mxu(r_ref[:, :TILE], p_ref[0, rows, :], NT)
                    for k in range(1, last + 1):
                        acc = acc + mxu(
                            r_ref[:, k * TILE : (k + 1) * TILE], p_ref[k, rows, :], NT
                        )
                    out[:, rows] = acc.astype(jnp.bfloat16)


def apply_rows(where, own, gathered, chunks, token):
    return pl.pallas_call(
        apply_kernel,
        out_shape=jax.ShapeDtypeStruct((TILE, PW), jnp.bfloat16),
        in_specs=[pl.BlockSpec(memory_space=pltpu.SMEM)] + [HBM] * (9 + CHUNKS),
        out_specs=pl.BlockSpec(memory_space=pltpu.VMEM),
        scratch_shapes=[
            pltpu.VMEM((BLOCKS, PW, TILE), jnp.bfloat16),
            pltpu.VMEM((TILE, PW), jnp.bfloat16),
            pltpu.SemaphoreType.DMA((2, BLOCKS)),
            pltpu.SemaphoreType.DMA((8,)),
        ],
        compiler_params=pltpu.CompilerParams(vmem_limit_bytes=60 << 20),
        name="apply_rows",
    )(where, own, *gathered, *chunks, token)


def device(child, z, ylo, core, col):
    return (child * 32 + z * 4 + ylo * 2 + core) * 4 + col


def pairs_of(move):
    found = []
    for child in range(2):
        for z in range(8):
            for ylo in range(2):
                for core in range(2):
                    for col in range(4):
                        target = move(child, z, ylo, core, col)
                        if target is not None:
                            found.append((device(child, z, ylo, core, col), device(*target)))
    return found


def moves(member, *steps):
    allowed = dict(steps)
    return pairs_of(
        lambda c, z, y, k, j: (c, z, y, k, allowed[j]) if member(c, z, y, k) and j in allowed else None
    )


def is_second(c, z, y, k):
    return (c, y, k) == (0, 0, 1)


def is_other(c, z, y, k):
    return (c, y, k) != (0, 0, 1)


def spread_rows(chunks, z, y, core):
    kept = chunks[0]
    total = None
    for k in range(1, 8):
        pairs = pairs_of(
            lambda c, zz, yy, kk, j: (0, k, 0, 0, j) if (c, zz, yy, kk) == (0, 0, 0, 0) else None
        )
        got = lax.ppermute(chunks[k], ALL, pairs)
        total = got if total is None else total + got
    chunk = jnp.where(z == 0, kept, total)
    total = None
    for to in (1, 3, 2):
        pairs = pairs_of(
            lambda c, zz, yy, kk, j: (to // 2, zz, to % 2, 0, j) if (c, yy, kk) == (0, 0, 0) else None
        )
        got = lax.ppermute(chunk, ALL, pairs)
        total = got if total is None else total + got
    chunk = jnp.where(y == 0, chunk, total)
    def ring(part, first=0, second=0):
        steps = (first, second)
        return lax.ppermute(
            part,
            ALL,
            pairs_of(
                lambda c, zz, yy, kk, j: (c, (zz + steps[kk]) % 8, yy, kk, j) if steps[kk] else None
            ),
        )

    two = ring(chunk, 2)
    one = ring(chunk, 1)
    chunk, one = lax.optimization_barrier((chunk, one))
    got = lax.ppermute(
        chunk, ALL, pairs_of(lambda c, zz, yy, kk, j: (c, zz, yy, 1, j) if kk == 0 else None)
    )
    chunk = jnp.where(core == 0, chunk, got)
    four = ring(chunk, 4, -2)
    three = ring(chunk, 3, -1)
    below = ring(chunk, 0, -3)
    local = jnp.concatenate([three, four, jnp.where(core == 0, one, below), two], axis=0)
    other = lax.ppermute(
        local, ALL, pairs_of(lambda c, zz, yy, kk, j: (c, zz, yy, 1 - kk, j))
    )
    return [chunk, local, other]


def shards(front, left_factors, right_factors):
    side = lax.axis_index("child")
    row = lax.axis_index("row")
    column = lax.axis_index("col")
    z, y, core = row // 4, 2 * side + (row // 2) % 2, row % 2
    tiles = right_factors.shape[1] // 2
    left_all = left_factors[0, 0].reshape(RANK, 2 * tiles, TILE).transpose(1, 0, 2)
    both = jnp.stack([left_all, right_factors[0]])
    sent = lax.dynamic_slice_in_dim(both, (1 - side) * tiles, tiles, 1)
    kept = lax.dynamic_slice_in_dim(both, side * tiles, tiles, 1)
    got = lax.ppermute(
        sent, ALL, pairs_of(lambda c, zz, yy, kk, j: (1 - c, zz, yy, kk, j))
    )
    factors = jnp.concatenate([kept, got], axis=2)
    update = jnp.einsum("trk,trn->tkn", factors[0], factors[1], preferred_element_type=jnp.float32)
    own = (front.astype(jnp.float32) - update.reshape(PW, TILE)).astype(jnp.bfloat16)
    second = jnp.logical_and(y == 0, core == 1)
    first = jnp.logical_and(jnp.logical_and(y == 0, z == 0), core == 0)
    near = lax.ppermute(own, ALL, moves(is_other, (0, 1), (1, 2), (2, 3)))
    wrap = lax.ppermute(own, ALL, moves(is_other, (0, 3)))
    back = lax.ppermute(own[HALF:], ALL, moves(is_other, (1, 0)))
    near, wrap, back = lax.optimization_barrier((near, wrap, back))
    token = lax.ppermute(
        near[:8, :128] + wrap[:8, :128],
        ALL,
        pairs_of(lambda c, zz, yy, kk, j: (0, zz, 0, 1, j) if (c, yy, kk) == (0, 1, 0) else None),
    )
    held, token = lax.optimization_barrier((own, token))
    along = moves(is_second, (0, 1), (1, 2), (2, 3))
    upper = lax.ppermute(
        jnp.where(second, held[:HALF], near[:HALF]), ALL, moves(is_other, (1, 2), (2, 3)) + along
    )
    mixed = jnp.where(column == 0, back, wrap[HALF:])
    lower = lax.ppermute(
        jnp.where(second, held[HALF:], mixed), ALL, moves(is_other, (0, 3), (3, 2)) + along
    )
    late_wrap = lax.ppermute(held, ALL, moves(is_second, (0, 3)))
    late_upper = lax.ppermute(upper, ALL, moves(is_second, (1, 2), (2, 3)))
    late_lower = lax.ppermute(lower, ALL, moves(is_second, (1, 2), (2, 3)))
    where = jnp.stack([first, second, column, z, core]).astype(jnp.int32)
    where, *gathered = lax.optimization_barrier(
        (where, near, wrap, upper, lower, late_wrap, late_upper, late_lower)
    )
    chunks = factor_rows(where, own, gathered[:4])
    chunks = spread_rows(chunks, z, y, core)
    return apply_rows(where, own, gathered, chunks, token)


def solution(mesh):
    in_specs = (
        P(("row", "child"), "col"),
        P("child", "col", None, "row"),
        P("child", "row", None, "col"),
    )
    out_specs = P("col", ("row", "child"))
    return jax.shard_map(shards, mesh=mesh, in_specs=in_specs, out_specs=out_specs, check_vma=False)
```

```python
import functools

import jax
import jax.numpy as jnp
from jax import lax
from jax.experimental import pallas as pl
from jax.experimental.pallas import tpu as pltpu
from jax.sharding import PartitionSpec as P

TILE = 512
RANK = 64
PW = 2048
BLOCKS = PW // TILE
ROOT_ITERS = 3
ALL = ("child", "row", "col")
NT = (((1,), (1,)), ((), ()))
NN = (((1,), (0,)), ((), ()))


def mxu(left, right, dims):
    return lax.dot_general(
        left.astype(jnp.bfloat16),
        right.astype(jnp.bfloat16),
        dims,
        preferred_element_type=jnp.float32,
    )


def leaf_inverse(tile_ref, x_ref, g_ref, n_ref, nb_ref):
    part = TILE // 2
    top, low = slice(0, part), slice(part, TILE)
    diag = lax.broadcasted_iota(jnp.int32, (part, part), 0) == lax.broadcasted_iota(
        jnp.int32, (part, part), 1
    )
    under = lax.broadcasted_iota(jnp.int32, (part, part), 0) > lax.broadcasted_iota(
        jnp.int32, (part, part), 1
    )

    def lower(mat):
        return jnp.where(under, mat, jnp.where(diag, 0.5 * mat, 0.0))

    def scales(block):
        picked = jnp.where(diag, tile_ref[block, block], 0.0)
        return (
            lax.rsqrt(jnp.sum(picked, axis=1, keepdims=True)),
            lax.rsqrt(jnp.sum(picked, axis=0, keepdims=True)),
        )

    (down0, across0), (down1, across1) = scales(top), scales(low)
    eye = diag.astype(jnp.float32)
    g00 = tile_ref[top, top] * down0 * across0 - eye
    g10 = tile_ref[low, top] * down1 * across0
    g01 = tile_ref[top, low] * down0 * across1
    g11 = tile_ref[low, low] * down1 * across1 - eye
    g_ref[top, top] = g00.astype(jnp.bfloat16)
    g_ref[low, top] = g10.astype(jnp.bfloat16)
    g_ref[top, low] = g01.astype(jnp.bfloat16)
    g_ref[low, low] = g11.astype(jnp.bfloat16)
    n_ref[top, top] = lower(g00)
    n_ref[low, top] = g10
    n_ref[low, low] = lower(g11)
    nb_ref[top, top] = lower(g00).astype(jnp.bfloat16)
    nb_ref[low, top] = g10.astype(jnp.bfloat16)
    nb_ref[low, low] = lower(g11).astype(jnp.bfloat16)

    def step(_, carry):
        n00, n10, n11 = n_ref[top, top], n_ref[low, top], n_ref[low, low]
        b00, b10, b11 = nb_ref[top, top], nb_ref[low, top], nb_ref[low, low]
        scaled00 = tile_ref[top, top] * down0 * across0 - eye
        scaled10 = tile_ref[low, top] * down1 * across0
        scaled11 = tile_ref[low, low] * down1 * across1 - eye
        e00 = scaled00 - n00 - mxu(b00, g_ref[top, top], NN)
        e10 = scaled10 - n10 - mxu(nb_ref[low, :], g_ref[:, top], NN)
        e11 = scaled11 - n11 - mxu(nb_ref[low, :], g_ref[:, low], NN)
        c00, c10, c11 = e00.astype(jnp.bfloat16), e10.astype(jnp.bfloat16), e11.astype(jnp.bfloat16)
        p00 = lower(e00 - jnp.where(diag, n00, 0.0) - mxu(c00, b00, NT))
        p10 = e10 - mxu(c10, b00, NT)
        p11 = lower(
            e11 - jnp.where(diag, n11, 0.0) - mxu(c10, b10, NT) - mxu(c11, b11, NT)
        )
        f00, f10, f11 = p00.astype(jnp.bfloat16), p10.astype(jnp.bfloat16), p11.astype(jnp.bfloat16)
        n00 = n00 + p00 - mxu(f00, b00, NN)
        n10 = n10 + p10 - mxu(f10, b00, NN) - mxu(f11, b10, NN)
        n11 = n11 + p11 - mxu(f11, b11, NN)
        n_ref[top, top], n_ref[low, top], n_ref[low, low] = n00, n10, n11
        nb_ref[top, top] = n00.astype(jnp.bfloat16)
        nb_ref[low, top] = n10.astype(jnp.bfloat16)
        nb_ref[low, low] = n11.astype(jnp.bfloat16)
        return carry

    lax.fori_loop(0, ROOT_ITERS, step, 0)
    x_ref[top, top] = ((eye - n_ref[top, top]) * across0).astype(jnp.bfloat16)
    x_ref[top, low] = jnp.zeros((part, part), jnp.bfloat16)
    x_ref[low, top] = (-n_ref[low, top] * across0).astype(jnp.bfloat16)
    x_ref[low, low] = ((eye - n_ref[low, low]) * across1).astype(jnp.bfloat16)


HALF = PW // 2


def start_columns(col, own, near, far, wrap, dest, sems):
    for last in range(BLOCKS):
        sources = {0: wrap} if last == 3 else {}
        if last >= 2:
            sources[last - 2] = far
        if last >= 1:
            sources[last - 1] = near
        sources[last] = own

        @pl.when(col == last)
        def _():
            for column, part in sources.items():
                for at in range(2):
                    rows = pl.ds(at * HALF, HALF)
                    source = part[at] if isinstance(part, tuple) else part.at[rows]
                    pltpu.make_async_copy(
                        source, dest.at[column, rows], sems.at[at, column]
                    ).start()


def wait_column(like, column, at, dest, sems):
    rows = pl.ds(pl.multiple_of(at * HALF, HALF), HALF)
    pltpu.make_async_copy(
        like.at[pl.ds(0, HALF)], dest.at[column, rows], sems.at[at, column]
    ).wait()


def factor_kernel(where_ref, own, *refs):
    parts, outs = tuple(refs[:4]), refs[4:12]
    t_ref, s_ref, l_ref, x_ref, r_ref, g_ref, n_ref, e_ref, sems = refs[12:]
    col = where_ref[2]

    @pl.when(where_ref[0] == 1)
    def _():
        start_columns(col, own, parts[0], parts[2:4], parts[1], t_ref, sems)

        def rows_of(i):
            return pl.ds(pl.multiple_of(i * TILE, TILE), TILE)

        def symmetric(i, j):
            low = t_ref[j, rows_of(i), :].astype(jnp.float32)
            high = t_ref[i, rows_of(j), :].astype(jnp.float32)
            s_ref[i, j] = 0.5 * (low + high.T)

        wait_column(own, 0, 0, t_ref, sems)
        symmetric(0, 0)

        @pl.loop(0, col + 1)
        def _(j):
            leaf_inverse(s_ref.at[j, j], x_ref.at[j], g_ref, n_ref, e_ref)

            @pl.when(j == 0)
            def _():
                wait_column(own, 0, 1, t_ref, sems)

                @pl.loop(1, col + 1)
                def _(i):
                    for at in range(2):
                        wait_column(own, i, at, t_ref, sems)

                @pl.loop(1, col + 1)
                def _(i):
                    @pl.loop(0, i + 1)
                    def _(k):
                        symmetric(i, k)

            @pl.loop(j + 1, col + 1)
            def _(i):
                l_ref[i, j] = mxu(s_ref[i, j], x_ref[j], NT).astype(jnp.bfloat16)

                @pl.loop(j + 1, i + 1)
                def _(k):
                    s_ref[i, k] = s_ref[i, k] - mxu(l_ref[i, j], l_ref[k, j], NT)

        r_ref[col] = x_ref[col]

        @pl.loop(0, BLOCKS)
        def _(step):
            k = BLOCKS - 1 - step

            @pl.when(k > col)
            def _():
                r_ref[k] = jnp.zeros((TILE, TILE), jnp.bfloat16)

            @pl.when(k < col)
            def _():
                n_ref[...] = jnp.zeros((TILE, TILE), jnp.float32)

                @pl.loop(k + 1, col + 1)
                def _(m):
                    n_ref[...] += mxu(r_ref[m], l_ref[m, k], NN)

                r_ref[k] = (-mxu(n_ref[...], x_ref[k], NN)).astype(jnp.bfloat16)

        for z in range(8):
            for k in range(BLOCKS):
                outs[z][:, k * TILE : (k + 1) * TILE] = r_ref[k, z * 64 : (z + 1) * 64, :]


HBM = pl.BlockSpec(memory_space=pltpu.HBM)


def factor_rows(where, own, parts):
    return pl.pallas_call(
        factor_kernel,
        out_shape=[jax.ShapeDtypeStruct((64, PW), jnp.bfloat16)] * 8,
        in_specs=[pl.BlockSpec(memory_space=pltpu.SMEM)] + [HBM] * 5,
        out_specs=[pl.BlockSpec(memory_space=pltpu.VMEM)] * 8,
        scratch_shapes=[
            pltpu.VMEM((BLOCKS, PW, TILE), jnp.bfloat16),
            pltpu.VMEM((BLOCKS, BLOCKS, TILE, TILE), jnp.float32),
            pltpu.VMEM((BLOCKS, BLOCKS, TILE, TILE), jnp.bfloat16),
            pltpu.VMEM((BLOCKS, TILE, TILE), jnp.bfloat16),
            pltpu.VMEM((BLOCKS, TILE, TILE), jnp.bfloat16),
            pltpu.VMEM((TILE, TILE), jnp.bfloat16),
            pltpu.VMEM((TILE, TILE), jnp.float32),
            pltpu.VMEM((TILE, TILE), jnp.bfloat16),
            pltpu.SemaphoreType.DMA((2, BLOCKS)),
        ],
        compiler_params=pltpu.CompilerParams(vmem_limit_bytes=56 << 20),
        name="factor_rows",
    )(where, own, *parts)


CHUNKS = 6


def apply_kernel(where_ref, own, *refs):
    near, wrap, upper, lower, late_wrap, late_far = refs[:6]
    chunks = refs[6 : 6 + CHUNKS]
    out, p_ref, r_ref, psems, rsems = refs[7 + CHUNKS :]
    second, col, z, core = where_ref[1], where_ref[2], where_ref[3], where_ref[4]
    sign = 1 - 2 * core
    swapped = chunks[5]

    def piece(slot, part, at, size):
        rows = pl.ds(pl.multiple_of(at, size), size)
        return pltpu.make_async_copy(part, r_ref.at[rows], rsems.at[slot])

    pieces = [piece(0, chunks[0], z * 64, 64)]
    for by in range(1, 4):
        down, up = lax.rem(z - sign * by + 8, 8) * 64, lax.rem(z + sign * by + 8, 8) * 64
        pieces.append(piece(by, chunks[by], down, 64))
        pieces.append(piece(by + 3, swapped.at[pl.ds(by * 64 - 64, 64)], up, 64))
    far = lax.rem(z + 4, 8) * 64
    pieces.append(piece(7, chunks[4], far + core * 32, 32))
    pieces.append(piece(8, swapped.at[pl.ds(192, 32)], far + (1 - core) * 32, 32))
    for copy in pieces:
        copy.start()

    for flag, (last_near, last_far, last_wrap) in enumerate(
        ((near, (upper, lower), wrap), ((upper, lower), late_far, late_wrap))
    ):

        @pl.when(second == flag)
        def _():
            start_columns(col, own, last_near, last_far, last_wrap, p_ref, psems)

    for copy in pieces:
        copy.wait()
    for last in range(BLOCKS):

        @pl.when(col == last)
        def _():
            @pl.loop(0, 2)
            def _(at):
                for column in range(last + 1):
                    wait_column(near, column, at, p_ref, psems)

                @pl.loop(0, HALF // TILE)
                def _(tile):
                    rows = pl.ds(pl.multiple_of(at * HALF + tile * TILE, TILE), TILE)
                    acc = mxu(r_ref[:, :TILE], p_ref[0, rows, :], NT)
                    for k in range(1, last + 1):
                        acc = acc + mxu(
                            r_ref[:, k * TILE : (k + 1) * TILE], p_ref[k, rows, :], NT
                        )
                    out[:, rows] = acc.astype(jnp.bfloat16)


def apply_rows(where, own, gathered, chunks, token):
    return pl.pallas_call(
        apply_kernel,
        out_shape=jax.ShapeDtypeStruct((TILE, PW), jnp.bfloat16),
        in_specs=[pl.BlockSpec(memory_space=pltpu.SMEM)] + [HBM] * (8 + CHUNKS),
        out_specs=pl.BlockSpec(memory_space=pltpu.VMEM),
        scratch_shapes=[
            pltpu.VMEM((BLOCKS, PW, TILE), jnp.bfloat16),
            pltpu.VMEM((TILE, PW), jnp.bfloat16),
            pltpu.SemaphoreType.DMA((2, BLOCKS)),
            pltpu.SemaphoreType.DMA((9,)),
        ],
        compiler_params=pltpu.CompilerParams(vmem_limit_bytes=60 << 20),
        name="apply_rows",
    )(where, own, *gathered, *chunks, token)


def device(child, z, ylo, core, col):
    return (child * 32 + z * 4 + ylo * 2 + core) * 4 + col


def pairs_of(move):
    found = []
    for child in range(2):
        for z in range(8):
            for ylo in range(2):
                for core in range(2):
                    for col in range(4):
                        target = move(child, z, ylo, core, col)
                        if target is not None:
                            found.append((device(child, z, ylo, core, col), device(*target)))
    return found


def moves(member, *steps):
    allowed = dict(steps)
    return pairs_of(
        lambda c, z, y, k, j: (c, z, y, k, allowed[j]) if member(c, z, y, k) and j in allowed else None
    )


def is_second(c, z, y, k):
    return (c, y, k) == (0, 0, 1)


def is_other(c, z, y, k):
    return (c, y, k) != (0, 0, 1)


def spread_rows(chunks, z, y, core, late_far):
    kept = chunks[0]
    total = None
    for k in range(1, 8):
        pairs = pairs_of(
            lambda c, zz, yy, kk, j: (0, k, 0, 0, j) if (c, zz, yy, kk) == (0, 0, 0, 0) else None
        )
        got = lax.ppermute(chunks[k], ALL, pairs)
        total = got if total is None else total + got
    chunk = jnp.where(z == 0, kept, total)
    total = None
    for to in (1, 3, 2):
        pairs = pairs_of(
            lambda c, zz, yy, kk, j: (to // 2, zz, to % 2, 0, j) if (c, yy, kk) == (0, 0, 0) else None
        )
        got = lax.ppermute(chunk, ALL, pairs)
        total = got if total is None else total + got
    chunk = jnp.where(y == 0, chunk, total)
    chunk, late_far = lax.optimization_barrier((chunk, late_far))
    got = lax.ppermute(
        chunk, ALL, pairs_of(lambda c, zz, yy, kk, j: (c, zz, yy, 1, j) if kk == 0 else None)
    )
    chunk = jnp.where(core == 0, chunk, got)
    swap = pairs_of(lambda c, zz, yy, kk, j: (c, zz, yy, 1 - kk, j))
    across = pairs_of(lambda c, zz, yy, kk, j: (c, (zz + 4) % 8, yy, kk, j))
    part = lax.dynamic_slice_in_dim(chunk, core * 32, 32, 0)
    half = lax.ppermute(part, ALL, across)
    direct = {}
    for by in (3, 2, 1):
        pairs = pairs_of(lambda c, zz, yy, kk, j: (c, (zz + (1 - 2 * kk) * by) % 8, yy, kk, j))
        direct[by] = lax.ppermute(chunk, ALL, pairs)
    mine = [direct[by] for by in (1, 2, 3)] + [half]
    theirs = lax.ppermute(jnp.concatenate(mine, axis=0), ALL, swap)
    return [chunk] + mine + [theirs], late_far


def shards(front, left_factors, right_factors):
    side = lax.axis_index("child")
    row = lax.axis_index("row")
    column = lax.axis_index("col")
    z, y, core = row // 4, 2 * side + (row // 2) % 2, row % 2
    tiles = right_factors.shape[1] // 2
    left_all = left_factors[0, 0].reshape(RANK, 2 * tiles, TILE).transpose(1, 0, 2)
    both = jnp.stack([left_all, right_factors[0]])
    sent = lax.dynamic_slice_in_dim(both, (1 - side) * tiles, tiles, 1)
    kept = lax.dynamic_slice_in_dim(both, side * tiles, tiles, 1)
    got = lax.ppermute(
        sent, ALL, pairs_of(lambda c, zz, yy, kk, j: (1 - c, zz, yy, kk, j))
    )
    factors = jnp.concatenate([kept, got], axis=2)
    update = jnp.einsum("trk,trn->tkn", factors[0], factors[1], preferred_element_type=jnp.float32)
    own = (front.astype(jnp.float32) - update.reshape(PW, TILE)).astype(jnp.bfloat16)
    second = jnp.logical_and(y == 0, core == 1)
    first = jnp.logical_and(jnp.logical_and(y == 0, z == 0), core == 0)
    near = lax.ppermute(own, ALL, moves(is_other, (0, 1), (1, 2), (2, 3)))
    wrap = lax.ppermute(own, ALL, moves(is_other, (0, 3)))
    back = lax.ppermute(own[HALF:], ALL, moves(is_other, (1, 0)))
    near, wrap, back = lax.optimization_barrier((near, wrap, back))
    token = lax.ppermute(
        near[:8, :128] + wrap[:8, :128],
        ALL,
        pairs_of(lambda c, zz, yy, kk, j: (0, zz, 0, 1, j) if (c, yy, kk) == (0, 1, 0) else None),
    )
    held, token = lax.optimization_barrier((own, token))
    along = moves(is_second, (0, 1), (1, 2), (2, 3))
    upper = lax.ppermute(
        jnp.where(second, held[:HALF], near[:HALF]), ALL, moves(is_other, (1, 2), (2, 3)) + along
    )
    mixed = jnp.where(column == 0, back, wrap[HALF:])
    lower = lax.ppermute(
        jnp.where(second, held[HALF:], mixed), ALL, moves(is_other, (0, 3), (3, 2)) + along
    )
    late_wrap = lax.ppermute(held, ALL, moves(is_second, (0, 3)))
    late_far = lax.ppermute(
        jnp.concatenate([upper, lower], axis=0), ALL, moves(is_second, (1, 2), (2, 3))
    )
    where = jnp.stack([first, second, column, z, core]).astype(jnp.int32)
    where, *gathered = lax.optimization_barrier(
        (where, near, wrap, upper, lower, late_wrap)
    )
    chunks = factor_rows(where, own, gathered[:4])
    chunks, late_far = spread_rows(chunks, z, y, core, late_far)
    return apply_rows(where, own, gathered + [late_far], chunks, token)


def solution(mesh):
    in_specs = (
        P(("row", "child"), "col"),
        P("child", "col", None, "row"),
        P("child", "row", None, "col"),
    )
    out_specs = P("col", ("row", "child"))
    return jax.shard_map(shards, mesh=mesh, in_specs=in_specs, out_specs=out_specs, check_vma=False)
```

```python
import functools

import jax
import jax.numpy as jnp
from jax import lax
from jax.experimental import pallas as pl
from jax.experimental.pallas import tpu as pltpu
from jax.sharding import PartitionSpec as P

TILE = 512
RANK = 64
PW = 2048
BLOCKS = PW // TILE
MOST_STEPS = 8
STEP_BOUND = 1e-4
ALL = ("child", "row", "col")
NT = (((1,), (1,)), ((), ()))
NN = (((1,), (0,)), ((), ()))


def mxu(left, right, dims):
    return lax.dot_general(
        left.astype(jnp.bfloat16),
        right.astype(jnp.bfloat16),
        dims,
        preferred_element_type=jnp.float32,
    )


def leaf_inverse(tile_ref, x_ref, g_ref, n_ref, nb_ref):
    part = TILE // 2
    top, low = slice(0, part), slice(part, TILE)
    diag = lax.broadcasted_iota(jnp.int32, (part, part), 0) == lax.broadcasted_iota(
        jnp.int32, (part, part), 1
    )
    under = lax.broadcasted_iota(jnp.int32, (part, part), 0) > lax.broadcasted_iota(
        jnp.int32, (part, part), 1
    )

    def lower(mat):
        return jnp.where(under, mat, jnp.where(diag, 0.5 * mat, 0.0))

    def scales(block):
        picked = jnp.where(diag, tile_ref[block, block], 0.0)
        return (
            lax.rsqrt(jnp.sum(picked, axis=1, keepdims=True)),
            lax.rsqrt(jnp.sum(picked, axis=0, keepdims=True)),
        )

    (down0, across0), (down1, across1) = scales(top), scales(low)
    eye = diag.astype(jnp.float32)
    g00 = tile_ref[top, top] * down0 * across0 - eye
    g10 = tile_ref[low, top] * down1 * across0
    g01 = tile_ref[top, low] * down0 * across1
    g11 = tile_ref[low, low] * down1 * across1 - eye
    g_ref[top, top] = g00.astype(jnp.bfloat16)
    g_ref[low, top] = g10.astype(jnp.bfloat16)
    g_ref[top, low] = g01.astype(jnp.bfloat16)
    g_ref[low, low] = g11.astype(jnp.bfloat16)
    n_ref[top, top] = lower(g00)
    n_ref[low, top] = g10
    n_ref[low, low] = lower(g11)
    nb_ref[top, top] = lower(g00).astype(jnp.bfloat16)
    nb_ref[low, top] = g10.astype(jnp.bfloat16)
    nb_ref[low, low] = lower(g11).astype(jnp.bfloat16)

    def step(state):
        n00, n10, n11 = n_ref[top, top], n_ref[low, top], n_ref[low, low]
        b00, b10, b11 = nb_ref[top, top], nb_ref[low, top], nb_ref[low, low]
        scaled00 = tile_ref[top, top] * down0 * across0 - eye
        scaled10 = tile_ref[low, top] * down1 * across0
        scaled11 = tile_ref[low, low] * down1 * across1 - eye
        e00 = scaled00 - n00 - mxu(b00, g_ref[top, top], NN)
        e10 = scaled10 - n10 - mxu(nb_ref[low, :], g_ref[:, top], NN)
        e11 = scaled11 - n11 - mxu(nb_ref[low, :], g_ref[:, low], NN)
        c00, c10, c11 = e00.astype(jnp.bfloat16), e10.astype(jnp.bfloat16), e11.astype(jnp.bfloat16)
        p00 = lower(e00 - jnp.where(diag, n00, 0.0) - mxu(c00, b00, NT))
        p10 = e10 - mxu(c10, b00, NT)
        p11 = lower(
            e11 - jnp.where(diag, n11, 0.0) - mxu(c10, b10, NT) - mxu(c11, b11, NT)
        )
        f00, f10, f11 = p00.astype(jnp.bfloat16), p10.astype(jnp.bfloat16), p11.astype(jnp.bfloat16)
        n00 = n00 + p00 - mxu(f00, b00, NN)
        n10 = n10 + p10 - mxu(f10, b00, NN) - mxu(f11, b10, NN)
        n11 = n11 + p11 - mxu(f11, b11, NN)
        n_ref[top, top], n_ref[low, top], n_ref[low, low] = n00, n10, n11
        nb_ref[top, top] = n00.astype(jnp.bfloat16)
        nb_ref[low, top] = n10.astype(jnp.bfloat16)
        nb_ref[low, low] = n11.astype(jnp.bfloat16)
        return state[0] + 1, jnp.sum(p00 * p00 + p11 * p11 + p10 * p10)

    lax.while_loop(
        lambda state: jnp.logical_and(state[0] < MOST_STEPS, state[1] > STEP_BOUND),
        step,
        (jnp.int32(0), jnp.float32(1.0)),
    )
    x_ref[top, top] = ((eye - n_ref[top, top]) * across0).astype(jnp.bfloat16)
    x_ref[top, low] = jnp.zeros((part, part), jnp.bfloat16)
    x_ref[low, top] = (-n_ref[low, top] * across0).astype(jnp.bfloat16)
    x_ref[low, low] = ((eye - n_ref[low, low]) * across1).astype(jnp.bfloat16)


HALF = PW // 2


def start_columns(col, own, near, far, wrap, dest, sems):
    for last in range(BLOCKS):
        sources = {0: wrap} if last == 3 else {}
        if last >= 2:
            sources[last - 2] = far
        if last >= 1:
            sources[last - 1] = near
        sources[last] = own

        @pl.when(col == last)
        def _():
            for column, part in sources.items():
                for at in range(2):
                    rows = pl.ds(at * HALF, HALF)
                    source = part[at] if isinstance(part, tuple) else part.at[rows]
                    pltpu.make_async_copy(
                        source, dest.at[column, rows], sems.at[at, column]
                    ).start()


def wait_column(like, column, at, dest, sems):
    rows = pl.ds(pl.multiple_of(at * HALF, HALF), HALF)
    pltpu.make_async_copy(
        like.at[pl.ds(0, HALF)], dest.at[column, rows], sems.at[at, column]
    ).wait()


def factor_kernel(where_ref, own, *refs):
    parts, outs = tuple(refs[:4]), refs[4:12]
    t_ref, s_ref, l_ref, x_ref, r_ref, g_ref, n_ref, e_ref, sems = refs[12:]
    col = where_ref[2]

    @pl.when(where_ref[0] == 1)
    def _():
        start_columns(col, own, parts[0], parts[2:4], parts[1], t_ref, sems)

        def rows_of(i):
            return pl.ds(pl.multiple_of(i * TILE, TILE), TILE)

        def symmetric(i, j):
            low = t_ref[j, rows_of(i), :].astype(jnp.float32)
            high = t_ref[i, rows_of(j), :].astype(jnp.float32)
            s_ref[i, j] = 0.5 * (low + high.T)

        wait_column(own, 0, 0, t_ref, sems)
        symmetric(0, 0)

        @pl.loop(0, col + 1)
        def _(j):
            leaf_inverse(s_ref.at[j, j], x_ref.at[j], g_ref, n_ref, e_ref)

            @pl.when(j == 0)
            def _():
                wait_column(own, 0, 1, t_ref, sems)

                @pl.loop(1, col + 1)
                def _(i):
                    for at in range(2):
                        wait_column(own, i, at, t_ref, sems)

                @pl.loop(1, col + 1)
                def _(i):
                    @pl.loop(0, i + 1)
                    def _(k):
                        symmetric(i, k)

            @pl.loop(j + 1, col + 1)
            def _(i):
                l_ref[i, j] = mxu(s_ref[i, j], x_ref[j], NT).astype(jnp.bfloat16)

                @pl.loop(j + 1, i + 1)
                def _(k):
                    s_ref[i, k] = s_ref[i, k] - mxu(l_ref[i, j], l_ref[k, j], NT)

        r_ref[col] = x_ref[col]

        @pl.loop(0, BLOCKS)
        def _(step):
            k = BLOCKS - 1 - step

            @pl.when(k > col)
            def _():
                r_ref[k] = jnp.zeros((TILE, TILE), jnp.bfloat16)

            @pl.when(k < col)
            def _():
                n_ref[...] = jnp.zeros((TILE, TILE), jnp.float32)

                @pl.loop(k + 1, col + 1)
                def _(m):
                    n_ref[...] += mxu(r_ref[m], l_ref[m, k], NN)

                r_ref[k] = (-mxu(n_ref[...], x_ref[k], NN)).astype(jnp.bfloat16)

        for z in range(8):
            for k in range(BLOCKS):
                outs[z][:, k * TILE : (k + 1) * TILE] = r_ref[k, z * 64 : (z + 1) * 64, :]


HBM = pl.BlockSpec(memory_space=pltpu.HBM)


def factor_rows(where, own, parts):
    return pl.pallas_call(
        factor_kernel,
        out_shape=[jax.ShapeDtypeStruct((64, PW), jnp.bfloat16)] * 8,
        in_specs=[pl.BlockSpec(memory_space=pltpu.SMEM)] + [HBM] * 5,
        out_specs=[pl.BlockSpec(memory_space=pltpu.VMEM)] * 8,
        scratch_shapes=[
            pltpu.VMEM((BLOCKS, PW, TILE), jnp.bfloat16),
            pltpu.VMEM((BLOCKS, BLOCKS, TILE, TILE), jnp.float32),
            pltpu.VMEM((BLOCKS, BLOCKS, TILE, TILE), jnp.bfloat16),
            pltpu.VMEM((BLOCKS, TILE, TILE), jnp.bfloat16),
            pltpu.VMEM((BLOCKS, TILE, TILE), jnp.bfloat16),
            pltpu.VMEM((TILE, TILE), jnp.bfloat16),
            pltpu.VMEM((TILE, TILE), jnp.float32),
            pltpu.VMEM((TILE, TILE), jnp.bfloat16),
            pltpu.SemaphoreType.DMA((2, BLOCKS)),
        ],
        compiler_params=pltpu.CompilerParams(vmem_limit_bytes=56 << 20),
        name="factor_rows",
    )(where, own, *parts)


CHUNKS = 6


def apply_kernel(where_ref, own, *refs):
    near, wrap, upper, lower, late_wrap, late_far = refs[:6]
    chunks = refs[6 : 6 + CHUNKS]
    out, p_ref, r_ref, psems, rsems = refs[7 + CHUNKS :]
    second, col, z, core = where_ref[1], where_ref[2], where_ref[3], where_ref[4]
    sign = 1 - 2 * core
    swapped = chunks[5]

    def piece(slot, part, at, size):
        rows = pl.ds(pl.multiple_of(at, size), size)
        return pltpu.make_async_copy(part, r_ref.at[rows], rsems.at[slot])

    pieces = [piece(0, chunks[0], z * 64, 64)]
    for by in range(1, 4):
        down, up = lax.rem(z - sign * by + 8, 8) * 64, lax.rem(z + sign * by + 8, 8) * 64
        pieces.append(piece(by, chunks[by], down, 64))
        pieces.append(piece(by + 3, swapped.at[pl.ds(by * 64 - 64, 64)], up, 64))
    far = lax.rem(z + 4, 8) * 64
    pieces.append(piece(7, chunks[4], far + core * 32, 32))
    pieces.append(piece(8, swapped.at[pl.ds(192, 32)], far + (1 - core) * 32, 32))
    for copy in pieces:
        copy.start()

    for flag, (last_near, last_far, last_wrap) in enumerate(
        ((near, (upper, lower), wrap), ((upper, lower), late_far, late_wrap))
    ):

        @pl.when(second == flag)
        def _():
            start_columns(col, own, last_near, last_far, last_wrap, p_ref, psems)

    for copy in pieces:
        copy.wait()
    for last in range(BLOCKS):

        @pl.when(col == last)
        def _():
            @pl.loop(0, 2)
            def _(at):
                for column in range(last + 1):
                    wait_column(near, column, at, p_ref, psems)

                @pl.loop(0, HALF // TILE)
                def _(tile):
                    rows = pl.ds(pl.multiple_of(at * HALF + tile * TILE, TILE), TILE)
                    acc = mxu(r_ref[:, :TILE], p_ref[0, rows, :], NT)
                    for k in range(1, last + 1):
                        acc = acc + mxu(
                            r_ref[:, k * TILE : (k + 1) * TILE], p_ref[k, rows, :], NT
                        )
                    out[:, rows] = acc.astype(jnp.bfloat16)


def apply_rows(where, own, gathered, chunks, token):
    return pl.pallas_call(
        apply_kernel,
        out_shape=jax.ShapeDtypeStruct((TILE, PW), jnp.bfloat16),
        in_specs=[pl.BlockSpec(memory_space=pltpu.SMEM)] + [HBM] * (8 + CHUNKS),
        out_specs=pl.BlockSpec(memory_space=pltpu.VMEM),
        scratch_shapes=[
            pltpu.VMEM((BLOCKS, PW, TILE), jnp.bfloat16),
            pltpu.VMEM((TILE, PW), jnp.bfloat16),
            pltpu.SemaphoreType.DMA((2, BLOCKS)),
            pltpu.SemaphoreType.DMA((9,)),
        ],
        compiler_params=pltpu.CompilerParams(vmem_limit_bytes=60 << 20),
        name="apply_rows",
    )(where, own, *gathered, *chunks, token)


def device(child, z, ylo, core, col):
    return (child * 32 + z * 4 + ylo * 2 + core) * 4 + col


def pairs_of(move):
    found = []
    for child in range(2):
        for z in range(8):
            for ylo in range(2):
                for core in range(2):
                    for col in range(4):
                        target = move(child, z, ylo, core, col)
                        if target is not None:
                            found.append((device(child, z, ylo, core, col), device(*target)))
    return found


def moves(member, *steps):
    allowed = dict(steps)
    return pairs_of(
        lambda c, z, y, k, j: (c, z, y, k, allowed[j]) if member(c, z, y, k) and j in allowed else None
    )


def is_second(c, z, y, k):
    return (c, y, k) == (0, 0, 1)


def is_other(c, z, y, k):
    return (c, y, k) != (0, 0, 1)


def spread_rows(chunks, z, y, core, late_far):
    kept = chunks[0]
    total = None
    for k in range(1, 8):
        pairs = pairs_of(
            lambda c, zz, yy, kk, j: (0, k, 0, 0, j) if (c, zz, yy, kk) == (0, 0, 0, 0) else None
        )
        got = lax.ppermute(chunks[k], ALL, pairs)
        total = got if total is None else total + got
    chunk = jnp.where(z == 0, kept, total)
    total = None
    for to in (1, 3, 2):
        pairs = pairs_of(
            lambda c, zz, yy, kk, j: (to // 2, zz, to % 2, 0, j) if (c, yy, kk) == (0, 0, 0) else None
        )
        got = lax.ppermute(chunk, ALL, pairs)
        total = got if total is None else total + got
    chunk = jnp.where(y == 0, chunk, total)
    chunk, late_far = lax.optimization_barrier((chunk, late_far))
    got = lax.ppermute(
        chunk, ALL, pairs_of(lambda c, zz, yy, kk, j: (c, zz, yy, 1, j) if kk == 0 else None)
    )
    chunk = jnp.where(core == 0, chunk, got)
    swap = pairs_of(lambda c, zz, yy, kk, j: (c, zz, yy, 1 - kk, j))
    across = pairs_of(lambda c, zz, yy, kk, j: (c, (zz + 4) % 8, yy, kk, j))
    part = lax.dynamic_slice_in_dim(chunk, core * 32, 32, 0)
    half = lax.ppermute(part, ALL, across)
    direct = {}
    for by in (3, 2, 1):
        pairs = pairs_of(lambda c, zz, yy, kk, j: (c, (zz + (1 - 2 * kk) * by) % 8, yy, kk, j))
        direct[by] = lax.ppermute(chunk, ALL, pairs)
    mine = [direct[by] for by in (1, 2, 3)] + [half]
    theirs = lax.ppermute(jnp.concatenate(mine, axis=0), ALL, swap)
    return [chunk] + mine + [theirs], late_far


def shards(front, left_factors, right_factors):
    side = lax.axis_index("child")
    row = lax.axis_index("row")
    column = lax.axis_index("col")
    z, y, core = row // 4, 2 * side + (row // 2) % 2, row % 2
    tiles = right_factors.shape[1] // 2
    left_all = left_factors[0, 0].reshape(RANK, 2 * tiles, TILE).transpose(1, 0, 2)
    both = jnp.stack([left_all, right_factors[0]])
    sent = lax.dynamic_slice_in_dim(both, (1 - side) * tiles, tiles, 1)
    kept = lax.dynamic_slice_in_dim(both, side * tiles, tiles, 1)
    got = lax.ppermute(
        sent, ALL, pairs_of(lambda c, zz, yy, kk, j: (1 - c, zz, yy, kk, j))
    )
    factors = jnp.concatenate([kept, got], axis=2)
    update = jnp.einsum("trk,trn->tkn", factors[0], factors[1], preferred_element_type=jnp.float32)
    own = (front.astype(jnp.float32) - update.reshape(PW, TILE)).astype(jnp.bfloat16)
    second = jnp.logical_and(y == 0, core == 1)
    first = jnp.logical_and(jnp.logical_and(y == 0, z == 0), core == 0)
    near = lax.ppermute(own, ALL, moves(is_other, (0, 1), (1, 2), (2, 3)))
    wrap = lax.ppermute(own, ALL, moves(is_other, (0, 3)))
    back = lax.ppermute(own[HALF:], ALL, moves(is_other, (1, 0)))
    near, wrap, back = lax.optimization_barrier((near, wrap, back))
    token = lax.ppermute(
        near[:8, :128] + wrap[:8, :128],
        ALL,
        pairs_of(lambda c, zz, yy, kk, j: (0, zz, 0, 1, j) if (c, yy, kk) == (0, 1, 0) else None),
    )
    held, token = lax.optimization_barrier((own, token))
    along = moves(is_second, (0, 1), (1, 2), (2, 3))
    upper = lax.ppermute(
        jnp.where(second, held[:HALF], near[:HALF]), ALL, moves(is_other, (1, 2), (2, 3)) + along
    )
    mixed = jnp.where(column == 0, back, wrap[HALF:])
    lower = lax.ppermute(
        jnp.where(second, held[HALF:], mixed), ALL, moves(is_other, (0, 3), (3, 2)) + along
    )
    late_wrap = lax.ppermute(held, ALL, moves(is_second, (0, 3)))
    late_far = lax.ppermute(
        jnp.concatenate([upper, lower], axis=0), ALL, moves(is_second, (1, 2), (2, 3))
    )
    where = jnp.stack([first, second, column, z, core]).astype(jnp.int32)
    where, *gathered = lax.optimization_barrier(
        (where, near, wrap, upper, lower, late_wrap)
    )
    chunks = factor_rows(where, own, gathered[:4])
    chunks, late_far = spread_rows(chunks, z, y, core, late_far)
    return apply_rows(where, own, gathered + [late_far], chunks, token)


def solution(mesh):
    in_specs = (
        P(("row", "child"), "col"),
        P("child", "col", None, "row"),
        P("child", "row", None, "col"),
    )
    out_specs = P("col", ("row", "child"))
    return jax.shard_map(shards, mesh=mesh, in_specs=in_specs, out_specs=out_specs, check_vma=False)
```

```python
import functools

import jax
import jax.numpy as jnp
from jax import lax
from jax.experimental import pallas as pl
from jax.experimental.pallas import tpu as pltpu
from jax.sharding import PartitionSpec as P

TILE = 512
RANK = 64
PW = 2048
BLOCKS = PW // TILE
MOST_STEPS = 8
STEP_BOUND = 1e-4
ALL = ("child", "row", "col")
NT = (((1,), (1,)), ((), ()))
NN = (((1,), (0,)), ((), ()))


def mxu(left, right, dims):
    return lax.dot_general(
        left.astype(jnp.bfloat16),
        right.astype(jnp.bfloat16),
        dims,
        preferred_element_type=jnp.float32,
    )


def leaf_inverse(tile_ref, x_ref, g_ref, n_ref, nb_ref):
    part = TILE // 2
    top, low = slice(0, part), slice(part, TILE)
    diag = lax.broadcasted_iota(jnp.int32, (part, part), 0) == lax.broadcasted_iota(
        jnp.int32, (part, part), 1
    )
    under = lax.broadcasted_iota(jnp.int32, (part, part), 0) > lax.broadcasted_iota(
        jnp.int32, (part, part), 1
    )

    def lower(mat):
        return jnp.where(under, mat, jnp.where(diag, 0.5 * mat, 0.0))

    def scales(block):
        picked = jnp.where(diag, tile_ref[block, block], 0.0)
        return (
            lax.rsqrt(jnp.sum(picked, axis=1, keepdims=True)),
            lax.rsqrt(jnp.sum(picked, axis=0, keepdims=True)),
        )

    (down0, across0), (down1, across1) = scales(top), scales(low)
    eye = diag.astype(jnp.float32)
    g00 = tile_ref[top, top] * down0 * across0 - eye
    g10 = tile_ref[low, top] * down1 * across0
    g01 = tile_ref[top, low] * down0 * across1
    g11 = tile_ref[low, low] * down1 * across1 - eye
    g_ref[top, top] = g00.astype(jnp.bfloat16)
    g_ref[low, top] = g10.astype(jnp.bfloat16)
    g_ref[top, low] = g01.astype(jnp.bfloat16)
    g_ref[low, low] = g11.astype(jnp.bfloat16)
    n_ref[top, top] = lower(g00)
    n_ref[low, top] = g10
    n_ref[low, low] = lower(g11)
    nb_ref[top, top] = lower(g00).astype(jnp.bfloat16)
    nb_ref[low, top] = g10.astype(jnp.bfloat16)
    nb_ref[low, low] = lower(g11).astype(jnp.bfloat16)

    def step(state):
        n00, n10, n11 = n_ref[top, top], n_ref[low, top], n_ref[low, low]
        b00, b10, b11 = nb_ref[top, top], nb_ref[low, top], nb_ref[low, low]
        scaled00 = tile_ref[top, top] * down0 * across0 - eye
        scaled10 = tile_ref[low, top] * down1 * across0
        scaled11 = tile_ref[low, low] * down1 * across1 - eye
        e00 = scaled00 - n00 - mxu(b00, g_ref[top, top], NN)
        e10 = scaled10 - n10 - mxu(nb_ref[low, :], g_ref[:, top], NN)
        e11 = scaled11 - n11 - mxu(nb_ref[low, :], g_ref[:, low], NN)
        c00, c10, c11 = e00.astype(jnp.bfloat16), e10.astype(jnp.bfloat16), e11.astype(jnp.bfloat16)
        p00 = lower(e00 - jnp.where(diag, n00, 0.0) - mxu(c00, b00, NT))
        p10 = e10 - mxu(c10, b00, NT)
        p11 = lower(
            e11 - jnp.where(diag, n11, 0.0) - mxu(c10, b10, NT) - mxu(c11, b11, NT)
        )
        f00, f10, f11 = p00.astype(jnp.bfloat16), p10.astype(jnp.bfloat16), p11.astype(jnp.bfloat16)
        n00 = n00 + p00 - mxu(f00, b00, NN)
        n10 = n10 + p10 - mxu(f10, b00, NN) - mxu(f11, b10, NN)
        n11 = n11 + p11 - mxu(f11, b11, NN)
        n_ref[top, top], n_ref[low, top], n_ref[low, low] = n00, n10, n11
        nb_ref[top, top] = n00.astype(jnp.bfloat16)
        nb_ref[low, top] = n10.astype(jnp.bfloat16)
        nb_ref[low, low] = n11.astype(jnp.bfloat16)
        return state[0] + 1, jnp.sum(p00 * p00 + p11 * p11 + p10 * p10)

    lax.while_loop(
        lambda state: jnp.logical_and(state[0] < MOST_STEPS, state[1] > STEP_BOUND),
        step,
        (jnp.int32(0), jnp.float32(1.0)),
    )
    x_ref[top, top] = ((eye - n_ref[top, top]) * across0).astype(jnp.bfloat16)
    x_ref[top, low] = jnp.zeros((part, part), jnp.bfloat16)
    x_ref[low, top] = (-n_ref[low, top] * across0).astype(jnp.bfloat16)
    x_ref[low, low] = ((eye - n_ref[low, low]) * across1).astype(jnp.bfloat16)


HALF = PW // 2


def start_columns(col, own, near, far, wrap, dest, sems):
    for last in range(BLOCKS):
        sources = {0: wrap} if last == 3 else {}
        if last >= 2:
            sources[last - 2] = far
        if last >= 1:
            sources[last - 1] = near
        sources[last] = own

        @pl.when(col == last)
        def _():
            for column, part in sources.items():
                for at in range(2):
                    rows = pl.ds(at * HALF, HALF)
                    source = part[at] if isinstance(part, tuple) else part.at[rows]
                    pltpu.make_async_copy(
                        source, dest.at[column, rows], sems.at[at, column]
                    ).start()


def wait_column(like, column, at, dest, sems):
    rows = pl.ds(pl.multiple_of(at * HALF, HALF), HALF)
    pltpu.make_async_copy(
        like.at[pl.ds(0, HALF)], dest.at[column, rows], sems.at[at, column]
    ).wait()


def factor_kernel(where_ref, own, *refs):
    parts, outs = tuple(refs[:4]), refs[4:12]
    t_ref, s_ref, l_ref, x_ref, r_ref, g_ref, n_ref, e_ref, sems = refs[12:]
    col = where_ref[2]

    @pl.when(where_ref[0] == 1)
    def _():
        start_columns(col, own, parts[0], parts[2:4], parts[1], t_ref, sems)

        def rows_of(i):
            return pl.ds(pl.multiple_of(i * TILE, TILE), TILE)

        def symmetric(i, j):
            low = t_ref[j, rows_of(i), :].astype(jnp.float32)
            high = t_ref[i, rows_of(j), :].astype(jnp.float32)
            s_ref[i, j] = 0.5 * (low + high.T)

        wait_column(own, 0, 0, t_ref, sems)
        symmetric(0, 0)

        @pl.loop(0, col + 1)
        def _(j):
            leaf_inverse(s_ref.at[j, j], x_ref.at[j], g_ref, n_ref, e_ref)

            @pl.when(j == 0)
            def _():
                wait_column(own, 0, 1, t_ref, sems)

                @pl.loop(1, col + 1)
                def _(i):
                    for at in range(2):
                        wait_column(own, i, at, t_ref, sems)

                @pl.loop(1, col + 1)
                def _(i):
                    @pl.loop(0, i + 1)
                    def _(k):
                        symmetric(i, k)

            @pl.loop(j + 1, col + 1)
            def _(i):
                l_ref[i, j] = mxu(s_ref[i, j], x_ref[j], NT).astype(jnp.bfloat16)

                @pl.loop(j + 1, i + 1)
                def _(k):
                    s_ref[i, k] = s_ref[i, k] - mxu(l_ref[i, j], l_ref[k, j], NT)

        r_ref[col] = x_ref[col]

        @pl.loop(0, BLOCKS)
        def _(step):
            k = BLOCKS - 1 - step

            @pl.when(k > col)
            def _():
                r_ref[k] = jnp.zeros((TILE, TILE), jnp.bfloat16)

            @pl.when(k < col)
            def _():
                n_ref[...] = jnp.zeros((TILE, TILE), jnp.float32)

                @pl.loop(k + 1, col + 1)
                def _(m):
                    n_ref[...] += mxu(r_ref[m], l_ref[m, k], NN)

                r_ref[k] = (-mxu(n_ref[...], x_ref[k], NN)).astype(jnp.bfloat16)

        for z in range(8):
            for k in range(BLOCKS):
                outs[z][:, k * TILE : (k + 1) * TILE] = r_ref[k, z * 64 : (z + 1) * 64, :]


HBM = pl.BlockSpec(memory_space=pltpu.HBM)


def factor_rows(where, own, parts):
    return pl.pallas_call(
        factor_kernel,
        out_shape=[jax.ShapeDtypeStruct((64, PW), jnp.bfloat16)] * 8,
        in_specs=[pl.BlockSpec(memory_space=pltpu.SMEM)] + [HBM] * 5,
        out_specs=[pl.BlockSpec(memory_space=pltpu.VMEM)] * 8,
        scratch_shapes=[
            pltpu.VMEM((BLOCKS, PW, TILE), jnp.bfloat16),
            pltpu.VMEM((BLOCKS, BLOCKS, TILE, TILE), jnp.float32),
            pltpu.VMEM((BLOCKS, BLOCKS, TILE, TILE), jnp.bfloat16),
            pltpu.VMEM((BLOCKS, TILE, TILE), jnp.bfloat16),
            pltpu.VMEM((BLOCKS, TILE, TILE), jnp.bfloat16),
            pltpu.VMEM((TILE, TILE), jnp.bfloat16),
            pltpu.VMEM((TILE, TILE), jnp.float32),
            pltpu.VMEM((TILE, TILE), jnp.bfloat16),
            pltpu.SemaphoreType.DMA((2, BLOCKS)),
        ],
        compiler_params=pltpu.CompilerParams(vmem_limit_bytes=56 << 20),
        name="factor_rows",
    )(where, own, *parts)


CHUNKS = 6


def apply_kernel(where_ref, own, *refs):
    near, wrap, upper, lower, late_wrap, late_far = refs[:6]
    chunks = refs[6 : 6 + CHUNKS]
    out, p_ref, r_ref, psems, rsems = refs[7 + CHUNKS :]
    second, col, z, core = where_ref[1], where_ref[2], where_ref[3], where_ref[4]
    sign = 1 - 2 * core
    swapped = chunks[5]

    def piece(slot, part, at, size):
        rows = pl.ds(pl.multiple_of(at, size), size)
        return pltpu.make_async_copy(part, r_ref.at[rows], rsems.at[slot])

    pieces = [piece(0, chunks[0], z * 64, 64)]
    for by in range(1, 4):
        down, up = lax.rem(z - sign * by + 8, 8) * 64, lax.rem(z + sign * by + 8, 8) * 64
        pieces.append(piece(by, chunks[by], down, 64))
        pieces.append(piece(by + 3, swapped.at[pl.ds(by * 64 - 64, 64)], up, 64))
    far = lax.rem(z + 4, 8) * 64
    pieces.append(piece(7, chunks[4], far + core * 32, 32))
    pieces.append(piece(8, swapped.at[pl.ds(192, 32)], far + (1 - core) * 32, 32))
    for copy in pieces:
        copy.start()

    for flag, (last_near, last_far, last_wrap) in enumerate(
        ((near, (upper, lower), wrap), ((upper, lower), late_far, late_wrap))
    ):

        @pl.when(second == flag)
        def _():
            start_columns(col, own, last_near, last_far, last_wrap, p_ref, psems)

    for copy in pieces:
        copy.wait()
    for last in range(BLOCKS):

        @pl.when(col == last)
        def _():
            @pl.loop(0, 2)
            def _(at):
                for column in range(last + 1):
                    wait_column(near, column, at, p_ref, psems)

                @pl.loop(0, HALF // TILE)
                def _(tile):
                    rows = pl.ds(pl.multiple_of(at * HALF + tile * TILE, TILE), TILE)
                    acc = mxu(r_ref[:, :TILE], p_ref[0, rows, :], NT)
                    for k in range(1, last + 1):
                        acc = acc + mxu(
                            r_ref[:, k * TILE : (k + 1) * TILE], p_ref[k, rows, :], NT
                        )
                    out[:, rows] = acc.astype(jnp.bfloat16)


def apply_rows(where, own, gathered, chunks, token):
    return pl.pallas_call(
        apply_kernel,
        out_shape=jax.ShapeDtypeStruct((TILE, PW), jnp.bfloat16),
        in_specs=[pl.BlockSpec(memory_space=pltpu.SMEM)] + [HBM] * (8 + CHUNKS),
        out_specs=pl.BlockSpec(memory_space=pltpu.VMEM),
        scratch_shapes=[
            pltpu.VMEM((BLOCKS, PW, TILE), jnp.bfloat16),
            pltpu.VMEM((TILE, PW), jnp.bfloat16),
            pltpu.SemaphoreType.DMA((2, BLOCKS)),
            pltpu.SemaphoreType.DMA((9,)),
        ],
        compiler_params=pltpu.CompilerParams(vmem_limit_bytes=60 << 20),
        name="apply_rows",
    )(where, own, *gathered, *chunks, token)


def device(child, z, ylo, core, col):
    return (child * 32 + z * 4 + ylo * 2 + core) * 4 + col


def pairs_of(move):
    found = []
    for child in range(2):
        for z in range(8):
            for ylo in range(2):
                for core in range(2):
                    for col in range(4):
                        target = move(child, z, ylo, core, col)
                        if target is not None:
                            found.append((device(child, z, ylo, core, col), device(*target)))
    return found


def moves(member, *steps):
    allowed = dict(steps)
    return pairs_of(
        lambda c, z, y, k, j: (c, z, y, k, allowed[j]) if member(c, z, y, k) and j in allowed else None
    )


def is_second(c, z, y, k):
    return (c, y, k) == (0, 0, 1)


def is_other(c, z, y, k):
    return (c, y, k) != (0, 0, 1)


def spread_rows(chunks, z, y, core, late_far):
    kept = chunks[0]
    total = None
    for k in range(1, 8):
        pairs = pairs_of(
            lambda c, zz, yy, kk, j: (0, k, 0, 0, j) if (c, zz, yy, kk) == (0, 0, 0, 0) else None
        )
        got = lax.ppermute(chunks[k], ALL, pairs)
        total = got if total is None else total + got
    chunk = jnp.where(z == 0, kept, total)
    total = None
    for to in (1, 3, 2):
        pairs = pairs_of(
            lambda c, zz, yy, kk, j: (to // 2, zz, to % 2, 0, j) if (c, yy, kk) == (0, 0, 0) else None
        )
        got = lax.ppermute(chunk, ALL, pairs)
        total = got if total is None else total + got
    chunk = jnp.where(y == 0, chunk, total)

    got = lax.ppermute(
        chunk, ALL, pairs_of(lambda c, zz, yy, kk, j: (c, zz, yy, 1, j) if kk == 0 else None)
    )
    chunk = jnp.where(core == 0, chunk, got)
    swap = pairs_of(lambda c, zz, yy, kk, j: (c, zz, yy, 1 - kk, j))
    across = pairs_of(lambda c, zz, yy, kk, j: (c, (zz + 4) % 8, yy, kk, j))
    part = lax.dynamic_slice_in_dim(chunk, core * 32, 32, 0)
    half = lax.ppermute(part, ALL, across)
    direct = {}
    for by in (3, 2, 1):
        pairs = pairs_of(lambda c, zz, yy, kk, j: (c, (zz + (1 - 2 * kk) * by) % 8, yy, kk, j))
        direct[by] = lax.ppermute(chunk, ALL, pairs)
    mine = [direct[by] for by in (1, 2, 3)] + [half]
    theirs = lax.ppermute(jnp.concatenate(mine, axis=0), ALL, swap)
    return [chunk] + mine + [theirs], late_far


def shards(front, left_factors, right_factors):
    side = lax.axis_index("child")
    row = lax.axis_index("row")
    column = lax.axis_index("col")
    z, y, core = row // 4, 2 * side + (row // 2) % 2, row % 2
    tiles = right_factors.shape[1] // 2
    left_all = left_factors[0, 0].reshape(RANK, 2 * tiles, TILE).transpose(1, 0, 2)
    both = jnp.stack([left_all, right_factors[0]])
    sent = lax.dynamic_slice_in_dim(both, (1 - side) * tiles, tiles, 1)
    kept = lax.dynamic_slice_in_dim(both, side * tiles, tiles, 1)
    got = lax.ppermute(
        sent, ALL, pairs_of(lambda c, zz, yy, kk, j: (1 - c, zz, yy, kk, j))
    )
    factors = jnp.concatenate([kept, got], axis=2)
    update = jnp.einsum("trk,trn->tkn", factors[0], factors[1], preferred_element_type=jnp.float32)
    own = (front.astype(jnp.float32) - update.reshape(PW, TILE)).astype(jnp.bfloat16)
    second = jnp.logical_and(y == 0, core == 1)
    first = jnp.logical_and(jnp.logical_and(y == 0, z == 0), core == 0)
    near = lax.ppermute(own, ALL, moves(is_other, (0, 1), (1, 2), (2, 3)))
    wrap = lax.ppermute(own, ALL, moves(is_other, (0, 3)))
    back = lax.ppermute(own[HALF:], ALL, moves(is_other, (1, 0)))
    near, wrap, back = lax.optimization_barrier((near, wrap, back))
    token = lax.ppermute(
        near[:8, :128] + wrap[:8, :128],
        ALL,
        pairs_of(lambda c, zz, yy, kk, j: (0, zz, 0, 1, j) if (c, yy, kk) == (0, 1, 0) else None),
    )
    held, token = lax.optimization_barrier((own, token))
    along = moves(is_second, (0, 1), (1, 2), (2, 3))
    upper = lax.ppermute(
        jnp.where(second, held[:HALF], near[:HALF]), ALL, moves(is_other, (1, 2), (2, 3)) + along
    )
    mixed = jnp.where(column == 0, back, wrap[HALF:])
    lower = lax.ppermute(
        jnp.where(second, held[HALF:], mixed), ALL, moves(is_other, (0, 3), (3, 2)) + along
    )
    late_wrap = lax.ppermute(held, ALL, moves(is_second, (0, 3)))
    late_far = lax.ppermute(
        jnp.concatenate([upper, lower], axis=0), ALL, moves(is_second, (1, 2), (2, 3))
    )
    where = jnp.stack([first, second, column, z, core]).astype(jnp.int32)
    where, *gathered = lax.optimization_barrier(
        (where, near, wrap, upper, lower, late_wrap)
    )
    chunks = factor_rows(where, own, gathered[:4])
    chunks, late_far = spread_rows(chunks, z, y, core, late_far)
    return apply_rows(where, own, gathered + [late_far], chunks, token)


def solution(mesh):
    in_specs = (
        P(("row", "child"), "col"),
        P("child", "col", None, "row"),
        P("child", "row", None, "col"),
    )
    out_specs = P("col", ("row", "child"))
    return jax.shard_map(shards, mesh=mesh, in_specs=in_specs, out_specs=out_specs, check_vma=False)
```
